128 devices in a mesh: dp: 8 (over z, core), seq: 16 (over y, x).
Axes of the slice: x: 4, y: 4, z: 4, core: 2. Of those that a mesh axis runs over, the one named last changes fastest.
Arguments:
- tokens: bfloat16 [16384, 2688], P(('dp', 'seq')), may hold values from -6 to 6
- q_weight: bfloat16 [2688, 4096], P('dp', 'seq'), may hold values from -0.125 to 0.125
- key_projection: bfloat16 [2688, 2048], P('dp', 'seq'), may hold values from -0.125 to 0.125
- value_projection: bfloat16 [2688, 2048], P('dp', 'seq'), may hold values from -0.125 to 0.125
- query_norm_gain: float32 [128], replicated, may hold values from 0.5 to 2.5
- key_norm_gain: float32 [128], replicated, may hold values from 0.5 to 2.5
- doc_lengths: int32 [8, 4], P('dp'), may hold values from 1 to 1536, 2048 in all within a row
- out_cot: bfloat16 [16384, 4096], P('dp', 'seq'), may hold values from -6 to 6
Outputs:
- attn_out: bfloat16 [16384, 4096], P(('dp', 'seq'))
- token_grad: bfloat16 [16384, 2688], P(('dp', 'seq'))
- q_weight_grad: float32 [2688, 4096], P('dp', 'seq')
- k_weight_grad: float32 [2688, 2048], P('dp', 'seq')
- v_weight_grad: float32 [2688, 2048], P('dp', 'seq')
The draws below stay inside these ranges and needn't reach their ends.
Inputs may be any that keep to these rules, and one draw needn't show every extreme that they name: `doc_lengths`: each row's 4 lengths add up to 2048, and in every row the longest document has exactly 1536 tokens.
All inputs are finite; a program needn't handle non-finite values.
Results may differ from the reference program's by a relative error of at most 0.015.
Values may be sent and summed in bfloat16 or wider, within the bound.
A program may use at most 128 MiB of HBM per device.

```python
import math
import jax
import jax.numpy as jnp
import numpy as np
from jax import lax

MODEL_WIDTH = 2688
QUERY_HEADS = 32
KEY_VALUE_HEADS = 16
HEAD_WIDTH = 128
WINDOW = 1024
DOCS = 4
SEQ_LEN = 2048
ROWS = 16384
HQ_DEV = 2
KV_DEV = 1
N_DP = 8


def steps_of(rng, extent, split, low, high):
    def one(dim, parts):
        steps = jax.random.uniform(jax.random.fold_in(jax.random.fold_in(rng, 6), dim), (parts,), jnp.float32, low / len(split), high / len(split))
        return jnp.repeat(jnp.exp(steps), extent[dim] // parts).reshape((-1,) + (1,) * (len(extent) - dim - 1))

    level = one(*split[0])
    for cut in split[1:]:
        level = level * one(*cut)
    return level


def split_up(amount, total, most, skew):
    weights = [(1 << 20) // math.isqrt(rank ** skew) + 1 for rank in range(2, amount + 1)]
    surplus, counts = total - most - (amount - 1), [1] * (amount - 1)
    while surplus > 0:
        movable = [i for i in range(amount - 1) if counts[i] < most]
        whole, budget = sum([weights[i] for i in movable]), surplus
        for i in movable:
            addition = min(most - counts[i], max(1, budget * weights[i] // whole), surplus)
            counts[i] = counts[i] + addition
            surplus = surplus - addition
    return np.array([most] + counts)


def ragged_sizes(rng, number_of, total, bound, lean):
    if number_of == 2:
        one = jax.random.randint(rng, (), max(1, total - bound), min(bound, total - 1) + 1)
        return jnp.stack([one, total - one])
    tallies = jnp.asarray(split_up(number_of, total, bound, lean), jnp.int32)
    twos = (number_of - 1) // 2
    source_of, receiver = tallies[1:1 + 2 * twos:2], tallies[2:2 + 2 * twos:2]
    room = jnp.minimum(source_of - 1, bound - receiver)
    shifted = jax.random.randint(jax.random.fold_in(rng, 1), (twos,), 0, 1 << 20) % (room + 1)
    tallies = tallies.at[1:1 + 2 * twos:2].set(source_of - shifted).at[2:2 + 2 * twos:2].set(receiver + shifted)
    return tallies[jax.random.permutation(jax.random.fold_in(rng, 2), number_of)]


def normal_values(key, dims, scale, bound, cuts=(), kind=jnp.bfloat16):
    values = scale * jax.random.normal(key, dims, jnp.float32)
    if cuts:
        values = values * steps_of(key, dims, cuts, -0.22, 0.18)
    return jnp.clip(values, -bound, bound).astype(kind)


def setup_inputs(seed: int = 0) -> dict:
    key_list = jax.random.split(jax.random.key(seed), 9)
    tokens = normal_values(key_list[0], (ROWS, MODEL_WIDTH), 1.0, 6.0, ((0, 128),))
    q_weight = normal_values(key_list[1], (MODEL_WIDTH, QUERY_HEADS * HEAD_WIDTH), MODEL_WIDTH ** -0.5, 0.125, ((0, 8), (1, 16)))
    key_projection = normal_values(key_list[2], (MODEL_WIDTH, KEY_VALUE_HEADS * HEAD_WIDTH), MODEL_WIDTH ** -0.5, 0.125, ((0, 8), (1, 16)))
    value_projection = normal_values(key_list[3], (MODEL_WIDTH, KEY_VALUE_HEADS * HEAD_WIDTH), MODEL_WIDTH ** -0.5, 0.125, ((0, 8), (1, 16)))
    query_norm_gain = jnp.clip(jnp.exp(jax.random.uniform(key_list[4], (HEAD_WIDTH,), jnp.float32, math.log(0.5), math.log(2.5))), 0.5, 2.5)
    key_norm_gain = jnp.clip(jnp.exp(jax.random.uniform(key_list[5], (HEAD_WIDTH,), jnp.float32, math.log(0.5), math.log(2.5))), 0.5, 2.5)
    doc_lengths = jax.vmap(lambda own: ragged_sizes(own, DOCS, SEQ_LEN, 3 * SEQ_LEN // 4, 1))(jax.random.split(key_list[6], N_DP)).reshape((N_DP, DOCS)).astype(jnp.int32)
    out_cot = normal_values(key_list[7], (ROWS, QUERY_HEADS * HEAD_WIDTH), 1.0, 6.0, ((0, 8), (1, 16)))
    return {"tokens": tokens, "q_weight": q_weight, "key_projection": key_projection, "value_projection": value_projection, "query_norm_gain": query_norm_gain, "key_norm_gain": key_norm_gain, "doc_lengths": doc_lengths, "out_cot": out_cot}


score_scale = 168.0 ** (-0.5)
rope_base = 10000.0
norm_eps = 1e-06

def doc_layout(length_row, length):
    ends = jnp.cumsum(length_row, dtype=jnp.int32)
    starts = ends - length_row
    token = jnp.arange(length, dtype=jnp.int32)
    doc_index = lax.optimization_barrier(jnp.sum((token[:, None] >= ends[None, :]).astype(jnp.int32), axis=1, dtype=jnp.int32))
    member = doc_index[:, None] == jnp.arange(length_row.shape[0], dtype=jnp.int32)[None, :]
    position = token - lax.optimization_barrier(jnp.sum(jnp.where(member, starts[None, :], 0), axis=1, dtype=jnp.int32))
    return (doc_index, position)

def rope_tables(position, head_size):
    half = head_size // 2
    inverse = rope_base ** (-jnp.arange(half, dtype=jnp.float32) * (2.0 / head_size))
    angle = position.astype(jnp.float32)[:, None] * inverse[None, :]
    cosine = jnp.concatenate([jnp.cos(angle), jnp.cos(angle)], axis=1)
    sine = jnp.concatenate([jnp.sin(angle), jnp.sin(angle)], axis=1)
    return (cosine, sine)

def norm_rotate(vectors, gain, cosine, sine):
    factor = lax.rsqrt(lax.optimization_barrier(jnp.mean(vectors * vectors, axis=-1, keepdims=True)) + norm_eps)
    normed = vectors * factor * gain
    half = vectors.shape[-1] // 2
    turned = jnp.concatenate([-normed[..., half:], normed[..., :half]], axis=-1)
    return normed * cosine[:, None, :] + turned * sine[:, None, :]

def shape_heads(projected_rows, query_norm_gain, key_norm_gain, cosine, sine, query_heads, value_heads, head_size):
    length = projected_rows.shape[0]
    query_cols = query_heads * head_size
    key_columns = value_heads * head_size
    queries = projected_rows[:, :query_cols].reshape(length, query_heads, head_size)
    keys = projected_rows[:, query_cols:query_cols + key_columns].reshape(length, value_heads, head_size)
    values = projected_rows[:, query_cols + key_columns:].reshape(length, value_heads, head_size)
    return (norm_rotate(queries, query_norm_gain, cosine, sine), norm_rotate(keys, key_norm_gain, cosine, sine), values)

def band_mask(doc_index, query_start, key_start, query_rows, key_rows):
    query_pos = query_start + jnp.arange(query_rows, dtype=jnp.int32)
    key_pos = key_start + jnp.arange(key_rows, dtype=jnp.int32)
    query_doc = lax.dynamic_slice_in_dim(doc_index, query_start, query_rows, 0)
    key_doc = lax.dynamic_slice_in_dim(doc_index, key_start, key_rows, 0)
    spacing = query_pos[:, None] - key_pos[None, :]
    return (query_doc[:, None] == key_doc[None, :]) & (spacing >= 0) & (spacing < WINDOW)

def block_probs(query_part, key_part, allowed):
    scores = jnp.einsum('qhgd,khd->hgqk', query_part, key_part, preferred_element_type=jnp.float32) * score_scale
    weights = jnp.where(allowed[None, None], jnp.exp(scores), 0.0)
    return weights / lax.optimization_barrier(jnp.sum(weights, axis=-1, keepdims=True))

def layer_kernel(projected_rows, length_row, cotangent, query_norm_gain, key_norm_gain, query_heads, value_heads):
    length = projected_rows.shape[0]
    doc_index, position = doc_layout(length_row, length)
    cosine, sine = rope_tables(position, HEAD_WIDTH)
    (queries, keys, values), pull = jax.vjp(lambda inner: shape_heads(inner, query_norm_gain, key_norm_gain, cosine, sine, query_heads, value_heads, HEAD_WIDTH), projected_rows)
    group = query_heads // value_heads
    query_bf = queries.astype(jnp.bfloat16).reshape(length, value_heads, group, HEAD_WIDTH)
    key_bf = keys.astype(jnp.bfloat16)
    value_bf = values.astype(jnp.bfloat16)
    grad_out = cotangent.reshape(length, value_heads, group, HEAD_WIDTH)
    query_rows = min(512, length)
    key_rows = min(length, query_rows + WINDOW)
    blocks = length // query_rows

    def block_view(index):
        index = index.astype(jnp.int32)
        query_start = index * query_rows
        key_start = jnp.maximum(query_start + query_rows - key_rows, 0)
        query_part = lax.dynamic_slice_in_dim(query_bf, query_start, query_rows, 0)
        key_part = lax.dynamic_slice_in_dim(key_bf, key_start, key_rows, 0)
        value_part = lax.dynamic_slice_in_dim(value_bf, key_start, key_rows, 0)
        allowed = band_mask(doc_index, query_start, key_start, query_rows, key_rows)
        return (query_start, key_start, query_part, key_part, value_part, block_probs(query_part, key_part, allowed))

    def forward_block(index):
        _, _, _, _, value_part, probs = block_view(index)
        mixed = jnp.einsum('hgqk,khd->qhgd', probs.astype(jnp.bfloat16), value_part, preferred_element_type=jnp.float32)
        return mixed.astype(jnp.bfloat16).reshape(query_rows, query_heads * HEAD_WIDTH)
    head_output = lax.map(forward_block, jnp.arange(blocks, dtype=jnp.int32)).reshape(length, query_heads * HEAD_WIDTH)

    def backward_block(index, carry):
        grad_query, grad_key, grad_value = carry
        query_start, key_start, query_part, key_part, value_part, probs = block_view(index)
        grad_part = lax.dynamic_slice_in_dim(grad_out, query_start, query_rows, 0)
        probs_bf = probs.astype(jnp.bfloat16)
        value_term = jnp.einsum('hgqk,qhgd->khd', probs_bf, grad_part, preferred_element_type=jnp.float32)
        grad_probs = jnp.einsum('qhgd,khd->hgqk', grad_part, value_part, preferred_element_type=jnp.float32)
        delta = lax.optimization_barrier(jnp.sum(probs * grad_probs, axis=-1, keepdims=True))
        grad_scores = (probs * (grad_probs - delta)).astype(jnp.bfloat16)
        query_term = jnp.einsum('hgqk,khd->qhgd', grad_scores, key_part, preferred_element_type=jnp.float32) * score_scale
        key_term = jnp.einsum('hgqk,qhgd->khd', grad_scores, query_part, preferred_element_type=jnp.float32) * score_scale
        grad_query = lax.dynamic_update_slice_in_dim(grad_query, query_term, query_start, 0)
        grad_key = lax.dynamic_update_slice_in_dim(grad_key, lax.dynamic_slice_in_dim(grad_key, key_start, key_rows, 0) + key_term, key_start, 0)
        grad_value = lax.dynamic_update_slice_in_dim(grad_value, lax.dynamic_slice_in_dim(grad_value, key_start, key_rows, 0) + value_term, key_start, 0)
        return (grad_query, grad_key, grad_value)
    start_grads = (jnp.zeros((length, value_heads, group, HEAD_WIDTH), jnp.float32), jnp.zeros((length, value_heads, HEAD_WIDTH), jnp.float32), jnp.zeros((length, value_heads, HEAD_WIDTH), jnp.float32))
    grad_query, grad_key, grad_value = lax.fori_loop(0, blocks, backward_block, start_grads)
    projection_gradient, = pull((grad_query.reshape(length, query_heads, HEAD_WIDTH), grad_key, grad_value))
    return (head_output, projection_gradient.astype(jnp.bfloat16))

def reference(tokens, q_weight, key_projection, value_projection, query_norm_gain, key_norm_gain, doc_lengths, out_cot):
    joined = jnp.concatenate([q_weight, key_projection, value_projection], axis=1)
    query_cols = QUERY_HEADS * HEAD_WIDTH
    key_columns = KEY_VALUE_HEADS * HEAD_WIDTH

    def one_row(grads, row):
        row = row.astype(jnp.int32)
        first = row * SEQ_LEN
        row_tokens = lax.dynamic_slice_in_dim(tokens, first, SEQ_LEN, 0)
        row_cotangent = lax.dynamic_slice_in_dim(out_cot, first, SEQ_LEN, 0)
        length_row = lax.dynamic_index_in_dim(doc_lengths, row, 0, keepdims=False)
        projected_rows = jnp.dot(row_tokens, joined, preferred_element_type=jnp.float32)
        head_output, projection_gradient = layer_kernel(projected_rows, length_row, row_cotangent, query_norm_gain, key_norm_gain, QUERY_HEADS, KEY_VALUE_HEADS)

        def add_group(index, summed):
            index = index.astype(jnp.int32)
            pieces = []
            weights = []
            for base, width in ((0, HQ_DEV * HEAD_WIDTH), (query_cols, KV_DEV * HEAD_WIDTH), (query_cols + key_columns, KV_DEV * HEAD_WIDTH)):
                first_col = base + index * width
                pieces.append(lax.dynamic_slice_in_dim(projection_gradient, first_col, width, 1))
                weights.append(lax.dynamic_slice_in_dim(joined, first_col, width, 1))
            group_grad = jnp.concatenate(pieces, axis=1)
            group_weight = jnp.concatenate(weights, axis=1)
            term = lax.dot_general(group_grad, group_weight, (((1,), (1,)), ((), ())), preferred_element_type=jnp.float32)
            rounded = lax.optimization_barrier(term.astype(jnp.bfloat16))
            return summed + rounded.astype(jnp.float32)
        token_grad = lax.fori_loop(0, QUERY_HEADS // HQ_DEV, add_group, jnp.zeros((SEQ_LEN, MODEL_WIDTH), jnp.float32)).astype(jnp.bfloat16)
        grads = grads + lax.dot_general(row_tokens, projection_gradient, (((0,), (0,)), ((), ())), preferred_element_type=jnp.float32)
        return (grads, (head_output, token_grad))
    start_grads = jnp.zeros((MODEL_WIDTH, query_cols + 2 * key_columns), jnp.float32)
    grads, (outs, token_grads) = lax.scan(one_row, start_grads, jnp.arange(N_DP, dtype=jnp.int32))
    attn_out = outs.reshape(N_DP * SEQ_LEN, query_cols)
    token_grad = token_grads.reshape(N_DP * SEQ_LEN, MODEL_WIDTH)
    return (attn_out, token_grad, grads[:, :query_cols], grads[:, query_cols:query_cols + key_columns], grads[:, query_cols + key_columns:])
```

```python
import functools
import math

import jax
import jax.numpy as jnp
from jax import lax
from jax.experimental import pallas as pl
from jax.experimental.pallas import tpu as pltpu
from jax.sharding import PartitionSpec as P

HEAD = 128
WINDOW = 1024
BLOCK = 256
score_scale = 168.0 ** (-0.5)
exp_scale = score_scale * math.log2(math.e)
rope_base = 10000.0
norm_eps = 1e-06
NN = (((1,), (0,)), ((), ()))
NT = (((1,), (1,)), ((), ()))


def mm(a, b, dims=NN):
    return lax.dot_general(a, b, dims, preferred_element_type=jnp.float32)


def rope_inputs(length_row, length):
    ends = jnp.cumsum(length_row, dtype=jnp.int32)
    token = jnp.arange(length, dtype=jnp.int32)
    start = jnp.max(jnp.where(token[:, None] >= ends[None, :], ends[None, :], 0), axis=1)
    position = token - start
    half = HEAD // 2
    inverse = rope_base ** (-jnp.arange(half, dtype=jnp.float32) * (2.0 / HEAD))
    angle = position.astype(jnp.float32)[:, None] * inverse[None, :]
    cosine, sine = jnp.cos(angle), jnp.sin(angle)
    return (
        jnp.concatenate([cosine, cosine], axis=1),
        jnp.concatenate([-sine, sine], axis=1),
        ends,
    )


def norm_factor(x):
    return lax.rsqrt(jnp.mean(x * x, axis=-1, keepdims=True) + norm_eps)


def rotate(n, cosine, sine):
    return n * cosine + pltpu.roll(n, HEAD // 2, 1) * sine


def rotate_back(g, cosine, sine):
    return g * cosine + pltpu.roll(g * sine, HEAD // 2, 1)


def norm_back(dn, x, gain):
    factor = norm_factor(x)
    dn = dn * gain
    inner = jnp.sum(x * dn, axis=-1, keepdims=True) * (1.0 / HEAD)
    return factor * dn - x * (factor * factor * factor * inner)


def attention_kernel(
    ends_ref, proj_ref, cot_ref, cos_ref, sin_ref, gq_ref, gk_ref, out_ref, dproj_ref,
    q_s, k_s, kt_s, v_s, vt_s, e_s, eb_s, dk_s, dv_s, acc_s, dot_s, row_s,
):
    length = proj_ref.shape[0]
    blocks = length // BLOCK
    span = WINDOW // BLOCK
    e0, e1, e2 = ends_ref[0], ends_ref[1], ends_ref[2]

    def start_of(t):
        zero = t * 0
        return jnp.maximum(
            jnp.maximum(jnp.where(t >= e0, e0, zero), jnp.where(t >= e1, e1, zero)),
            jnp.where(t >= e2, e2, zero),
        )

    @pl.loop(0, blocks)
    def _(i):
        rows = pl.ds(pl.multiple_of(i * BLOCK, BLOCK), BLOCK)
        cosine, sine = cos_ref[rows, :], sin_ref[rows, :]
        for h in range(2):
            x = proj_ref[rows, h * HEAD : (h + 1) * HEAD]
            n = x * norm_factor(x) * gq_ref[...]
            q_s[i, h * BLOCK : (h + 1) * BLOCK, :] = rotate(n, cosine, sine).astype(jnp.bfloat16)
        x = proj_ref[rows, 2 * HEAD : 3 * HEAD]
        n = x * norm_factor(x) * gk_ref[...]
        key = rotate(n, cosine, sine)
        k_s[i] = key.astype(jnp.bfloat16)
        kt_s[i] = key.T.astype(jnp.bfloat16)
        value = proj_ref[rows, 3 * HEAD : 4 * HEAD]
        v_s[i] = value.astype(jnp.bfloat16)
        vt_s[i] = value.T.astype(jnp.bfloat16)
        dk_s[i] = jnp.zeros((BLOCK, HEAD), jnp.float32)
        dv_s[i] = jnp.zeros((BLOCK, HEAD), jnp.float32)

    @pl.loop(0, blocks)
    def _(i):
        q0 = i * BLOCK
        rows = pl.ds(pl.multiple_of(q0, BLOCK), BLOCK)
        token = q0 + lax.broadcasted_iota(jnp.int32, (1, BLOCK), 1)
        low = jnp.maximum(start_of(token), token - (WINDOW - 1))
        token2 = jnp.concatenate([token, token], axis=1)
        low2 = jnp.concatenate([low, low], axis=1)
        first = jnp.maximum(start_of(q0), q0 - (WINDOW - 1)) // BLOCK
        first = jnp.maximum(first, 0)

        acc_s[...] = jnp.zeros_like(acc_s)
        row_s[...] = jnp.zeros_like(row_s)
        query = q_s[i]

        @pl.loop(first, i + 1)
        def _(j):
            slot = j - i + span
            s = mm(k_s[j], query, NT)
            key_pos = j * BLOCK + lax.broadcasted_iota(jnp.int32, (BLOCK, 2 * BLOCK), 0)
            e = jnp.where((key_pos >= low2) & (key_pos <= token2), jnp.exp2(s * exp_scale), 0.0)
            e_s[slot] = e
            eb = e.astype(jnp.bfloat16)
            eb_s[slot] = eb
            row_s[...] += jnp.sum(e.reshape(BLOCK // 8, 8, 2 * BLOCK), axis=0)
            acc_s[...] += mm(vt_s[j], eb)

        inv = 1.0 / jnp.sum(row_s[...], axis=0, keepdims=True)
        out_t = acc_s[...] * inv
        dot = jnp.concatenate(
            [cot_ref[rows, h * HEAD : (h + 1) * HEAD].astype(jnp.float32).T for h in range(2)], axis=1
        )
        for h in range(2):
            out_ref[rows, h * HEAD : (h + 1) * HEAD] = (
                out_t[:, h * BLOCK : (h + 1) * BLOCK].T.astype(jnp.bfloat16)
            )
        delta = jnp.sum(out_t * dot, axis=0, keepdims=True) * inv
        dot_s[...] = (dot * inv).astype(jnp.bfloat16)
        acc_s[...] = jnp.zeros_like(acc_s)

        @pl.loop(first, i + 1)
        def _(j):
            slot = j - i + span
            dp = mm(v_s[j], dot_s[...])
            ds = (e_s[slot] * (dp - delta)).astype(jnp.bfloat16)
            dv_s[j] += mm(eb_s[slot], dot_s[...], NT)
            dk_s[j] += mm(ds, query)
            acc_s[...] += mm(kt_s[j], ds)

        cosine, sine = cos_ref[rows, :], sin_ref[rows, :]
        for h in range(2):
            g = acc_s[:, h * BLOCK : (h + 1) * BLOCK].T * score_scale
            x = proj_ref[rows, h * HEAD : (h + 1) * HEAD]
            dx = norm_back(rotate_back(g, cosine, sine), x, gq_ref[...])
            dproj_ref[rows, h * HEAD : (h + 1) * HEAD] = dx.astype(jnp.bfloat16)

    @pl.loop(0, blocks)
    def _(i):
        rows = pl.ds(pl.multiple_of(i * BLOCK, BLOCK), BLOCK)
        cosine, sine = cos_ref[rows, :], sin_ref[rows, :]
        x = proj_ref[rows, 2 * HEAD : 3 * HEAD]
        dx = norm_back(rotate_back(dk_s[i] * score_scale, cosine, sine), x, gk_ref[...])
        dproj_ref[rows, 2 * HEAD : 3 * HEAD] = dx.astype(jnp.bfloat16)
        dproj_ref[rows, 3 * HEAD : 4 * HEAD] = dv_s[i].astype(jnp.bfloat16)


def attention(ends, proj, cot, cosine, sine, gain_q, gain_k):
    length = proj.shape[0]
    blocks = length // BLOCK
    slots = WINDOW // BLOCK + 1
    vmem = pl.BlockSpec(memory_space=pltpu.VMEM)
    bf, f32 = jnp.bfloat16, jnp.float32
    return pl.pallas_call(
        attention_kernel,
        out_shape=(
            jax.ShapeDtypeStruct((length, 2 * HEAD), bf),
            jax.ShapeDtypeStruct((length, 4 * HEAD), bf),
        ),
        in_specs=[pl.BlockSpec(memory_space=pltpu.SMEM)] + [vmem] * 6,
        out_specs=(vmem, vmem),
        scratch_shapes=[
            pltpu.VMEM((blocks, 2 * BLOCK, HEAD), bf),
            pltpu.VMEM((blocks, BLOCK, HEAD), bf),
            pltpu.VMEM((blocks, HEAD, BLOCK), bf),
            pltpu.VMEM((blocks, BLOCK, HEAD), bf),
            pltpu.VMEM((blocks, HEAD, BLOCK), bf),
            pltpu.VMEM((slots, BLOCK, 2 * BLOCK), f32),
            pltpu.VMEM((slots, BLOCK, 2 * BLOCK), bf),
            pltpu.VMEM((blocks, BLOCK, HEAD), f32),
            pltpu.VMEM((blocks, BLOCK, HEAD), f32),
            pltpu.VMEM((HEAD, 2 * BLOCK), f32),
            pltpu.VMEM((HEAD, 2 * BLOCK), bf),
            pltpu.VMEM((8, 2 * BLOCK), f32),
        ],
        compiler_params=pltpu.CompilerParams(vmem_limit_bytes=48 * 1024 * 1024),
        name="attention",
    )(ends, proj, cot, cosine, sine, gain_q.reshape(1, HEAD), gain_k.reshape(1, HEAD))


def local(
    tokens, q_weight, key_projection, value_projection, query_norm_gain, key_norm_gain, doc_lengths, out_cot
):
    joined = jnp.concatenate([q_weight, key_projection, value_projection], axis=1)
    joined = lax.all_gather(joined, "dp", axis=0, tiled=True)
    row_tokens = lax.all_gather(tokens, "seq", axis=0, tiled=True)
    cosine, sine, ends = rope_inputs(doc_lengths[0], row_tokens.shape[0])
    proj = jnp.dot(row_tokens, joined, preferred_element_type=jnp.float32)
    head_output, dproj = attention(ends, proj, out_cot, cosine, sine, query_norm_gain, key_norm_gain)
    token_grad = lax.psum_scatter(
        lax.dot_general(dproj, joined, NT, preferred_element_type=jnp.float32).astype(jnp.bfloat16),
        "seq",
        scatter_dimension=0,
        tiled=True,
    )
    weight_terms = lax.dot_general(
        row_tokens, dproj, (((0,), (0,)), ((), ())), preferred_element_type=jnp.float32
    ).astype(jnp.bfloat16)
    grads = lax.psum_scatter(weight_terms, "dp", scatter_dimension=0, tiled=True).astype(jnp.float32)
    attn_out = lax.all_to_all(head_output, "seq", split_axis=0, concat_axis=1, tiled=True)
    qc = q_weight.shape[1]
    kc = key_projection.shape[1]
    return (attn_out, token_grad, grads[:, :qc], grads[:, qc : qc + kc], grads[:, qc + kc :])


def solution(mesh):
    placed = (
        P(("dp", "seq"), None),
        P("dp", "seq"),
        P("dp", "seq"),
        P("dp", "seq"),
        P(),
        P(),
        P("dp", None),
        P("dp", "seq"),
    )
    return jax.shard_map(
        local,
        mesh=mesh,
        in_specs=placed,
        out_specs=(
            P(("dp", "seq"), None),
            P(("dp", "seq"), None),
            P("dp", "seq"),
            P("dp", "seq"),
            P("dp", "seq"),
        ),
        check_vma=False,
    )
```

```python
import functools
import math

import jax
import jax.numpy as jnp
from jax import lax
from jax.experimental import pallas as pl
from jax.experimental.pallas import tpu as pltpu
from jax.sharding import PartitionSpec as P

HEAD = 128
WINDOW = 1024
BLOCK = 256
score_scale = 168.0 ** (-0.5)
exp_scale = score_scale * math.log2(math.e)
rope_base = 10000.0
norm_eps = 1e-06
NN = (((1,), (0,)), ((), ()))
NT = (((1,), (1,)), ((), ()))


def mm(a, b, dims=NN):
    return lax.dot_general(a, b, dims, preferred_element_type=jnp.float32)


def rope_inputs(length):
    position = jnp.arange(length, dtype=jnp.int32)
    half = HEAD // 2
    inverse = rope_base ** (-jnp.arange(half, dtype=jnp.float32) * (2.0 / HEAD))
    angle = position.astype(jnp.float32)[:, None] * inverse[None, :]
    cosine, sine = jnp.cos(angle), jnp.sin(angle)
    return (
        jnp.concatenate([cosine, cosine], axis=1),
        jnp.concatenate([-sine, sine], axis=1),
    )


def norm_factor(x):
    return lax.rsqrt(jnp.mean(x * x, axis=-1, keepdims=True) + norm_eps)


def rotate(n, cosine, sine):
    return n * cosine + pltpu.roll(n, HEAD // 2, 1) * sine


def rotate_back(g, cosine, sine):
    return g * cosine + pltpu.roll(g * sine, HEAD // 2, 1)


def norm_back(dn, x, gain):
    factor = norm_factor(x)
    dn = dn * gain
    inner = jnp.sum(x * dn, axis=-1, keepdims=True) * (1.0 / HEAD)
    return factor * dn - x * (factor * factor * factor * inner)


def attention_kernel(
    docs_ref, docs2_ref, proj_ref, cot_own, cot_got, cos_ref, sin_ref, gq_ref, gk_ref, out_ref, dproj_ref,
    cot_ref, cot_sem, q_s, k_s, kt_s, v_s, vt_s, e_s, eb_s, dk_s, dv_s, acc_s, dot_s, row_s,
):
    length = proj_ref.shape[0]
    blocks = length // BLOCK
    span = WINDOW // BLOCK
    same = docs_ref[0, 4] == 1
    pl.when(same)(lambda: pltpu.make_async_copy(cot_own, cot_ref, cot_sem).start())
    pl.when(jnp.logical_not(same))(lambda: pltpu.make_async_copy(cot_got, cot_ref, cot_sem).start())
    e0, e1, e2 = [jnp.where(same, docs_ref[0, k], docs2_ref[0, k]) for k in range(3)]
    e1 = e0 + e1
    e2 = e1 + e2

    def start_of(t):
        zero = t * 0
        return jnp.maximum(
            jnp.maximum(jnp.where(t >= e0, e0, zero), jnp.where(t >= e1, e1, zero)),
            jnp.where(t >= e2, e2, zero),
        )

    @pl.loop(0, blocks)
    def _(i):
        rows = pl.ds(pl.multiple_of(i * BLOCK, BLOCK), BLOCK)
        cosine, sine = cos_ref[rows, :], sin_ref[rows, :]
        for h in range(2):
            x = proj_ref[rows, h * HEAD : (h + 1) * HEAD]
            n = x * norm_factor(x) * gq_ref[...]
            q_s[i, h * BLOCK : (h + 1) * BLOCK, :] = rotate(n, cosine, sine).astype(jnp.bfloat16)
        x = proj_ref[rows, 2 * HEAD : 3 * HEAD]
        n = x * norm_factor(x) * gk_ref[...]
        key = rotate(n, cosine, sine)
        k_s[i] = key.astype(jnp.bfloat16)
        kt_s[i] = key.T.astype(jnp.bfloat16)
        value = proj_ref[rows, 3 * HEAD : 4 * HEAD]
        v_s[i] = value.astype(jnp.bfloat16)
        vt_s[i] = value.T.astype(jnp.bfloat16)
        dk_s[i] = jnp.zeros((BLOCK, HEAD), jnp.float32)
        dv_s[i] = jnp.zeros((BLOCK, HEAD), jnp.float32)

    pltpu.make_async_copy(cot_own, cot_ref, cot_sem).wait()

    @pl.loop(0, blocks)
    def _(i):
        q0 = i * BLOCK
        rows = pl.ds(pl.multiple_of(q0, BLOCK), BLOCK)
        token = q0 + lax.broadcasted_iota(jnp.int32, (1, BLOCK), 1)
        low = jnp.maximum(start_of(token), token - (WINDOW - 1))
        token2 = jnp.concatenate([token, token], axis=1)
        low2 = jnp.concatenate([low, low], axis=1)
        first = jnp.maximum(start_of(q0), q0 - (WINDOW - 1)) // BLOCK
        first = jnp.maximum(first, 0)

        acc_s[...] = jnp.zeros_like(acc_s)
        row_s[...] = jnp.zeros_like(row_s)
        query = q_s[i]

        @pl.loop(first, i + 1)
        def _(j):
            slot = j - i + span
            s = mm(k_s[j], query, NT)
            key_pos = j * BLOCK + lax.broadcasted_iota(jnp.int32, (BLOCK, 2 * BLOCK), 0)
            e = jnp.where((key_pos >= low2) & (key_pos <= token2), jnp.exp2(s * exp_scale), 0.0)
            e_s[slot] = e
            eb = e.astype(jnp.bfloat16)
            eb_s[slot] = eb
            row_s[...] += jnp.sum(e.reshape(BLOCK // 8, 8, 2 * BLOCK), axis=0)
            acc_s[...] += mm(vt_s[j], eb)

        inv = 1.0 / jnp.sum(row_s[...], axis=0, keepdims=True)
        out_t = acc_s[...] * inv
        dot = jnp.concatenate(
            [cot_ref[rows, h * HEAD : (h + 1) * HEAD].astype(jnp.float32).T for h in range(2)], axis=1
        )
        for h in range(2):
            out_ref[rows, h * HEAD : (h + 1) * HEAD] = (
                out_t[:, h * BLOCK : (h + 1) * BLOCK].T.astype(jnp.bfloat16)
            )
        delta = jnp.sum(out_t * dot, axis=0, keepdims=True) * inv
        dot_s[...] = (dot * inv).astype(jnp.bfloat16)
        acc_s[...] = jnp.zeros_like(acc_s)

        @pl.loop(first, i + 1)
        def _(j):
            slot = j - i + span
            dp = mm(v_s[j], dot_s[...])
            ds = (e_s[slot] * (dp - delta)).astype(jnp.bfloat16)
            dv_s[j] += mm(eb_s[slot], dot_s[...], NT)
            dk_s[j] += mm(ds, query)
            acc_s[...] += mm(kt_s[j], ds)

        cosine, sine = cos_ref[rows, :], sin_ref[rows, :]
        for h in range(2):
            g = acc_s[:, h * BLOCK : (h + 1) * BLOCK].T * score_scale
            x = proj_ref[rows, h * HEAD : (h + 1) * HEAD]
            dx = norm_back(rotate_back(g, cosine, sine), x, gq_ref[...])
            dproj_ref[rows, h * HEAD : (h + 1) * HEAD] = dx.astype(jnp.bfloat16)

    @pl.loop(0, blocks)
    def _(i):
        rows = pl.ds(pl.multiple_of(i * BLOCK, BLOCK), BLOCK)
        cosine, sine = cos_ref[rows, :], sin_ref[rows, :]
        x = proj_ref[rows, 2 * HEAD : 3 * HEAD]
        dx = norm_back(rotate_back(dk_s[i] * score_scale, cosine, sine), x, gk_ref[...])
        dproj_ref[rows, 2 * HEAD : 3 * HEAD] = dx.astype(jnp.bfloat16)
        dproj_ref[rows, 3 * HEAD : 4 * HEAD] = dv_s[i].astype(jnp.bfloat16)


def attention(docs, docs2, proj, cot, cot2, cosine, sine, gain_q, gain_k):
    length = proj.shape[0]
    blocks = length // BLOCK
    slots = WINDOW // BLOCK + 1
    vmem = pl.BlockSpec(memory_space=pltpu.VMEM)
    bf, f32 = jnp.bfloat16, jnp.float32
    return pl.pallas_call(
        attention_kernel,
        out_shape=(
            jax.ShapeDtypeStruct((length, 2 * HEAD), bf),
            jax.ShapeDtypeStruct((length, 4 * HEAD), bf),
        ),
        in_specs=[pl.BlockSpec(memory_space=pltpu.SMEM)] * 2
        + [vmem, pl.BlockSpec(memory_space=pl.ANY), pl.BlockSpec(memory_space=pl.ANY)]
        + [vmem] * 4,
        out_specs=(vmem, vmem),
        scratch_shapes=[
            pltpu.VMEM((length, 2 * HEAD), bf),
            pltpu.SemaphoreType.DMA(()),
            pltpu.VMEM((blocks, 2 * BLOCK, HEAD), bf),
            pltpu.VMEM((blocks, BLOCK, HEAD), bf),
            pltpu.VMEM((blocks, HEAD, BLOCK), bf),
            pltpu.VMEM((blocks, BLOCK, HEAD), bf),
            pltpu.VMEM((blocks, HEAD, BLOCK), bf),
            pltpu.VMEM((slots, BLOCK, 2 * BLOCK), f32),
            pltpu.VMEM((slots, BLOCK, 2 * BLOCK), bf),
            pltpu.VMEM((blocks, BLOCK, HEAD), f32),
            pltpu.VMEM((blocks, BLOCK, HEAD), f32),
            pltpu.VMEM((HEAD, 2 * BLOCK), f32),
            pltpu.VMEM((HEAD, 2 * BLOCK), bf),
            pltpu.VMEM((8, 2 * BLOCK), f32),
        ],
        compiler_params=pltpu.CompilerParams(vmem_limit_bytes=48 * 1024 * 1024),
        name="attention",
    )(docs, docs2, proj, cot, cot2, cosine, sine, gain_q.reshape(1, HEAD), gain_k.reshape(1, HEAD))


MESH = pl.DeviceIdType.MESH
KH = 1408
HALF_ROWS = 64


class Place:
    def __init__(self):
        d, s = lax.axis_index("dp"), lax.axis_index("seq")
        self.z, self.c = d // 2, d % 2
        self.y, self.x = s // 4, s % 4
        self.t = self.x // 2
        self.xp = 3 - self.x
        self.xs = self.x + 1 - 2 * (self.x % 2)
        self.xsp = 3 - self.xs
        self.up_y, self.down_y, self.far_y = (self.y + 1) % 4, (self.y + 3) % 4, (self.y + 2) % 4
        self.same = self.c == self.t
        self.beside = self.at(x=self.xs)
        self.up, self.down = self.at(y=self.up_y), self.at(y=self.down_y)
        self.sibling = self.at(c=1 - self.c)

    def at(self, z=None, c=None, y=None, x=None):
        z = self.z if z is None else z
        c = self.c if c is None else c
        y = self.y if y is None else y
        x = self.x if x is None else x
        return (z * 2 + c, y * 4 + x)


class Sends:
    def __init__(self, sems):
        self.sems, self.count, self.open = sems, 0, []

    def sem(self):
        self.count += 1
        return self.sems.at[self.count - 1]

    def send(self, src, dst, recv, device, when=None):
        copy = pltpu.make_async_remote_copy(
            src_ref=src, dst_ref=dst, send_sem=self.sem(), recv_sem=recv,
            device_id=device, device_id_type=MESH,
        )
        if when is None:
            copy.start()
        else:
            pl.when(when)(copy.start)
        self.open.append((copy, when))

    def finish(self):
        for copy, when in self.open:
            if when is None:
                copy.wait_send()
            else:
                pl.when(when)(copy.wait_send)


def arrive(dst, sem):
    pltpu.make_async_copy(dst, dst, sem).wait()


def gather_kernel(
    tok2, wj, cot, docs, proj_out, tok_out, w_out, cot_out, docs_out,
    tok, w, wx, other, sib, send_s, p_s, q_s, first_s, w_s, misc_s, sib_s, local_s,
):
    me = Place()
    z, c, y, x, t, same = me.z, me.c, me.y, me.x, me.t, me.same
    sends = Sends(send_s)
    width = 4 * HEAD
    part = {"p": (pl.ds(0, HALF_ROWS), p_s), "q": (pl.ds(HALF_ROWS, HALF_ROWS), q_s)}
    piece_rows = wj.shape[0]

    def forward(name, slot, device):
        rows, sems = part[name]
        ref = tok.at[slot, rows, :]
        sends.send(ref, ref, sems.at[slot], device)

    def landed(name, slot):
        rows, sems = part[name]
        arrive(tok.at[slot, rows, :], sems.at[slot])

    own, pair = y * 4 + x, y * 4 + me.xp
    target_x = jnp.where(same, x, me.xp)
    first = first_s.at[jnp.where(same, 0, 1)]
    for k in range(2):
        local = same & (c == k)
        sends.send(tok2.at[k], tok.at[own], first, me.at(c=k, x=target_x), when=jnp.logical_not(local))

        @pl.when(local)
        def _():
            pltpu.make_async_copy(tok2.at[k], tok.at[own], first_s.at[0]).start()

    sends.send(wj, wx, misc_s.at[0], me.at(x=me.xp))
    sends.send(docs, docs_out, misc_s.at[2], me.sibling)

    target_c = z // 2
    piece = (z % 2) * 2 + c

    def spread(src, g):
        rows = pl.ds(pl.multiple_of(piece * piece_rows, 16), piece_rows)
        dst = w.at[rows, pl.ds(pl.multiple_of(g * width, width), width)]
        sem = w_s.at[piece * 2 + g]
        here = target_c == c
        for k in (1, 3, 2):
            sends.send(src, dst, sem, me.at(z=(z + k) % 4, c=target_c))
        sends.send(src, dst, sem, me.sibling, when=jnp.logical_not(here))

        @pl.when(here)
        def _():
            pltpu.make_async_copy(src, dst, sem).start()

    w[pl.ds(4 * piece_rows, KH - 4 * piece_rows), :] = jnp.zeros((KH - 4 * piece_rows, 2 * width), jnp.bfloat16)
    for slot, sem in ((own, 0), (pair, 1)):
        arrive(tok.at[slot], first_s.at[sem])
        forward("q", slot, me.up)
        forward("q", slot, me.down)
        forward("p", slot, me.beside)
        forward("p", slot, me.up)
        forward("p", slot, me.down)
        forward("q", slot, me.beside)
        if sem == 0:
            spread(wj, t)
    arrive(wx, misc_s.at[0])
    spread(wx, 1 - t)
    swap = jnp.logical_not(same)
    sends.send(cot, cot_out, misc_s.at[1], me.at(c=1 - c, x=me.xp), when=swap)

    for column in (me.xs, me.xsp):
        slot = y * 4 + column
        landed("p", slot)
        forward("p", slot, me.up)
        forward("p", slot, me.down)
    below, above, far = me.down_y * 4, me.up_y * 4, me.far_y * 4
    landed("q", below + x)
    forward("q", below + x, me.up)
    forward("q", below + x, me.beside)
    landed("q", above + me.xp)
    forward("q", above + me.xp, me.down)
    forward("q", above + me.xp, me.beside)
    landed("q", below + me.xp)
    forward("q", below + me.xp, me.beside)
    landed("q", above + x)
    forward("q", above + x, me.beside)
    for column in (x, me.xp):
        landed("p", below + column)
        forward("p", below + column, me.up)
    for column in (me.xs, me.xsp):
        landed("p", above + column)
        forward("p", above + column, me.down)
    for column in (x, me.xp):
        landed("q", far + column)
        forward("q", far + column, me.beside)

    for i in range(4):
        for g in range(2):
            arrive(
                w.at[pl.ds(i * piece_rows, piece_rows), pl.ds(g * width, width)], w_s.at[i * 2 + g]
            )
    pltpu.make_async_copy(w, w_out, local_s.at[4]).start()

    beside = (me.xs, me.xsp)
    here = (x, me.xp)
    plan = (
        (me.y, (), beside),
        (me.down_y, beside, beside),
        (me.up_y, here, beside),
        (me.far_y, here + beside, beside),
    )
    for n, (row, need_p, need_q) in enumerate(plan):
        for column in need_p:
            landed("p", row * 4 + column)
        for column in need_q:
            landed("q", row * 4 + column)
        slots = pl.ds(pl.multiple_of(row * 4, 4), 4)
        rows = pl.ds(pl.multiple_of(row * 512, 512), 512)
        pltpu.make_async_copy(tok.at[slots], tok_out.at[slots], local_s.at[n]).start()
        block = tok[slots].reshape(512, KH)
        other[rows, :] = mm(block, w[:, pl.ds(pl.multiple_of((1 - c) * width, width), width)])
        sends.send(other.at[rows, :], sib.at[rows, :], sib_s.at[n], me.sibling)
        proj_out[rows, :] = mm(block, w[:, pl.ds(pl.multiple_of(c * width, width), width)])
    for n, (row, _, _) in enumerate(plan):
        rows = pl.ds(pl.multiple_of(row * 512, 512), 512)
        arrive(sib.at[rows, :], sib_s.at[n])
        proj_out[rows, :] += sib[rows, :]
        slots = pl.ds(pl.multiple_of(row * 4, 4), 4)
        pltpu.make_async_copy(tok.at[slots], tok_out.at[slots], local_s.at[n]).wait()
    pltpu.make_async_copy(w, w_out, local_s.at[4]).wait()
    arrive(docs_out, misc_s.at[2])
    pl.when(swap)(lambda: arrive(cot_out, misc_s.at[1]))
    sends.finish()


def gather(tok2, wj, cot, docs):
    f32, bf = jnp.float32, jnp.bfloat16
    anywhere = pl.BlockSpec(memory_space=pl.ANY)
    dma = pltpu.SemaphoreType.DMA
    length = cot.shape[0]
    return pl.pallas_call(
        gather_kernel,
        out_shape=(
            jax.ShapeDtypeStruct((length, 4 * HEAD), f32),
            jax.ShapeDtypeStruct((16, 128, KH), bf),
            jax.ShapeDtypeStruct((KH, 8 * HEAD), bf),
            jax.ShapeDtypeStruct(cot.shape, bf),
            jax.ShapeDtypeStruct(docs.shape, docs.dtype),
        ),
        in_specs=[anywhere] * 4,
        out_specs=(pl.BlockSpec(memory_space=pltpu.VMEM),) + (anywhere,) * 4,
        scratch_shapes=[
            pltpu.VMEM((16, 128, KH), bf),
            pltpu.VMEM((KH, 8 * HEAD), bf),
            pltpu.VMEM(wj.shape, bf),
            pltpu.VMEM((length, 4 * HEAD), f32),
            pltpu.VMEM((length, 4 * HEAD), f32),
            dma((60,)), dma((16,)), dma((16,)), dma((2,)), dma((8,)), dma((3,)), dma((4,)), dma((5,)),
        ],
        compiler_params=pltpu.CompilerParams(
            has_side_effects=True, vmem_limit_bytes=56 * 1024 * 1024
        ),
        name="gather",
    )(tok2, wj, cot, docs)


def scatter_kernel(
    attn, dproj, tok_in, w_in, attn_out, grad_out, gq_out, gk_out, gv_out,
    tok, w, dpj, terms, dw, rqx, rp1, rp2, rpx, rq1, rq2, rw,
    send_s, attn_s, dp_s, local_s, qx_s, p1_s, p2_s, px_s, q1_s, q2_s, rw_s, g_s,
):
    me = Place()
    z, c, y, x, t, same = me.z, me.c, me.y, me.x, me.t, me.same
    sends = Sends(send_s)
    width = 4 * HEAD
    p_rows, q_rows = pl.ds(0, HALF_ROWS), pl.ds(HALF_ROWS, HALF_ROWS)
    order = (me.far_y, me.up_y, me.down_y, y)
    mine = pl.ds(pl.multiple_of(c * width, width), width)
    piece_rows = gq_out.shape[0]

    pltpu.make_async_copy(w_in, w, local_s.at[4]).start()
    for n, row in enumerate(order):
        rows = pl.ds(pl.multiple_of(row * 512, 512), 512)
        pltpu.make_async_copy(dproj.at[rows, :], dpj.at[rows, mine], local_s.at[n]).start()
        sends.send(dproj.at[rows, :], dpj.at[rows, mine], dp_s.at[n], me.sibling)
    pltpu.make_async_copy(tok_in, tok, local_s.at[5]).start()

    def add(dst, *sources):
        total = dst[...].astype(jnp.float32)
        for source in sources:
            total = total + source[...].astype(jnp.float32)
        dst[...] = total.astype(jnp.bfloat16)

    def compute(n):
        row = order[n]
        rows = pl.ds(pl.multiple_of(row * 512, 512), 512)
        arrive(dpj.at[rows, pl.ds(0, width)], local_s.at[n])
        arrive(dpj.at[rows, pl.ds(0, width)], dp_s.at[n])
        if n == 0:
            arrive(w, local_s.at[4])
        slots = pl.ds(pl.multiple_of(row * 4, 4), 4)
        term = mm(dpj[rows, :], w[...], NT).astype(jnp.bfloat16)
        terms[slots] = term.reshape(4, 128, KH)
        for k, column in enumerate((me.xs, me.xsp)):
            sends.send(terms.at[row * 4 + column, q_rows, :], rqx.at[n, k], qx_s.at[n, k], me.beside)

    far, up, down, own = me.far_y * 4, me.up_y * 4, me.down_y * 4, y * 4
    compute(0)
    sends.send(terms.at[pl.ds(far, 2), p_rows, :], rp1.at[0], p1_s.at[0], me.up)
    sends.send(terms.at[pl.ds(far + 2, 2), p_rows, :], rp1.at[1], p1_s.at[1], me.down)
    compute(1)
    compute(2)
    compute(3)
    arrive(rp1.at[0], p1_s.at[0])
    add(terms.at[pl.ds(up, 2), p_rows, :], rp1.at[0])
    sends.send(terms.at[pl.ds(up, 4), p_rows, :], rp2.at[0], p2_s.at[0], me.up)
    arrive(rp1.at[1], p1_s.at[1])
    add(terms.at[pl.ds(down + 2, 2), p_rows, :], rp1.at[1])
    sends.send(terms.at[pl.ds(down, 4), p_rows, :], rp2.at[1], p2_s.at[1], me.down)

    group = y * 4 + jnp.where(same, x, me.xp)
    columns = pl.ds(pl.multiple_of(group * 2 * HEAD, 2 * HEAD), 2 * HEAD)
    for dy in range(4):
        for dx in range(4):
            to_y, to_x = (y + dy) % 4, (x + dx) % 4
            rows = pl.ds(pl.multiple_of((to_y * 4 + to_x) * 128, 128), 128)
            src, dst = attn.at[rows, :], attn_out.at[:, columns]
            if dy == 0 and dx == 0:
                sends.send(src, dst, attn_s.at[group], me.sibling, when=jnp.logical_not(same))

                @pl.when(same)
                def _():
                    pltpu.make_async_copy(src, dst, attn_s.at[group]).start()
            else:
                sends.send(src, dst, attn_s.at[group], me.at(c=t, y=to_y, x=to_x))

    def weight_terms(i):
        if i == 0:
            arrive(tok, local_s.at[5])
        low, high = i * 384, min(KH, i * 384 + 384)
        cut = min(high, 4 * piece_rows)
        left = tok[:, :, low:high].reshape(16 * 128, high - low)
        term = mm(left, dpj[...], (((0,), (0,)), ((), ())))
        dw[low:cut, :] = term[: cut - low].astype(jnp.bfloat16)
        for g in range(2):
            src = dw.at[pl.ds(i * piece_rows, piece_rows), pl.ds(g * width, width)]
            dst, sem = rw.at[z * 2 + t], rw_s.at[z * 2 + t]
            to_z, to_c = 2 * c + i // 2, i % 2
            stays = (to_z == z) & (c == to_c) & (t == g)
            sends.send(
                src, dst, sem, me.at(z=to_z, c=to_c, x=jnp.where(t == g, x, me.xp)),
                when=jnp.logical_not(stays),
            )

            @pl.when(stays)
            def _():
                pltpu.make_async_copy(src, dst, sem).start()

    def exchanged(n):
        for k, column in enumerate((x, me.xp)):
            arrive(rqx.at[n, k], qx_s.at[n, k])
            add(terms.at[order[n] * 4 + column, q_rows, :], rqx.at[n, k])

    weight_terms(0)
    exchanged(0)
    sends.send(terms.at[far + x, q_rows, :], rq1.at[0], q1_s.at[0], me.up)
    sends.send(terms.at[far + me.xp, q_rows, :], rq1.at[1], q1_s.at[1], me.down)
    weight_terms(1)
    for n, base, extra, device in ((1, up, x, me.up), (2, down, me.xp, me.down)):
        exchanged(n)
        arrive(rq1.at[n - 1], q1_s.at[n - 1])
        add(terms.at[base + extra, q_rows, :], rq1.at[n - 1])
        for k, column in enumerate((x, me.xp)):
            sends.send(terms.at[base + column, q_rows, :], rq2.at[n - 1, k], q2_s.at[n - 1, k], device)
    weight_terms(2)
    arrive(rp2.at[0], p2_s.at[0])
    arrive(rp2.at[1], p2_s.at[1])
    add(terms.at[pl.ds(own, 4), p_rows, :], rp2.at[0], rp2.at[1])
    for k, column in enumerate((me.xs, me.xsp)):
        sends.send(terms.at[own + column, p_rows, :], rpx.at[k], px_s.at[k], me.beside)
    weight_terms(3)
    for k, column in enumerate((x, me.xp)):
        arrive(rqx.at[3, k], qx_s.at[3, k])
        arrive(rq2.at[0, k], q2_s.at[0, k])
        arrive(rq2.at[1, k], q2_s.at[1, k])
        add(terms.at[own + column, q_rows, :], rqx.at[3, k], rq2.at[0, k], rq2.at[1, k])
        arrive(rpx.at[k], px_s.at[k])
        add(terms.at[own + column, p_rows, :], rpx.at[k])
    sends.send(terms.at[own + me.xp], grad_out.at[c], g_s.at[c], me.at(c=t, x=me.xp))
    src, dst = terms.at[own + x], grad_out.at[c]
    sends.send(src, dst, g_s.at[c], me.sibling, when=jnp.logical_not(same))

    @pl.when(same)
    def _():
        pltpu.make_async_copy(src, dst, g_s.at[c]).start()

    for k in range(8):
        arrive(rw.at[k], rw_s.at[k])
    total = rw[0].astype(jnp.float32)
    for k in range(1, 8):
        total = total + rw[k].astype(jnp.float32)
    gq_out[...] = total[:, : 2 * HEAD]
    gk_out[...] = total[:, 2 * HEAD : 3 * HEAD]
    gv_out[...] = total[:, 3 * HEAD :]
    for k in range(16):
        arrive(attn_out.at[:, pl.ds(k * 2 * HEAD, 2 * HEAD)], attn_s.at[k])
    for k in range(2):
        arrive(grad_out.at[k], g_s.at[k])
    sends.finish()


def scatter(attn, dproj, tok, w, piece_rows):
    f32, bf = jnp.float32, jnp.bfloat16
    anywhere = pl.BlockSpec(memory_space=pl.ANY)
    vmem = pl.BlockSpec(memory_space=pltpu.VMEM)
    dma = pltpu.SemaphoreType.DMA
    length = attn.shape[0]
    half = (HALF_ROWS, KH)
    return pl.pallas_call(
        scatter_kernel,
        out_shape=(
            jax.ShapeDtypeStruct((128, 32 * HEAD), bf),
            jax.ShapeDtypeStruct((2, 128, KH), bf),
            jax.ShapeDtypeStruct((piece_rows, 2 * HEAD), f32),
            jax.ShapeDtypeStruct((piece_rows, HEAD), f32),
            jax.ShapeDtypeStruct((piece_rows, HEAD), f32),
        ),
        in_specs=[anywhere] * 4,
        out_specs=(anywhere, anywhere, vmem, vmem, vmem),
        scratch_shapes=[
            pltpu.VMEM((16, 128, KH), bf),
            pltpu.VMEM((KH, 8 * HEAD), bf),
            pltpu.VMEM((length, 8 * HEAD), bf),
            pltpu.VMEM((16, 128, KH), bf),
            pltpu.VMEM((4 * piece_rows, 8 * HEAD), bf),
            pltpu.VMEM((4, 2) + half, bf),
            pltpu.VMEM((2, 2) + half, bf),
            pltpu.VMEM((2, 4) + half, bf),
            pltpu.VMEM((2,) + half, bf),
            pltpu.VMEM((2,) + half, bf),
            pltpu.VMEM((2, 2) + half, bf),
            pltpu.VMEM((8, piece_rows, 4 * HEAD), bf),
            dma((60,)), dma((16,)), dma((4,)), dma((6,)), dma((4, 2)), dma((2,)), dma((2,)),
            dma((2,)), dma((2,)), dma((2, 2)), dma((8,)), dma((2,)),
        ],
        compiler_params=pltpu.CompilerParams(
            has_side_effects=True, vmem_limit_bytes=56 * 1024 * 1024
        ),
        name="scatter",
    )(attn, dproj, tok, w)


def local(
    tokens, q_weight, key_projection, value_projection, query_norm_gain, key_norm_gain, doc_lengths, out_cot
):
    wj = jnp.concatenate([q_weight, key_projection, value_projection], axis=1)
    rows, model = tokens.shape
    half = model // 2
    tok2 = jnp.pad(
        tokens.reshape(rows, 2, half).transpose(1, 0, 2), ((0, 0), (0, 0), (0, KH - half))
    )
    same = (lax.axis_index("dp") % 2 == (lax.axis_index("seq") % 4) // 2).astype(jnp.int32)
    docs = jnp.concatenate([doc_lengths[0], same[None], jnp.zeros((123,), jnp.int32)])
    docs = jnp.broadcast_to(docs[None, :], (8, 128))
    cosine, sine = rope_inputs(out_cot.shape[0])
    proj, tok, w, cot2, docs2 = gather(tok2, wj, out_cot, docs)
    attn, dproj = attention(
        docs, docs2, proj, out_cot, cot2, cosine, sine, query_norm_gain, key_norm_gain
    )
    attn_out, grad, gq, gk, gv = scatter(attn, dproj, tok, w, wj.shape[0])
    token_grad = jnp.concatenate([grad[0, :, :half], grad[1, :, :half]], axis=1)
    return (attn_out, token_grad, gq, gk, gv)


def solution(mesh):
    placed = (
        P(("dp", "seq"), None),
        P("dp", "seq"),
        P("dp", "seq"),
        P("dp", "seq"),
        P(),
        P(),
        P("dp", None),
        P("dp", "seq"),
    )
    return jax.shard_map(
        local,
        mesh=mesh,
        in_specs=placed,
        out_specs=(
            P(("dp", "seq"), None),
            P(("dp", "seq"), None),
            P("dp", "seq"),
            P("dp", "seq"),
            P("dp", "seq"),
        ),
        check_vma=False,
    )
```

```python
import functools
import math

import jax
import jax.numpy as jnp
import numpy as np
from jax import lax
from jax.experimental import pallas as pl
from jax.experimental.pallas import tpu as pltpu
from jax.sharding import PartitionSpec as P

HEAD = 128
WINDOW = 1024
BLOCK = 256
score_scale = 168.0 ** (-0.5)
exp_scale = score_scale * math.log2(math.e)
rope_base = 10000.0
norm_eps = 1e-06
NN = (((1,), (0,)), ((), ()))
NT = (((1,), (1,)), ((), ()))


def mm(a, b, dims=NN):
    return lax.dot_general(a, b, dims, preferred_element_type=jnp.float32)


def rope_tables(blocks):
    inverse = rope_base ** (-np.arange(HEAD // 2) * (2.0 / HEAD))
    inverse = np.concatenate([inverse, inverse])[None, :]
    coarse = (np.arange(blocks) * BLOCK)[:, None] * inverse
    fine = np.arange(BLOCK)[:, None] * inverse
    return [
        jnp.asarray(table, jnp.float32)
        for table in (np.cos(coarse), np.sin(coarse), np.cos(fine), np.sin(fine))
    ]


def norm_factor(x):
    return lax.rsqrt(jnp.mean(x * x, axis=-1, keepdims=True) + norm_eps)


def rotate(n, cosine, sine):
    return n * cosine + pltpu.roll(n, HEAD // 2, 1) * sine


def rotate_back(g, cosine, sine):
    return g * cosine + pltpu.roll(g * sine, HEAD // 2, 1)


def norm_back(dn, x, gain):
    factor = norm_factor(x)
    dn = dn * gain
    inner = jnp.sum(x * dn, axis=-1, keepdims=True) * (1.0 / HEAD)
    return factor * dn - x * (factor * factor * factor * inner)


def attention_kernel(
    docs_ref, docs2_ref, proj_ref, cot_own, cot_got, cos_a, sin_a, cos_b, sin_b, gq_ref, gk_ref, out_ref, dproj_ref,
    cot_ref, cot_sem, q_s, k_s, kt_s, v_s, vt_s, e_s, eb_s, dk_s, dv_s, acc_s, dot_s, row_s,
):
    length = proj_ref.shape[0]
    blocks = length // BLOCK
    span = WINDOW // BLOCK
    same = lax.axis_index("dp") % 2 == (lax.axis_index("seq") % 4) // 2
    lane = lax.broadcasted_iota(jnp.int32, (1, HEAD), 1)
    sign = jnp.where(lane < HEAD // 2, -1.0, 1.0)

    def tables(i):
        ca, sa = cos_a[pl.ds(i, 1), :], sin_a[pl.ds(i, 1), :]
        return ca * cos_b[...] - sa * sin_b[...], (sa * sign) * cos_b[...] + (ca * sign) * sin_b[...]

    pl.when(same)(lambda: pltpu.make_async_copy(cot_own, cot_ref, cot_sem).start())
    pl.when(jnp.logical_not(same))(lambda: pltpu.make_async_copy(cot_got, cot_ref, cot_sem).start())
    e0, e1, e2 = [jnp.where(same, docs_ref[0, k], docs2_ref[0, k]) for k in range(3)]
    e1 = e0 + e1
    e2 = e1 + e2

    def start_of(t):
        zero = t * 0
        return jnp.maximum(
            jnp.maximum(jnp.where(t >= e0, e0, zero), jnp.where(t >= e1, e1, zero)),
            jnp.where(t >= e2, e2, zero),
        )

    @pl.loop(0, blocks)
    def _(i):
        rows = pl.ds(pl.multiple_of(i * BLOCK, BLOCK), BLOCK)
        cosine, sine = tables(i)
        for h in range(2):
            x = proj_ref[rows, h * HEAD : (h + 1) * HEAD]
            n = x * norm_factor(x) * gq_ref[...]
            q_s[i, h * BLOCK : (h + 1) * BLOCK, :] = rotate(n, cosine, sine).astype(jnp.bfloat16)
        x = proj_ref[rows, 2 * HEAD : 3 * HEAD]
        n = x * norm_factor(x) * gk_ref[...]
        key = rotate(n, cosine, sine)
        k_s[i] = key.astype(jnp.bfloat16)
        kt_s[i] = key.T.astype(jnp.bfloat16)
        value = proj_ref[rows, 3 * HEAD : 4 * HEAD]
        v_s[i] = value.astype(jnp.bfloat16)
        vt_s[i] = value.T.astype(jnp.bfloat16)
        dk_s[i] = jnp.zeros((BLOCK, HEAD), jnp.float32)
        dv_s[i] = jnp.zeros((BLOCK, HEAD), jnp.float32)

    pltpu.make_async_copy(cot_own, cot_ref, cot_sem).wait()

    @pl.loop(0, blocks)
    def _(i):
        q0 = i * BLOCK
        rows = pl.ds(pl.multiple_of(q0, BLOCK), BLOCK)
        token = q0 + lax.broadcasted_iota(jnp.int32, (1, BLOCK), 1)
        low = jnp.maximum(start_of(token), token - (WINDOW - 1))
        token2 = jnp.concatenate([token, token], axis=1)
        low2 = jnp.concatenate([low, low], axis=1)
        first = jnp.maximum(start_of(q0), q0 - (WINDOW - 1)) // BLOCK
        first = jnp.maximum(first, 0)

        acc_s[...] = jnp.zeros_like(acc_s)
        row_s[...] = jnp.zeros_like(row_s)
        query = q_s[i]

        last = q0 + BLOCK - 1
        whole = jnp.maximum(start_of(last), last - (WINDOW - 1))

        def forward(j, masked):
            slot = j - i + span
            e = jnp.exp2(mm(k_s[j], query, NT) * exp_scale)
            if masked:
                key_pos = j * BLOCK + lax.broadcasted_iota(jnp.int32, (BLOCK, 2 * BLOCK), 0)
                e = jnp.where((key_pos >= low2) & (key_pos <= token2), e, 0.0)
            e_s[slot] = e
            eb = e.astype(jnp.bfloat16)
            eb_s[slot] = eb
            row_s[...] += jnp.sum(e.reshape(BLOCK // 8, 8, 2 * BLOCK), axis=0)
            acc_s[...] += mm(vt_s[j], eb)

        @pl.loop(first, i + 1)
        def _(j):
            free = (j * BLOCK >= whole) & (j < i)
            pl.when(free)(lambda: forward(j, False))
            pl.when(jnp.logical_not(free))(lambda: forward(j, True))

        inv = 1.0 / jnp.sum(row_s[...], axis=0, keepdims=True)
        out_t = acc_s[...] * inv
        dot = jnp.concatenate(
            [cot_ref[rows, h * HEAD : (h + 1) * HEAD].astype(jnp.float32).T for h in range(2)], axis=1
        )
        for h in range(2):
            out_ref[rows, h * HEAD : (h + 1) * HEAD] = (
                out_t[:, h * BLOCK : (h + 1) * BLOCK].T.astype(jnp.bfloat16)
            )
        delta = jnp.sum(out_t * dot, axis=0, keepdims=True) * inv
        dot_s[...] = (dot * inv).astype(jnp.bfloat16)
        acc_s[...] = jnp.zeros_like(acc_s)

        @pl.loop(first, i + 1)
        def _(j):
            slot = j - i + span
            dp = mm(v_s[j], dot_s[...])
            ds = (e_s[slot] * (dp - delta)).astype(jnp.bfloat16)
            dv_s[j] += mm(eb_s[slot], dot_s[...], NT)
            dk_s[j] += mm(ds, query)
            acc_s[...] += mm(kt_s[j], ds)

        cosine, sine = tables(i)
        for h in range(2):
            g = acc_s[:, h * BLOCK : (h + 1) * BLOCK].T * score_scale
            x = proj_ref[rows, h * HEAD : (h + 1) * HEAD]
            dx = norm_back(rotate_back(g, cosine, sine), x, gq_ref[...])
            dproj_ref[rows, h * HEAD : (h + 1) * HEAD] = dx.astype(jnp.bfloat16)

    @pl.loop(0, blocks)
    def _(i):
        rows = pl.ds(pl.multiple_of(i * BLOCK, BLOCK), BLOCK)
        cosine, sine = tables(i)
        x = proj_ref[rows, 2 * HEAD : 3 * HEAD]
        dx = norm_back(rotate_back(dk_s[i] * score_scale, cosine, sine), x, gk_ref[...])
        dproj_ref[rows, 2 * HEAD : 3 * HEAD] = dx.astype(jnp.bfloat16)
        dproj_ref[rows, 3 * HEAD : 4 * HEAD] = dv_s[i].astype(jnp.bfloat16)


def attention(docs, docs2, proj, cot, cot2, gain_q, gain_k):
    length = proj.shape[0]
    blocks = length // BLOCK
    slots = WINDOW // BLOCK + 1
    vmem = pl.BlockSpec(memory_space=pltpu.VMEM)
    bf, f32 = jnp.bfloat16, jnp.float32
    return pl.pallas_call(
        attention_kernel,
        out_shape=(
            jax.ShapeDtypeStruct((length, 2 * HEAD), bf),
            jax.ShapeDtypeStruct((length, 4 * HEAD), bf),
        ),
        in_specs=[pl.BlockSpec(memory_space=pltpu.SMEM)] * 2
        + [vmem, pl.BlockSpec(memory_space=pl.ANY), pl.BlockSpec(memory_space=pl.ANY)]
        + [vmem] * 6,
        out_specs=(vmem, vmem),
        scratch_shapes=[
            pltpu.VMEM((length, 2 * HEAD), bf),
            pltpu.SemaphoreType.DMA(()),
            pltpu.VMEM((blocks, 2 * BLOCK, HEAD), bf),
            pltpu.VMEM((blocks, BLOCK, HEAD), bf),
            pltpu.VMEM((blocks, HEAD, BLOCK), bf),
            pltpu.VMEM((blocks, BLOCK, HEAD), bf),
            pltpu.VMEM((blocks, HEAD, BLOCK), bf),
            pltpu.VMEM((slots, BLOCK, 2 * BLOCK), f32),
            pltpu.VMEM((slots, BLOCK, 2 * BLOCK), bf),
            pltpu.VMEM((blocks, BLOCK, HEAD), f32),
            pltpu.VMEM((blocks, BLOCK, HEAD), f32),
            pltpu.VMEM((HEAD, 2 * BLOCK), f32),
            pltpu.VMEM((HEAD, 2 * BLOCK), bf),
            pltpu.VMEM((8, 2 * BLOCK), f32),
        ],
        compiler_params=pltpu.CompilerParams(vmem_limit_bytes=60 * 1024 * 1024),
        name="attention",
    )(docs, docs2, proj, cot, cot2, *rope_tables(blocks), gain_q.reshape(1, HEAD), gain_k.reshape(1, HEAD))


MESH = pl.DeviceIdType.MESH
KH = 1408
PAD = 64
HALF_ROWS = 64


class Place:
    def __init__(self):
        d, s = lax.axis_index("dp"), lax.axis_index("seq")
        self.z, self.c = d // 2, d % 2
        self.y, self.x = s // 4, s % 4
        self.t = self.x // 2
        self.xp = 3 - self.x
        self.xs = self.x + 1 - 2 * (self.x % 2)
        self.xsp = 3 - self.xs
        self.up_y, self.down_y, self.far_y = (self.y + 1) % 4, (self.y + 3) % 4, (self.y + 2) % 4
        self.same = self.c == self.t
        self.beside = self.at(x=self.xs)
        self.up, self.down = self.at(y=self.up_y), self.at(y=self.down_y)
        self.sibling = self.at(c=1 - self.c)

    def at(self, z=None, c=None, y=None, x=None):
        z = self.z if z is None else z
        c = self.c if c is None else c
        y = self.y if y is None else y
        x = self.x if x is None else x
        return (z * 2 + c, y * 4 + x)


class Sends:
    def __init__(self, sems):
        self.sems, self.count, self.open = sems, 0, []

    def sem(self):
        self.count += 1
        return self.sems.at[self.count - 1]

    def send(self, src, dst, recv, device, when=None):
        copy = pltpu.make_async_remote_copy(
            src_ref=src, dst_ref=dst, send_sem=self.sem(), recv_sem=recv,
            device_id=device, device_id_type=MESH,
        )
        if when is None:
            copy.start()
        else:
            pl.when(when)(copy.start)
        self.open.append((copy, when))

    def finish(self):
        for copy, when in self.open:
            if when is None:
                copy.wait_send()
            else:
                pl.when(when)(copy.wait_send)


def arrive(dst, sem):
    pltpu.make_async_copy(dst, dst, sem).wait()


def gather_kernel(
    tokens, wq, wk, wv, cot, docs, proj_out, tok_out, w_out, cot_out, docs_out,
    tok, w, wj, wx, other, sib, send_s, p_s, q_s, first_s, w_s, misc_s, sib_s, local_s, join_s,
):
    me = Place()
    z, c, y, x, t, same = me.z, me.c, me.y, me.x, me.t, me.same
    sends = Sends(send_s)
    width = 4 * HEAD
    part = {"p": (pl.ds(0, HALF_ROWS), p_s), "q": (pl.ds(HALF_ROWS, HALF_ROWS), q_s)}
    piece_rows = wj.shape[0]
    joins = [
        pltpu.make_async_copy(src, wj.at[:, pl.ds(low, src.shape[1])], join_s.at[k])
        for k, (src, low) in enumerate(((wq, 0), (wk, 2 * HEAD), (wv, 3 * HEAD)))
    ]
    for join in joins:
        join.start()

    def forward(name, slot, device):
        rows, sems = part[name]
        ref = tok.at[slot, rows, :]
        sends.send(ref, ref, sems.at[slot], device)

    def landed(name, slot):
        rows, sems = part[name]
        arrive(tok.at[slot, rows, :], sems.at[slot])

    own, pair = y * 4 + x, y * 4 + me.xp
    target_x = jnp.where(same, x, me.xp)
    first = first_s.at[jnp.where(same, 0, 1)]
    for k in range(2):
        local = same & (c == k)
        src = tokens.at[:, pl.ds(k * (tokens.shape[1] - KH), KH)]
        sends.send(src, tok.at[own], first, me.at(c=k, x=target_x), when=jnp.logical_not(local))

        @pl.when(local)
        def _():
            pltpu.make_async_copy(src, tok.at[own], first_s.at[0]).start()

    for join in joins:
        join.wait()

    sends.send(wj, wx, misc_s.at[0], me.at(x=me.xp))
    sends.send(docs, docs_out, misc_s.at[2], me.sibling)

    target_c = z // 2
    piece = (z % 2) * 2 + c

    def spread(src, g):
        rows = pl.ds(pl.multiple_of(target_c * PAD + piece * piece_rows, 16), piece_rows)
        dst = w.at[rows, pl.ds(pl.multiple_of(g * width, width), width)]
        sem = w_s.at[piece * 2 + g]
        here = target_c == c
        for k in (1, 3, 2):
            sends.send(src, dst, sem, me.at(z=(z + k) % 4, c=target_c))
        sends.send(src, dst, sem, me.sibling, when=jnp.logical_not(here))

        @pl.when(here)
        def _():
            pltpu.make_async_copy(src, dst, sem).start()

    w[pl.ds(pl.multiple_of((1 - c) * 4 * piece_rows, PAD), PAD), :] = jnp.zeros((PAD, 2 * width), jnp.bfloat16)
    below, above, far = me.down_y * 4, me.up_y * 4, me.far_y * 4
    here, beside = (x, me.xp), (me.xs, me.xsp)
    for slot, sem in ((own, 0), (pair, 1)):
        arrive(tok.at[slot], first_s.at[sem])
        forward("q", slot, me.up)
        forward("q", slot, me.down)
        forward("p", slot, me.beside)
        forward("p", slot, me.up)
        forward("p", slot, me.down)
        forward("q", slot, me.beside)
        if sem == 0:
            spread(wj, t)
            landed("q", below + x)
            forward("q", below + x, me.up)
            forward("q", below + x, me.beside)
    arrive(wx, misc_s.at[0])
    spread(wx, 1 - t)
    swap = jnp.logical_not(same)
    sends.send(cot, cot_out, misc_s.at[1], me.at(c=1 - c, x=me.xp), when=swap)
    landed("q", above + x)
    forward("q", above + x, me.beside)
    landed("q", above + me.xp)
    forward("q", above + me.xp, me.down)
    forward("q", above + me.xp, me.beside)
    landed("q", below + me.xp)
    forward("q", below + me.xp, me.beside)
    for column in beside:
        landed("p", y * 4 + column)
        forward("p", y * 4 + column, me.up)
        forward("p", y * 4 + column, me.down)
    for column in here:
        landed("p", below + column)
        forward("p", below + column, me.up)
        landed("q", far + column)
        forward("q", far + column, me.beside)
    for column in beside:
        landed("p", above + column)
        forward("p", above + column, me.down)

    for i in range(4):
        for g in range(2):
            arrive(w.at[pl.ds(i * piece_rows, piece_rows), pl.ds(g * width, width)], w_s.at[i * 2 + g])
    pltpu.make_async_copy(w, w_out, local_s.at[4]).start()

    plan = (
        (0, "p", ()),
        (0, "q", beside),
        (1, "q", beside),
        (2, "q", beside),
        (1, "p", beside),
        (2, "p", here),
        (3, "p", here + beside),
        (3, "q", beside),
    )
    lines = (y, me.down_y, me.up_y, me.far_y)
    done = [0, 0, 0, 0]
    units = []
    for n, (line, name, need) in enumerate(plan):
        row = lines[line]
        for column in need:
            landed(name, row * 4 + column)
        slots = pl.ds(pl.multiple_of(row * 4, 4), 4)
        done[line] += 1
        if done[line] == 2:
            pltpu.make_async_copy(tok.at[slots], tok_out.at[slots], local_s.at[line]).start()
        rows = part[name][0]
        block = tok[slots, rows, :].reshape(4 * HALF_ROWS, KH)
        shape = (4, HALF_ROWS, width)
        other[slots, rows, :] = mm(block, w[:, pl.ds(pl.multiple_of((1 - c) * width, width), width)]).reshape(shape)
        sends.send(other.at[slots, rows, :], sib.at[slots, rows, :], sib_s.at[n], me.sibling)
        proj_out[slots, rows, :] = mm(block, w[:, pl.ds(pl.multiple_of(c * width, width), width)]).reshape(shape)
        units.append((slots, rows))
    for n, (slots, rows) in enumerate(units):
        arrive(sib.at[slots, rows, :], sib_s.at[n])
        proj_out[slots, rows, :] += sib[slots, rows, :]
    for n, row in enumerate(lines):
        slots = pl.ds(pl.multiple_of(row * 4, 4), 4)
        pltpu.make_async_copy(tok.at[slots], tok_out.at[slots], local_s.at[n]).wait()
    pltpu.make_async_copy(w, w_out, local_s.at[4]).wait()
    arrive(docs_out, misc_s.at[2])
    pl.when(swap)(lambda: arrive(cot_out, misc_s.at[1]))
    sends.finish()


def gather(tokens, wq, wk, wv, cot, docs):
    f32, bf = jnp.float32, jnp.bfloat16
    anywhere = pl.BlockSpec(memory_space=pl.ANY)
    dma = pltpu.SemaphoreType.DMA
    return pl.pallas_call(
        gather_kernel,
        out_shape=(
            jax.ShapeDtypeStruct((16, 128, 4 * HEAD), f32),
            jax.ShapeDtypeStruct((16, 128, KH), bf),
            jax.ShapeDtypeStruct((KH, 8 * HEAD), bf),
            jax.ShapeDtypeStruct(cot.shape, bf),
            jax.ShapeDtypeStruct(docs.shape, docs.dtype),
        ),
        in_specs=[anywhere] * 6,
        out_specs=(pl.BlockSpec(memory_space=pltpu.VMEM),) + (anywhere,) * 4,
        scratch_shapes=[
            pltpu.VMEM((16, 128, KH), bf),
            pltpu.VMEM((KH, 8 * HEAD), bf),
            pltpu.VMEM((wq.shape[0], 4 * HEAD), bf),
            pltpu.VMEM((wq.shape[0], 4 * HEAD), bf),
            pltpu.VMEM((16, 128, 4 * HEAD), f32),
            pltpu.VMEM((16, 128, 4 * HEAD), f32),
            dma((64,)), dma((16,)), dma((16,)), dma((2,)), dma((8,)), dma((3,)), dma((8,)), dma((5,)), dma((3,)),
        ],
        compiler_params=pltpu.CompilerParams(
            has_side_effects=True, vmem_limit_bytes=60 * 1024 * 1024
        ),
        name="gather",
    )(tokens, wq, wk, wv, cot, docs)


def scatter_kernel(
    attn, dproj, tok_in, w_in, attn_out, grad_out, gq_out, gk_out, gv_out,
    tok, w, dpj, terms, dw, rqx, rp1, rp2, rpx, rq1, rq2, rw, rwx, wsum,
    send_s, attn_s, dp_s, local_s, qx_s, p1_s, p2_s, px_s, q1_s, q2_s, rw_s, g_s, rwx_s,
):
    me = Place()
    z, c, y, x, t, same = me.z, me.c, me.y, me.x, me.t, me.same
    sends = Sends(send_s)
    width = 4 * HEAD
    p_rows, q_rows = pl.ds(0, HALF_ROWS), pl.ds(HALF_ROWS, HALF_ROWS)
    order = (me.far_y, me.up_y, me.down_y, y)
    mine = pl.ds(pl.multiple_of(c * width, width), width)
    piece_rows = gq_out.shape[0]

    pltpu.make_async_copy(w_in, w, local_s.at[4]).start()
    for n, row in enumerate(order):
        rows = pl.ds(pl.multiple_of(row * 512, 512), 512)
        pltpu.make_async_copy(dproj.at[rows, :], dpj.at[rows, mine], local_s.at[n]).start()
        sends.send(dproj.at[rows, :], dpj.at[rows, mine], dp_s.at[n], me.sibling)
    pltpu.make_async_copy(tok_in, tok, local_s.at[5]).start()

    def add(dst, *sources):
        total = dst[...].astype(jnp.float32)
        for source in sources:
            total = total + source[...].astype(jnp.float32)
        dst[...] = total.astype(jnp.bfloat16)

    def compute(n):
        row = order[n]
        rows = pl.ds(pl.multiple_of(row * 512, 512), 512)
        arrive(dpj.at[rows, pl.ds(0, width)], local_s.at[n])
        arrive(dpj.at[rows, pl.ds(0, width)], dp_s.at[n])
        if n == 0:
            arrive(w, local_s.at[4])
        slots = pl.ds(pl.multiple_of(row * 4, 4), 4)
        term = mm(dpj[rows, :], w[...], NT).astype(jnp.bfloat16)
        terms[slots] = term.reshape(4, 128, KH)
        for k, column in enumerate((me.xs, me.xsp)):
            sends.send(terms.at[row * 4 + column, q_rows, :], rqx.at[n, k], qx_s.at[n, k], me.beside)

    def weight_terms(i):
        if i == 0:
            arrive(tok, local_s.at[5])
        low, high = ((0, 512), (512, 768), (768, 1152), (1152, KH))[i]
        left = tok[:, :, low:high].reshape(16 * 128, high - low)
        dw[low:high, :] = mm(left, dpj[...], (((0,), (0,)), ((), ()))).astype(jnp.bfloat16)
        for g in range(2):
            rows = pl.ds(pl.multiple_of(c * PAD + i * piece_rows, 16), piece_rows)
            src = dw.at[rows, pl.ds(g * width, width)]
            dst, sem = rw.at[z * 2 + g], rw_s.at[z * 2 + g]
            to_z, to_c = 2 * c + i // 2, i % 2
            stays = (to_z == z) & (c == to_c)
            sends.send(src, dst, sem, me.at(z=to_z, c=to_c), when=jnp.logical_not(stays))

            @pl.when(stays)
            def _():
                pltpu.make_async_copy(src, dst, sem).start()

    def exchanged(n):
        for k, column in enumerate((x, me.xp)):
            arrive(rqx.at[n, k], qx_s.at[n, k])
            add(terms.at[order[n] * 4 + column, q_rows, :], rqx.at[n, k])

    def finish(n, rows):
        src, dst, sem = terms.at[own + me.xp, rows, :], grad_out.at[c, rows, :], g_s.at[c, n]
        sends.send(src, dst, sem, me.at(c=t, x=me.xp))
        src = terms.at[own + x, rows, :]
        sends.send(src, dst, sem, me.sibling, when=jnp.logical_not(same))

        @pl.when(same)
        def _():
            pltpu.make_async_copy(src, dst, sem).start()

    far, up, down, own = me.far_y * 4, me.up_y * 4, me.down_y * 4, y * 4
    group = y * 4 + jnp.where(same, x, me.xp)
    columns = pl.ds(pl.multiple_of(group * 2 * HEAD, 2 * HEAD), 2 * HEAD)
    for dy in range(4):
        for dx in range(4):
            to_y, to_x = (y + dy) % 4, (x + dx) % 4
            rows = pl.ds(pl.multiple_of((to_y * 4 + to_x) * 128, 128), 128)
            src, dst = attn.at[rows, :], attn_out.at[:, columns]
            if dy == 0 and dx == 0:
                sends.send(src, dst, attn_s.at[group], me.sibling, when=jnp.logical_not(same))

                @pl.when(same)
                def _():
                    pltpu.make_async_copy(src, dst, attn_s.at[group]).start()
            else:
                sends.send(src, dst, attn_s.at[group], me.at(c=t, y=to_y, x=to_x))

    compute(0)
    sends.send(terms.at[pl.ds(far, 2), p_rows, :], rp1.at[0], p1_s.at[0], me.up)
    sends.send(terms.at[pl.ds(far + 2, 2), p_rows, :], rp1.at[1], p1_s.at[1], me.down)
    compute(1)
    compute(2)
    compute(3)
    weight_terms(0)
    weight_terms(1)
    arrive(rp1.at[0], p1_s.at[0])
    add(terms.at[pl.ds(up, 2), p_rows, :], rp1.at[0])
    sends.send(terms.at[pl.ds(up, 4), p_rows, :], rp2.at[0], p2_s.at[0], me.up)
    arrive(rp1.at[1], p1_s.at[1])
    add(terms.at[pl.ds(down + 2, 2), p_rows, :], rp1.at[1])
    sends.send(terms.at[pl.ds(down, 4), p_rows, :], rp2.at[1], p2_s.at[1], me.down)
    weight_terms(2)
    weight_terms(3)
    exchanged(0)
    sends.send(terms.at[far + x, q_rows, :], rq1.at[0], q1_s.at[0], me.up)
    sends.send(terms.at[far + me.xp, q_rows, :], rq1.at[1], q1_s.at[1], me.down)
    for n, base, extra, device in ((1, up, x, me.up), (2, down, me.xp, me.down)):
        exchanged(n)
        arrive(rq1.at[n - 1], q1_s.at[n - 1])
        add(terms.at[base + extra, q_rows, :], rq1.at[n - 1])
        for k, column in enumerate((x, me.xp)):
            sends.send(terms.at[base + column, q_rows, :], rq2.at[n - 1, k], q2_s.at[n - 1, k], device)
    arrive(rp2.at[0], p2_s.at[0])
    arrive(rp2.at[1], p2_s.at[1])
    add(terms.at[pl.ds(own, 4), p_rows, :], rp2.at[0], rp2.at[1])
    for k, column in enumerate((me.xs, me.xsp)):
        sends.send(terms.at[own + column, p_rows, :], rpx.at[k], px_s.at[k], me.beside)

    def summed(g):
        total = rw[g].astype(jnp.float32)
        for k in range(1, 4):
            total = total + rw[2 * k + g].astype(jnp.float32)
        return total

    for k in range(8):
        arrive(rw.at[k], rw_s.at[k])
    wsum[...] = summed(1 - t).astype(jnp.bfloat16)
    sends.send(wsum, rwx, rwx_s.at[0], me.at(x=me.xp))
    for k, column in enumerate((x, me.xp)):
        arrive(rqx.at[3, k], qx_s.at[3, k])
        arrive(rq2.at[0, k], q2_s.at[0, k])
        arrive(rq2.at[1, k], q2_s.at[1, k])
        add(terms.at[own + column, q_rows, :], rqx.at[3, k], rq2.at[0, k], rq2.at[1, k])
    finish(1, q_rows)
    for k, column in enumerate((x, me.xp)):
        arrive(rpx.at[k], px_s.at[k])
        add(terms.at[own + column, p_rows, :], rpx.at[k])
    finish(0, p_rows)
    total = summed(t)
    arrive(rwx, rwx_s.at[0])
    total = total + rwx[...].astype(jnp.float32)
    gq_out[...] = total[:, : 2 * HEAD]
    gk_out[...] = total[:, 2 * HEAD : 3 * HEAD]
    gv_out[...] = total[:, 3 * HEAD :]
    for k in range(16):
        arrive(attn_out.at[:, pl.ds(k * 2 * HEAD, 2 * HEAD)], attn_s.at[k])
    for k in range(2):
        for n, rows in ((0, p_rows), (1, q_rows)):
            arrive(grad_out.at[k, rows, :], g_s.at[k, n])
    sends.finish()


def scatter(attn, dproj, tok, w, piece_rows):
    f32, bf = jnp.float32, jnp.bfloat16
    anywhere = pl.BlockSpec(memory_space=pl.ANY)
    vmem = pl.BlockSpec(memory_space=pltpu.VMEM)
    dma = pltpu.SemaphoreType.DMA
    length = attn.shape[0]
    half = (HALF_ROWS, KH)
    return pl.pallas_call(
        scatter_kernel,
        out_shape=(
            jax.ShapeDtypeStruct((128, 32 * HEAD), bf),
            jax.ShapeDtypeStruct((2, 128, KH), bf),
            jax.ShapeDtypeStruct((piece_rows, 2 * HEAD), f32),
            jax.ShapeDtypeStruct((piece_rows, HEAD), f32),
            jax.ShapeDtypeStruct((piece_rows, HEAD), f32),
        ),
        in_specs=[anywhere] * 4,
        out_specs=(anywhere, anywhere, vmem, vmem, vmem),
        scratch_shapes=[
            pltpu.VMEM((16, 128, KH), bf),
            pltpu.VMEM((KH, 8 * HEAD), bf),
            pltpu.VMEM((length, 8 * HEAD), bf),
            pltpu.VMEM((16, 128, KH), bf),
            pltpu.VMEM((KH, 8 * HEAD), bf),
            pltpu.VMEM((4, 2) + half, bf),
            pltpu.VMEM((2, 2) + half, bf),
            pltpu.VMEM((2, 4) + half, bf),
            pltpu.VMEM((2,) + half, bf),
            pltpu.VMEM((2,) + half, bf),
            pltpu.VMEM((2, 2) + half, bf),
            pltpu.VMEM((8, piece_rows, 4 * HEAD), bf),
            pltpu.VMEM((piece_rows, 4 * HEAD), bf),
            pltpu.VMEM((piece_rows, 4 * HEAD), bf),
            dma((60,)), dma((16,)), dma((4,)), dma((6,)), dma((4, 2)), dma((2,)), dma((2,)),
            dma((2,)), dma((2,)), dma((2, 2)), dma((8,)), dma((2, 2)), dma((1,)),
        ],
        compiler_params=pltpu.CompilerParams(
            has_side_effects=True, vmem_limit_bytes=60 * 1024 * 1024
        ),
        name="scatter",
    )(attn, dproj, tok, w)


def local(
    tokens, q_weight, key_projection, value_projection, query_norm_gain, key_norm_gain, doc_lengths, out_cot
):
    half = tokens.shape[1] // 2
    proj, tok, w, cot2, docs2 = gather(
        tokens, q_weight, key_projection, value_projection, out_cot, doc_lengths
    )
    proj = proj.reshape(out_cot.shape[0], 4 * HEAD)
    attn, dproj = attention(
        doc_lengths, docs2, proj, out_cot, cot2, query_norm_gain, key_norm_gain
    )
    attn_out, grad, gq, gk, gv = scatter(attn, dproj, tok, w, q_weight.shape[0])
    token_grad = jnp.concatenate([grad[0, :, :half], grad[1, :, PAD:]], axis=1)
    return (attn_out, token_grad, gq, gk, gv)


def solution(mesh):
    placed = (
        P(("dp", "seq"), None),
        P("dp", "seq"),
        P("dp", "seq"),
        P("dp", "seq"),
        P(),
        P(),
        P("dp", None),
        P("dp", "seq"),
    )
    return jax.shard_map(
        local,
        mesh=mesh,
        in_specs=placed,
        out_specs=(
            P(("dp", "seq"), None),
            P(("dp", "seq"), None),
            P("dp", "seq"),
            P("dp", "seq"),
            P("dp", "seq"),
        ),
        check_vma=False,
    )
```

```python
import functools
import math

import jax
import jax.numpy as jnp
import numpy as np
from jax import lax
from jax.experimental import pallas as pl
from jax.experimental.pallas import tpu as pltpu
from jax.sharding import PartitionSpec as P

HEAD = 128
WINDOW = 1024
BLOCK = 256
score_scale = 168.0 ** (-0.5)
exp_scale = score_scale * math.log2(math.e)
rope_base = 10000.0
norm_eps = 1e-06
NN = (((1,), (0,)), ((), ()))
NT = (((1,), (1,)), ((), ()))


def mm(a, b, dims=NN):
    return lax.dot_general(a, b, dims, preferred_element_type=jnp.float32)


def rope_tables(blocks):
    inverse = rope_base ** (-np.arange(HEAD // 2) * (2.0 / HEAD))
    inverse = np.concatenate([inverse, inverse])[None, :]
    coarse = (np.arange(blocks) * BLOCK)[:, None] * inverse
    fine = np.arange(BLOCK)[:, None] * inverse
    return [
        jnp.asarray(table, jnp.float32)
        for table in (np.cos(coarse), np.sin(coarse), np.cos(fine), np.sin(fine))
    ]


def norm_factor(x):
    return lax.rsqrt(jnp.mean(x * x, axis=-1, keepdims=True) + norm_eps)


def rotate(n, cosine, sine):
    return n * cosine + pltpu.roll(n, HEAD // 2, 1) * sine


def rotate_back(g, cosine, sine):
    return g * cosine + pltpu.roll(g * sine, HEAD // 2, 1)


def norm_back(dn, x, gain):
    factor = norm_factor(x)
    dn = dn * gain
    inner = jnp.sum(x * dn, axis=-1, keepdims=True) * (1.0 / HEAD)
    return factor * dn - x * (factor * factor * factor * inner)


def attention_kernel(
    docs_ref, docs2_ref, proj_ref, cot_own, cot_got, cos_a, sin_a, cos_b, sin_b, gq_ref, gk_ref, out_ref, dproj_ref,
    cot_ref, cot_sem, q_s, k_s, kt_s, v_s, vt_s, e_s, eb_s, dk_s, dv_s, acc_s, dot_s, row_s,
):
    length = proj_ref.shape[0]
    blocks = length // BLOCK
    span = WINDOW // BLOCK
    same = lax.axis_index("dp") % 2 == (lax.axis_index("seq") % 4) // 2
    lane = lax.broadcasted_iota(jnp.int32, (1, HEAD), 1)
    sign = jnp.where(lane < HEAD // 2, -1.0, 1.0)

    def tables(i):
        ca, sa = cos_a[pl.ds(i, 1), :], sin_a[pl.ds(i, 1), :]
        return ca * cos_b[...] - sa * sin_b[...], (sa * sign) * cos_b[...] + (ca * sign) * sin_b[...]

    pl.when(same)(lambda: pltpu.make_async_copy(cot_own, cot_ref, cot_sem).start())
    pl.when(jnp.logical_not(same))(lambda: pltpu.make_async_copy(cot_got, cot_ref, cot_sem).start())
    e0, e1, e2 = [jnp.where(same, docs_ref[0, k], docs2_ref[0, k]) for k in range(3)]
    e1 = e0 + e1
    e2 = e1 + e2

    def start_of(t):
        zero = t * 0
        return jnp.maximum(
            jnp.maximum(jnp.where(t >= e0, e0, zero), jnp.where(t >= e1, e1, zero)),
            jnp.where(t >= e2, e2, zero),
        )

    @pl.loop(0, blocks)
    def _(i):
        rows = pl.ds(pl.multiple_of(i * BLOCK, BLOCK), BLOCK)
        cosine, sine = tables(i)
        for h in range(2):
            x = proj_ref[rows, h * HEAD : (h + 1) * HEAD]
            n = x * norm_factor(x) * gq_ref[...]
            q_s[i, h * BLOCK : (h + 1) * BLOCK, :] = rotate(n, cosine, sine).astype(jnp.bfloat16)
        x = proj_ref[rows, 2 * HEAD : 3 * HEAD]
        n = x * norm_factor(x) * gk_ref[...]
        key = rotate(n, cosine, sine)
        k_s[i] = key.astype(jnp.bfloat16)
        kt_s[i] = key.astype(jnp.bfloat16).T
        value = proj_ref[rows, 3 * HEAD : 4 * HEAD]
        v_s[i] = value.astype(jnp.bfloat16)
        vt_s[i] = value.astype(jnp.bfloat16).T
        dk_s[i] = jnp.zeros((BLOCK, HEAD), jnp.float32)
        dv_s[i] = jnp.zeros((BLOCK, HEAD), jnp.float32)

    pltpu.make_async_copy(cot_own, cot_ref, cot_sem).wait()

    @pl.loop(0, blocks)
    def _(i):
        q0 = i * BLOCK
        rows = pl.ds(pl.multiple_of(q0, BLOCK), BLOCK)
        token = q0 + lax.broadcasted_iota(jnp.int32, (1, BLOCK), 1)
        low = jnp.maximum(start_of(token), token - (WINDOW - 1))
        token2 = jnp.concatenate([token, token], axis=1)
        low2 = jnp.concatenate([low, low], axis=1)
        first = jnp.maximum(start_of(q0), q0 - (WINDOW - 1)) // BLOCK
        first = jnp.maximum(first, 0)

        acc_s[...] = jnp.zeros_like(acc_s)
        row_s[...] = jnp.zeros_like(row_s)
        query = q_s[i]

        last = q0 + BLOCK - 1
        whole = jnp.maximum(start_of(last), last - (WINDOW - 1))

        def forward(j, masked):
            slot = j - i + span
            e = jnp.exp2(mm(k_s[j], query, NT) * exp_scale)
            if masked:
                key_pos = j * BLOCK + lax.broadcasted_iota(jnp.int32, (BLOCK, 2 * BLOCK), 0)
                e = jnp.where((key_pos >= low2) & (key_pos <= token2), e, 0.0)
            e_s[slot] = e
            eb = e.astype(jnp.bfloat16)
            eb_s[slot] = eb
            row_s[...] += jnp.sum(e.reshape(BLOCK // 8, 8, 2 * BLOCK), axis=0)
            acc_s[...] += mm(vt_s[j], eb)

        @pl.loop(first, i + 1)
        def _(j):
            free = (j * BLOCK >= whole) & (j < i)
            pl.when(free)(lambda: forward(j, False))
            pl.when(jnp.logical_not(free))(lambda: forward(j, True))

        inv = 1.0 / jnp.sum(row_s[...], axis=0, keepdims=True)
        out_t = acc_s[...] * inv
        dot = jnp.concatenate(
            [cot_ref[rows, h * HEAD : (h + 1) * HEAD].T.astype(jnp.float32) for h in range(2)], axis=1
        )
        for h in range(2):
            out_ref[rows, h * HEAD : (h + 1) * HEAD] = (
                out_t[:, h * BLOCK : (h + 1) * BLOCK].astype(jnp.bfloat16).T
            )
        delta = jnp.sum(out_t * dot, axis=0, keepdims=True) * inv
        dot_s[...] = (dot * inv).astype(jnp.bfloat16)
        dout = dot_s[...].T
        acc_s[...] = jnp.zeros_like(acc_s)

        @pl.loop(first, i + 1)
        def _(j):
            slot = j - i + span
            dp = mm(v_s[j], dot_s[...])
            ds = (e_s[slot] * (dp - delta)).astype(jnp.bfloat16)
            dv_s[j] += mm(eb_s[slot], dout)
            dk_s[j] += mm(ds, query)
            acc_s[...] += mm(kt_s[j], ds)

        cosine, sine = tables(i)
        for h in range(2):
            g = acc_s[:, h * BLOCK : (h + 1) * BLOCK].T * score_scale
            x = proj_ref[rows, h * HEAD : (h + 1) * HEAD]
            dx = norm_back(rotate_back(g, cosine, sine), x, gq_ref[...])
            dproj_ref[rows, h * HEAD : (h + 1) * HEAD] = dx.astype(jnp.bfloat16)

    @pl.loop(0, blocks)
    def _(i):
        rows = pl.ds(pl.multiple_of(i * BLOCK, BLOCK), BLOCK)
        cosine, sine = tables(i)
        x = proj_ref[rows, 2 * HEAD : 3 * HEAD]
        dx = norm_back(rotate_back(dk_s[i] * score_scale, cosine, sine), x, gk_ref[...])
        dproj_ref[rows, 2 * HEAD : 3 * HEAD] = dx.astype(jnp.bfloat16)
        dproj_ref[rows, 3 * HEAD : 4 * HEAD] = dv_s[i].astype(jnp.bfloat16)


def attention(docs, docs2, proj, cot, cot2, gain_q, gain_k):
    length = proj.shape[0]
    blocks = length // BLOCK
    slots = WINDOW // BLOCK + 1
    vmem = pl.BlockSpec(memory_space=pltpu.VMEM)
    bf, f32 = jnp.bfloat16, jnp.float32
    return pl.pallas_call(
        attention_kernel,
        out_shape=(
            jax.ShapeDtypeStruct((length, 2 * HEAD), bf),
            jax.ShapeDtypeStruct((length, 4 * HEAD), bf),
        ),
        in_specs=[pl.BlockSpec(memory_space=pltpu.SMEM)] * 2
        + [vmem, pl.BlockSpec(memory_space=pl.ANY), pl.BlockSpec(memory_space=pl.ANY)]
        + [vmem] * 6,
        out_specs=(vmem, vmem),
        scratch_shapes=[
            pltpu.VMEM((length, 2 * HEAD), bf),
            pltpu.SemaphoreType.DMA(()),
            pltpu.VMEM((blocks, 2 * BLOCK, HEAD), bf),
            pltpu.VMEM((blocks, BLOCK, HEAD), bf),
            pltpu.VMEM((blocks, HEAD, BLOCK), bf),
            pltpu.VMEM((blocks, BLOCK, HEAD), bf),
            pltpu.VMEM((blocks, HEAD, BLOCK), bf),
            pltpu.VMEM((slots, BLOCK, 2 * BLOCK), f32),
            pltpu.VMEM((slots, BLOCK, 2 * BLOCK), bf),
            pltpu.VMEM((blocks, BLOCK, HEAD), f32),
            pltpu.VMEM((blocks, BLOCK, HEAD), f32),
            pltpu.VMEM((HEAD, 2 * BLOCK), f32),
            pltpu.VMEM((HEAD, 2 * BLOCK), bf),
            pltpu.VMEM((8, 2 * BLOCK), f32),
        ],
        compiler_params=pltpu.CompilerParams(vmem_limit_bytes=60 * 1024 * 1024),
        name="attention",
    )(docs, docs2, proj, cot, cot2, *rope_tables(blocks), gain_q.reshape(1, HEAD), gain_k.reshape(1, HEAD))


MESH = pl.DeviceIdType.MESH
KH = 1408
PAD = 64
HALF_ROWS = 64


class Place:
    def __init__(self):
        d, s = lax.axis_index("dp"), lax.axis_index("seq")
        self.z, self.c = d // 2, d % 2
        self.y, self.x = s // 4, s % 4
        self.t = self.x // 2
        self.xp = 3 - self.x
        self.xs = self.x + 1 - 2 * (self.x % 2)
        self.xsp = 3 - self.xs
        self.up_y, self.down_y, self.far_y = (self.y + 1) % 4, (self.y + 3) % 4, (self.y + 2) % 4
        self.same = self.c == self.t
        self.beside = self.at(x=self.xs)
        self.up, self.down = self.at(y=self.up_y), self.at(y=self.down_y)
        self.sibling = self.at(c=1 - self.c)

    def at(self, z=None, c=None, y=None, x=None):
        z = self.z if z is None else z
        c = self.c if c is None else c
        y = self.y if y is None else y
        x = self.x if x is None else x
        return (z * 2 + c, y * 4 + x)


def meet(devices):
    barrier = pltpu.get_barrier_semaphore()
    for device in devices:
        pl.semaphore_signal(barrier, inc=1, device_id=device, device_id_type=MESH)
    pl.semaphore_wait(barrier, len(devices))


class Sends:
    def __init__(self, sems):
        self.sems, self.count, self.open = sems, 0, []

    def sem(self):
        self.count += 1
        return self.sems.at[self.count - 1]

    def send(self, src, dst, recv, device, when=None):
        copy = pltpu.make_async_remote_copy(
            src_ref=src, dst_ref=dst, send_sem=self.sem(), recv_sem=recv,
            device_id=device, device_id_type=MESH,
        )
        if when is None:
            copy.start()
        else:
            pl.when(when)(copy.start)
        self.open.append((copy, when))

    def finish(self):
        for copy, when in self.open:
            if when is None:
                copy.wait_send()
            else:
                pl.when(when)(copy.wait_send)


def arrive(dst, sem):
    pltpu.make_async_copy(dst, dst, sem).wait()


def gather_kernel(
    tokens, wq, wk, wv, cot, docs, proj_out, tok_out, w_out, cot_out, docs_out,
    tok, w, wj, wx, other, sib, send_s, p_s, q_s, first_s, w_s, misc_s, sib_s, local_s, join_s,
):
    me = Place()
    z, c, y, x, t, same = me.z, me.c, me.y, me.x, me.t, me.same
    sends = Sends(send_s)
    width = 4 * HEAD
    part = {"p": (pl.ds(0, HALF_ROWS), p_s), "q": (pl.ds(HALF_ROWS, HALF_ROWS), q_s)}
    piece_rows = wj.shape[0]
    joins = [
        pltpu.make_async_copy(src, wj.at[:, pl.ds(low, src.shape[1])], join_s.at[k])
        for k, (src, low) in enumerate(((wq, 0), (wk, 2 * HEAD), (wv, 3 * HEAD)))
    ]
    for join in joins:
        join.start()
    meet(
        [me.sibling, me.beside, me.up, me.down, me.at(c=0, x=me.xp), me.at(c=1, x=me.xp)]
        + [me.at(z=(z + k) % 4, c=core) for k in (1, 2, 3) for core in range(2)]
    )

    def forward(name, slot, device):
        rows, sems = part[name]
        ref = tok.at[slot, rows, :]
        sends.send(ref, ref, sems.at[slot], device)

    def landed(name, slot):
        rows, sems = part[name]
        arrive(tok.at[slot, rows, :], sems.at[slot])

    own, pair = y * 4 + x, y * 4 + me.xp
    target_x = jnp.where(same, x, me.xp)
    first = first_s.at[jnp.where(same, 0, 1)]
    for k in range(2):
        local = same & (c == k)
        src = tokens.at[:, pl.ds(k * (tokens.shape[1] - KH), KH)]
        sends.send(src, tok.at[own], first, me.at(c=k, x=target_x), when=jnp.logical_not(local))

        @pl.when(local)
        def _():
            pltpu.make_async_copy(src, tok.at[own], first_s.at[0]).start()

    for join in joins:
        join.wait()

    sends.send(wj, wx, misc_s.at[0], me.at(x=me.xp))
    sends.send(docs, docs_out, misc_s.at[2], me.sibling)

    target_c = z // 2
    piece = (z % 2) * 2 + c

    def spread(src, g):
        rows = pl.ds(pl.multiple_of(target_c * PAD + piece * piece_rows, 16), piece_rows)
        dst = w.at[rows, pl.ds(pl.multiple_of(g * width, width), width)]
        sem = w_s.at[piece * 2 + g]
        here = target_c == c
        for k in (1, 3, 2):
            sends.send(src, dst, sem, me.at(z=(z + k) % 4, c=target_c))
        sends.send(src, dst, sem, me.sibling, when=jnp.logical_not(here))

        @pl.when(here)
        def _():
            pltpu.make_async_copy(src, dst, sem).start()

    w[pl.ds(pl.multiple_of((1 - c) * 4 * piece_rows, PAD), PAD), :] = jnp.zeros((PAD, 2 * width), jnp.bfloat16)
    below, above, far = me.down_y * 4, me.up_y * 4, me.far_y * 4
    here, beside = (x, me.xp), (me.xs, me.xsp)
    for slot, sem in ((own, 0), (pair, 1)):
        arrive(tok.at[slot], first_s.at[sem])
        forward("q", slot, me.up)
        forward("q", slot, me.down)
        forward("p", slot, me.beside)
        forward("p", slot, me.up)
        forward("p", slot, me.down)
        forward("q", slot, me.beside)
        if sem == 0:
            spread(wj, t)
            landed("q", below + x)
            forward("q", below + x, me.up)
            forward("q", below + x, me.beside)
    arrive(wx, misc_s.at[0])
    spread(wx, 1 - t)
    swap = jnp.logical_not(same)
    sends.send(cot, cot_out, misc_s.at[1], me.at(c=1 - c, x=me.xp), when=swap)
    landed("q", above + x)
    forward("q", above + x, me.beside)
    landed("q", above + me.xp)
    forward("q", above + me.xp, me.down)
    forward("q", above + me.xp, me.beside)
    landed("q", below + me.xp)
    forward("q", below + me.xp, me.beside)
    for column in beside:
        landed("p", y * 4 + column)
        forward("p", y * 4 + column, me.up)
        forward("p", y * 4 + column, me.down)
    for column in here:
        landed("p", below + column)
        forward("p", below + column, me.up)
        landed("q", far + column)
        forward("q", far + column, me.beside)
    for column in beside:
        landed("p", above + column)
        forward("p", above + column, me.down)

    for i in range(4):
        for g in range(2):
            arrive(w.at[pl.ds(i * piece_rows, piece_rows), pl.ds(g * width, width)], w_s.at[i * 2 + g])
    pltpu.make_async_copy(w, w_out, local_s.at[4]).start()

    plan = (
        (0, "p", ()),
        (0, "q", beside),
        (1, "q", beside),
        (2, "q", beside),
        (1, "p", beside),
        (2, "p", here),
        (3, "p", here + beside),
        (3, "q", beside),
    )
    lines = (y, me.down_y, me.up_y, me.far_y)
    done = [0, 0, 0, 0]
    units = []
    for n, (line, name, need) in enumerate(plan):
        row = lines[line]
        for column in need:
            landed(name, row * 4 + column)
        slots = pl.ds(pl.multiple_of(row * 4, 4), 4)
        done[line] += 1
        if done[line] == 2:
            pltpu.make_async_copy(tok.at[slots], tok_out.at[slots], local_s.at[line]).start()
        rows = part[name][0]
        block = tok[slots, rows, :].reshape(4 * HALF_ROWS, KH)
        shape = (4, HALF_ROWS, width)
        other[slots, rows, :] = mm(block, w[:, pl.ds(pl.multiple_of((1 - c) * width, width), width)]).reshape(shape)
        sends.send(other.at[slots, rows, :], sib.at[slots, rows, :], sib_s.at[n], me.sibling)
        proj_out[slots, rows, :] = mm(block, w[:, pl.ds(pl.multiple_of(c * width, width), width)]).reshape(shape)
        units.append((slots, rows))
    for n, (slots, rows) in enumerate(units):
        arrive(sib.at[slots, rows, :], sib_s.at[n])
        proj_out[slots, rows, :] += sib[slots, rows, :]
    for n, row in enumerate(lines):
        slots = pl.ds(pl.multiple_of(row * 4, 4), 4)
        pltpu.make_async_copy(tok.at[slots], tok_out.at[slots], local_s.at[n]).wait()
    pltpu.make_async_copy(w, w_out, local_s.at[4]).wait()
    arrive(docs_out, misc_s.at[2])
    pl.when(swap)(lambda: arrive(cot_out, misc_s.at[1]))
    sends.finish()


def gather(tokens, wq, wk, wv, cot, docs):
    f32, bf = jnp.float32, jnp.bfloat16
    anywhere = pl.BlockSpec(memory_space=pl.ANY)
    dma = pltpu.SemaphoreType.DMA
    return pl.pallas_call(
        gather_kernel,
        out_shape=(
            jax.ShapeDtypeStruct((16, 128, 4 * HEAD), f32),
            jax.ShapeDtypeStruct((16, 128, KH), bf),
            jax.ShapeDtypeStruct((KH, 8 * HEAD), bf),
            jax.ShapeDtypeStruct(cot.shape, bf),
            jax.ShapeDtypeStruct(docs.shape, docs.dtype),
        ),
        in_specs=[anywhere] * 6,
        out_specs=(pl.BlockSpec(memory_space=pltpu.VMEM),) + (anywhere,) * 4,
        scratch_shapes=[
            pltpu.VMEM((16, 128, KH), bf),
            pltpu.VMEM((KH, 8 * HEAD), bf),
            pltpu.VMEM((wq.shape[0], 4 * HEAD), bf),
            pltpu.VMEM((wq.shape[0], 4 * HEAD), bf),
            pltpu.VMEM((16, 128, 4 * HEAD), f32),
            pltpu.VMEM((16, 128, 4 * HEAD), f32),
            dma((64,)), dma((16,)), dma((16,)), dma((2,)), dma((8,)), dma((3,)), dma((8,)), dma((5,)), dma((3,)),
        ],
        compiler_params=pltpu.CompilerParams(
            collective_id=0, has_side_effects=True, vmem_limit_bytes=60 * 1024 * 1024
        ),
        name="gather",
    )(tokens, wq, wk, wv, cot, docs)


def scatter_kernel(
    attn, dproj, tok_in, w_in, attn_out, grad_out, gq_out, gk_out, gv_out,
    tok, w, dpj, terms, dw, rqx, rp1, rp2, rpx, rq1, rq2, rw, rwx, wsum,
    send_s, attn_s, dp_s, local_s, qx_s, p1_s, p2_s, px_s, q1_s, q2_s, rw_s, g_s, rwx_s,
):
    me = Place()
    z, c, y, x, t, same = me.z, me.c, me.y, me.x, me.t, me.same
    sends = Sends(send_s)
    width = 4 * HEAD
    p_rows, q_rows = pl.ds(0, HALF_ROWS), pl.ds(HALF_ROWS, HALF_ROWS)
    order = (me.far_y, me.up_y, me.down_y, y)
    mine = pl.ds(pl.multiple_of(c * width, width), width)
    piece_rows = gq_out.shape[0]

    pltpu.make_async_copy(w_in, w, local_s.at[4]).start()
    meet(
        [me.sibling]
        + [
            me.at(c=core, y=(y + dy) % 4, x=(x + dx) % 4)
            for dy in range(4) for dx in range(4) if dy or dx for core in range(2)
        ]
        + [me.at(z=(z + k) % 4, c=core) for k in (1, 2, 3) for core in range(2)]
    )
    for n, row in enumerate(order):
        rows = pl.ds(pl.multiple_of(row * 512, 512), 512)
        pltpu.make_async_copy(dproj.at[rows, :], dpj.at[rows, mine], local_s.at[n]).start()
        sends.send(dproj.at[rows, :], dpj.at[rows, mine], dp_s.at[n], me.sibling)
    pltpu.make_async_copy(tok_in, tok, local_s.at[5]).start()

    def add(dst, *sources):
        total = dst[...].astype(jnp.float32)
        for source in sources:
            total = total + source[...].astype(jnp.float32)
        dst[...] = total.astype(jnp.bfloat16)

    def compute(n):
        row = order[n]
        rows = pl.ds(pl.multiple_of(row * 512, 512), 512)
        arrive(dpj.at[rows, pl.ds(0, width)], local_s.at[n])
        arrive(dpj.at[rows, pl.ds(0, width)], dp_s.at[n])
        if n == 0:
            arrive(w, local_s.at[4])
        slots = pl.ds(pl.multiple_of(row * 4, 4), 4)
        term = mm(dpj[rows, :], w[...], NT).astype(jnp.bfloat16)
        terms[slots] = term.reshape(4, 128, KH)
        for k, column in enumerate((me.xs, me.xsp)):
            sends.send(terms.at[row * 4 + column, q_rows, :], rqx.at[n, k], qx_s.at[n, k], me.beside)

    def weight_terms(i):
        if i == 0:
            arrive(tok, local_s.at[5])
        low, high = ((0, 512), (512, 768), (768, 1152), (1152, KH))[i]
        left = tok[:, :, low:high].reshape(16 * 128, high - low)
        dw[low:high, :] = mm(left, dpj[...], (((0,), (0,)), ((), ()))).astype(jnp.bfloat16)
        for g in range(2):
            rows = pl.ds(pl.multiple_of(c * PAD + i * piece_rows, 16), piece_rows)
            src = dw.at[rows, pl.ds(g * width, width)]
            dst, sem = rw.at[z * 2 + g], rw_s.at[z * 2 + g]
            to_z, to_c = 2 * c + i // 2, i % 2
            stays = (to_z == z) & (c == to_c)
            sends.send(src, dst, sem, me.at(z=to_z, c=to_c), when=jnp.logical_not(stays))

            @pl.when(stays)
            def _():
                pltpu.make_async_copy(src, dst, sem).start()

    def exchanged(n):
        for k, column in enumerate((x, me.xp)):
            arrive(rqx.at[n, k], qx_s.at[n, k])
            add(terms.at[order[n] * 4 + column, q_rows, :], rqx.at[n, k])

    def finish(n, rows):
        src, dst, sem = terms.at[own + me.xp, rows, :], grad_out.at[c, rows, :], g_s.at[c, n]
        sends.send(src, dst, sem, me.at(c=t, x=me.xp))
        src = terms.at[own + x, rows, :]
        sends.send(src, dst, sem, me.sibling, when=jnp.logical_not(same))

        @pl.when(same)
        def _():
            pltpu.make_async_copy(src, dst, sem).start()

    far, up, down, own = me.far_y * 4, me.up_y * 4, me.down_y * 4, y * 4
    group = y * 4 + jnp.where(same, x, me.xp)
    columns = pl.ds(pl.multiple_of(group * 2 * HEAD, 2 * HEAD), 2 * HEAD)
    for dy in range(4):
        for dx in range(4):
            to_y, to_x = (y + dy) % 4, (x + dx) % 4
            rows = pl.ds(pl.multiple_of((to_y * 4 + to_x) * 128, 128), 128)
            src, dst = attn.at[rows, :], attn_out.at[:, columns]
            if dy == 0 and dx == 0:
                sends.send(src, dst, attn_s.at[group], me.sibling, when=jnp.logical_not(same))

                @pl.when(same)
                def _():
                    pltpu.make_async_copy(src, dst, attn_s.at[group]).start()
            else:
                sends.send(src, dst, attn_s.at[group], me.at(c=t, y=to_y, x=to_x))

    compute(0)
    sends.send(terms.at[pl.ds(far, 2), p_rows, :], rp1.at[0], p1_s.at[0], me.up)
    sends.send(terms.at[pl.ds(far + 2, 2), p_rows, :], rp1.at[1], p1_s.at[1], me.down)
    compute(1)
    compute(2)
    compute(3)
    weight_terms(0)
    weight_terms(1)
    arrive(rp1.at[0], p1_s.at[0])
    add(terms.at[pl.ds(up, 2), p_rows, :], rp1.at[0])
    sends.send(terms.at[pl.ds(up, 4), p_rows, :], rp2.at[0], p2_s.at[0], me.up)
    arrive(rp1.at[1], p1_s.at[1])
    add(terms.at[pl.ds(down + 2, 2), p_rows, :], rp1.at[1])
    sends.send(terms.at[pl.ds(down, 4), p_rows, :], rp2.at[1], p2_s.at[1], me.down)
    weight_terms(2)
    weight_terms(3)
    exchanged(0)
    sends.send(terms.at[far + x, q_rows, :], rq1.at[0], q1_s.at[0], me.up)
    sends.send(terms.at[far + me.xp, q_rows, :], rq1.at[1], q1_s.at[1], me.down)
    for n, base, extra, device in ((1, up, x, me.up), (2, down, me.xp, me.down)):
        exchanged(n)
        arrive(rq1.at[n - 1], q1_s.at[n - 1])
        add(terms.at[base + extra, q_rows, :], rq1.at[n - 1])
        for k, column in enumerate((x, me.xp)):
            sends.send(terms.at[base + column, q_rows, :], rq2.at[n - 1, k], q2_s.at[n - 1, k], device)
    arrive(rp2.at[0], p2_s.at[0])
    arrive(rp2.at[1], p2_s.at[1])
    add(terms.at[pl.ds(own, 4), p_rows, :], rp2.at[0], rp2.at[1])
    for k, column in enumerate((me.xs, me.xsp)):
        sends.send(terms.at[own + column, p_rows, :], rpx.at[k], px_s.at[k], me.beside)

    def summed(g):
        total = rw[g].astype(jnp.float32)
        for k in range(1, 4):
            total = total + rw[2 * k + g].astype(jnp.float32)
        return total

    for k in range(8):
        arrive(rw.at[k], rw_s.at[k])
    wsum[...] = summed(1 - t).astype(jnp.bfloat16)
    sends.send(wsum, rwx, rwx_s.at[0], me.at(x=me.xp))
    for k, column in enumerate((x, me.xp)):
        arrive(rqx.at[3, k], qx_s.at[3, k])
        arrive(rq2.at[0, k], q2_s.at[0, k])
        arrive(rq2.at[1, k], q2_s.at[1, k])
        add(terms.at[own + column, q_rows, :], rqx.at[3, k], rq2.at[0, k], rq2.at[1, k])
    finish(1, q_rows)
    for k, column in enumerate((x, me.xp)):
        arrive(rpx.at[k], px_s.at[k])
        add(terms.at[own + column, p_rows, :], rpx.at[k])
    finish(0, p_rows)
    total = summed(t)
    arrive(rwx, rwx_s.at[0])
    total = total + rwx[...].astype(jnp.float32)
    gq_out[...] = total[:, : 2 * HEAD]
    gk_out[...] = total[:, 2 * HEAD : 3 * HEAD]
    gv_out[...] = total[:, 3 * HEAD :]
    for k in range(16):
        arrive(attn_out.at[:, pl.ds(k * 2 * HEAD, 2 * HEAD)], attn_s.at[k])
    for k in range(2):
        for n, rows in ((0, p_rows), (1, q_rows)):
            arrive(grad_out.at[k, rows, :], g_s.at[k, n])
    sends.finish()


def scatter(attn, dproj, tok, w, piece_rows):
    f32, bf = jnp.float32, jnp.bfloat16
    anywhere = pl.BlockSpec(memory_space=pl.ANY)
    vmem = pl.BlockSpec(memory_space=pltpu.VMEM)
    dma = pltpu.SemaphoreType.DMA
    length = attn.shape[0]
    half = (HALF_ROWS, KH)
    return pl.pallas_call(
        scatter_kernel,
        out_shape=(
            jax.ShapeDtypeStruct((128, 32 * HEAD), bf),
            jax.ShapeDtypeStruct((2, 128, KH), bf),
            jax.ShapeDtypeStruct((piece_rows, 2 * HEAD), f32),
            jax.ShapeDtypeStruct((piece_rows, HEAD), f32),
            jax.ShapeDtypeStruct((piece_rows, HEAD), f32),
        ),
        in_specs=[anywhere] * 4,
        out_specs=(anywhere, anywhere, vmem, vmem, vmem),
        scratch_shapes=[
            pltpu.VMEM((16, 128, KH), bf),
            pltpu.VMEM((KH, 8 * HEAD), bf),
            pltpu.VMEM((length, 8 * HEAD), bf),
            pltpu.VMEM((16, 128, KH), bf),
            pltpu.VMEM((KH, 8 * HEAD), bf),
            pltpu.VMEM((4, 2) + half, bf),
            pltpu.VMEM((2, 2) + half, bf),
            pltpu.VMEM((2, 4) + half, bf),
            pltpu.VMEM((2,) + half, bf),
            pltpu.VMEM((2,) + half, bf),
            pltpu.VMEM((2, 2) + half, bf),
            pltpu.VMEM((8, piece_rows, 4 * HEAD), bf),
            pltpu.VMEM((piece_rows, 4 * HEAD), bf),
            pltpu.VMEM((piece_rows, 4 * HEAD), bf),
            dma((60,)), dma((16,)), dma((4,)), dma((6,)), dma((4, 2)), dma((2,)), dma((2,)),
            dma((2,)), dma((2,)), dma((2, 2)), dma((8,)), dma((2, 2)), dma((1,)),
        ],
        compiler_params=pltpu.CompilerParams(
            collective_id=1, has_side_effects=True, vmem_limit_bytes=60 * 1024 * 1024
        ),
        name="scatter",
    )(attn, dproj, tok, w)


def local(
    tokens, q_weight, key_projection, value_projection, query_norm_gain, key_norm_gain, doc_lengths, out_cot
):
    half = tokens.shape[1] // 2
    proj, tok, w, cot2, docs2 = gather(
        tokens, q_weight, key_projection, value_projection, out_cot, doc_lengths
    )
    proj = proj.reshape(out_cot.shape[0], 4 * HEAD)
    attn, dproj = attention(
        doc_lengths, docs2, proj, out_cot, cot2, query_norm_gain, key_norm_gain
    )
    attn_out, grad, gq, gk, gv = scatter(attn, dproj, tok, w, q_weight.shape[0])
    token_grad = jnp.concatenate([grad[0, :, :half], grad[1, :, PAD:]], axis=1)
    return (attn_out, token_grad, gq, gk, gv)


def solution(mesh):
    placed = (
        P(("dp", "seq"), None),
        P("dp", "seq"),
        P("dp", "seq"),
        P("dp", "seq"),
        P(),
        P(),
        P("dp", None),
        P("dp", "seq"),
    )
    return jax.shard_map(
        local,
        mesh=mesh,
        in_specs=placed,
        out_specs=(
            P(("dp", "seq"), None),
            P(("dp", "seq"), None),
            P("dp", "seq"),
            P("dp", "seq"),
            P("dp", "seq"),
        ),
        check_vma=False,
    )
```

```python
import functools
import math

import jax
import jax.numpy as jnp
import numpy as np
from jax import lax
from jax.experimental import pallas as pl
from jax.experimental.pallas import tpu as pltpu
from jax.sharding import PartitionSpec as P

HEAD = 128
WINDOW = 1024
BLOCK = 256
UNROLL = 2
score_scale = 168.0 ** (-0.5)
exp_scale = score_scale * math.log2(math.e)
rope_base = 10000.0
norm_eps = 1e-06
NN = (((1,), (0,)), ((), ()))
NT = (((1,), (1,)), ((), ()))


def mm(a, b, dims=NN):
    return lax.dot_general(a, b, dims, preferred_element_type=jnp.float32)


def rope_tables(blocks):
    inverse = rope_base ** (-np.arange(HEAD // 2) * (2.0 / HEAD))
    inverse = np.concatenate([inverse, inverse])[None, :]
    coarse = (np.arange(blocks) * BLOCK)[:, None] * inverse
    fine = np.arange(BLOCK)[:, None] * inverse
    return [
        jnp.asarray(table, jnp.float32)
        for table in (np.cos(coarse), np.sin(coarse), np.cos(fine), np.sin(fine))
    ]


def norm_factor(x):
    return lax.rsqrt(jnp.mean(x * x, axis=-1, keepdims=True) + norm_eps)


def rotate(n, cosine, sine):
    return n * cosine + pltpu.roll(n, HEAD // 2, 1) * sine


def rotate_back(g, cosine, sine):
    return g * cosine + pltpu.roll(g * sine, HEAD // 2, 1)


def norm_back(dn, x, gain):
    factor = norm_factor(x)
    dn = dn * gain
    inner = jnp.sum(x * dn, axis=-1, keepdims=True) * (1.0 / HEAD)
    return factor * dn - x * (factor * factor * factor * inner)


def attention_kernel(
    docs_ref, docs2_ref, proj_hbm, cot_own, cot_got, cos_a, sin_a, cos_b, sin_b, gq_ref, gk_ref, out_hbm, dproj_hbm,
    cot_ref, cot_sem, proj_ref, out_ref, dproj_ref, in_sem, out_sem, q_s, k_s, kt_s, v_s, vt_s, e_s, eb_s, dk_s, dv_s, acc_s, dot_s, row_s,
):
    length = proj_hbm.shape[0]
    blocks = length // BLOCK
    span = WINDOW // BLOCK
    def block_rows(i):
        return pl.ds(pl.multiple_of(i * BLOCK, BLOCK), BLOCK)

    def load(i):
        rows = block_rows(i)
        return pltpu.make_async_copy(proj_hbm.at[rows, :], proj_ref.at[rows, :], in_sem.at[i])

    def store(i, k):
        rows = block_rows(i)
        src, dst, cols = (
            (out_ref, out_hbm, pl.ds(0, 2 * HEAD)),
            (dproj_ref, dproj_hbm, pl.ds(0, 2 * HEAD)),
            (dproj_ref, dproj_hbm, pl.ds(2 * HEAD, 2 * HEAD)),
        )[k]
        return pltpu.make_async_copy(src.at[rows, cols], dst.at[rows, cols], out_sem.at[i, k])

    for i in range(blocks):
        load(i).start()
    same = lax.axis_index("dp") % 2 == (lax.axis_index("seq") % 4) // 2
    lane = lax.broadcasted_iota(jnp.int32, (1, HEAD), 1)
    sign = jnp.where(lane < HEAD // 2, -1.0, 1.0)

    def tables(i):
        ca, sa = cos_a[pl.ds(i, 1), :], sin_a[pl.ds(i, 1), :]
        return ca * cos_b[...] - sa * sin_b[...], (sa * sign) * cos_b[...] + (ca * sign) * sin_b[...]

    pl.when(same)(lambda: pltpu.make_async_copy(cot_own, cot_ref, cot_sem).start())
    pl.when(jnp.logical_not(same))(lambda: pltpu.make_async_copy(cot_got, cot_ref, cot_sem).start())
    e0, e1, e2 = [jnp.where(same, docs_ref[0, k], docs2_ref[0, k]) for k in range(3)]
    e1 = e0 + e1
    e2 = e1 + e2

    def start_of(t):
        zero = t * 0
        return jnp.maximum(
            jnp.maximum(jnp.where(t >= e0, e0, zero), jnp.where(t >= e1, e1, zero)),
            jnp.where(t >= e2, e2, zero),
        )

    @pl.loop(0, blocks)
    def _(i):
        load(i).wait()
        rows = pl.ds(pl.multiple_of(i * BLOCK, BLOCK), BLOCK)
        cosine, sine = tables(i)
        for h in range(2):
            x = proj_ref[rows, h * HEAD : (h + 1) * HEAD]
            n = x * norm_factor(x) * gq_ref[...]
            q_s[i, h * BLOCK : (h + 1) * BLOCK, :] = rotate(n, cosine, sine).astype(jnp.bfloat16)
        x = proj_ref[rows, 2 * HEAD : 3 * HEAD]
        n = x * norm_factor(x) * gk_ref[...]
        key = rotate(n, cosine, sine)
        k_s[i] = key.astype(jnp.bfloat16)
        kt_s[i] = key.astype(jnp.bfloat16).T
        value = proj_ref[rows, 3 * HEAD : 4 * HEAD]
        v_s[i] = value.astype(jnp.bfloat16)
        vt_s[i] = value.astype(jnp.bfloat16).T
        dk_s[i] = jnp.zeros((BLOCK, HEAD), jnp.float32)
        dv_s[i] = jnp.zeros((BLOCK, HEAD), jnp.float32)

    pltpu.make_async_copy(cot_own, cot_ref, cot_sem).wait()

    @pl.loop(0, blocks)
    def _(i):
        q0 = i * BLOCK
        rows = pl.ds(pl.multiple_of(q0, BLOCK), BLOCK)
        token = q0 + lax.broadcasted_iota(jnp.int32, (1, BLOCK), 1)
        low = jnp.maximum(start_of(token), token - (WINDOW - 1))
        token2 = jnp.concatenate([token, token], axis=1)
        low2 = jnp.concatenate([low, low], axis=1)
        first = jnp.maximum(start_of(q0), q0 - (WINDOW - 1)) // BLOCK
        first = jnp.maximum(first, 0)

        acc_s[...] = jnp.zeros_like(acc_s)
        row_s[...] = jnp.zeros_like(row_s)
        query = q_s[i]

        steps = (i - first + UNROLL) // UNROLL
        start = i + 1 - steps * UNROLL

        @pl.loop(0, steps)
        def _(step):
            low_j = start + step * UNROLL
            keys = [jnp.maximum(low_j + u, 0) for u in range(UNROLL)]
            total, mixed = row_s[...], acc_s[...]
            scores = [mm(k_s[j], query, NT) for j in keys]
            for u, j in enumerate(keys):
                slot = low_j + u - i + span + UNROLL - 1
                key_pos = (low_j + u) * BLOCK + lax.broadcasted_iota(jnp.int32, (BLOCK, 2 * BLOCK), 0)
                e = jnp.exp2(scores[u] * exp_scale)
                e = jnp.where((key_pos >= low2) & (key_pos <= token2), e, 0.0)
                e_s[slot] = e
                eb = e.astype(jnp.bfloat16)
                eb_s[slot] = eb
                total += jnp.sum(e.reshape(BLOCK // 8, 8, 2 * BLOCK), axis=0)
                mixed += mm(vt_s[j], eb)
            row_s[...], acc_s[...] = total, mixed

        inv = 1.0 / jnp.sum(row_s[...], axis=0, keepdims=True)
        out_t = acc_s[...] * inv
        dot = jnp.concatenate(
            [cot_ref[rows, h * HEAD : (h + 1) * HEAD].T.astype(jnp.float32) for h in range(2)], axis=1
        )
        for h in range(2):
            out_ref[rows, h * HEAD : (h + 1) * HEAD] = (
                out_t[:, h * BLOCK : (h + 1) * BLOCK].astype(jnp.bfloat16).T
            )
        store(i, 0).start()
        delta = jnp.sum(out_t * dot, axis=0, keepdims=True) * inv
        dot_s[...] = (dot * inv).astype(jnp.bfloat16)
        dout = dot_s[...].T
        acc_s[...] = jnp.zeros_like(acc_s)

        @pl.loop(0, steps)
        def _(step):
            low_j = start + step * UNROLL
            keys = [jnp.maximum(low_j + u, 0) for u in range(UNROLL)]
            slots = [low_j + u - i + span + UNROLL - 1 for u in range(UNROLL)]
            d_probs = [mm(v_s[j], dot_s[...]) for j in keys]
            d_scores = [(e_s[slot] * (dp - delta)).astype(jnp.bfloat16) for slot, dp in zip(slots, d_probs)]
            d_values = [mm(eb_s[slot], dout) for slot in slots]
            d_keys = [mm(ds, query) for ds in d_scores]
            mixed = acc_s[...]
            for j, ds in zip(keys, d_scores):
                mixed += mm(kt_s[j], ds)
            acc_s[...] = mixed
            for j, dv, dk in zip(keys, d_values, d_keys):
                dv_s[j] += dv
                dk_s[j] += dk

        cosine, sine = tables(i)
        for h in range(2):
            g = acc_s[:, h * BLOCK : (h + 1) * BLOCK].T * score_scale
            x = proj_ref[rows, h * HEAD : (h + 1) * HEAD]
            dx = norm_back(rotate_back(g, cosine, sine), x, gq_ref[...])
            dproj_ref[rows, h * HEAD : (h + 1) * HEAD] = dx.astype(jnp.bfloat16)
        store(i, 1).start()

    @pl.loop(0, blocks)
    def _(i):
        rows = pl.ds(pl.multiple_of(i * BLOCK, BLOCK), BLOCK)
        cosine, sine = tables(i)
        x = proj_ref[rows, 2 * HEAD : 3 * HEAD]
        dx = norm_back(rotate_back(dk_s[i] * score_scale, cosine, sine), x, gk_ref[...])
        dproj_ref[rows, 2 * HEAD : 3 * HEAD] = dx.astype(jnp.bfloat16)
        dproj_ref[rows, 3 * HEAD : 4 * HEAD] = dv_s[i].astype(jnp.bfloat16)
        store(i, 2).start()

    for i in range(blocks):
        for k in range(3):
            store(i, k).wait()


def attention(docs, docs2, proj, cot, cot2, gain_q, gain_k):
    length = proj.shape[0]
    blocks = length // BLOCK
    slots = WINDOW // BLOCK + UNROLL
    vmem = pl.BlockSpec(memory_space=pltpu.VMEM)
    bf, f32 = jnp.bfloat16, jnp.float32
    return pl.pallas_call(
        attention_kernel,
        out_shape=(
            jax.ShapeDtypeStruct((length, 2 * HEAD), bf),
            jax.ShapeDtypeStruct((length, 4 * HEAD), bf),
        ),
        in_specs=[pl.BlockSpec(memory_space=pltpu.SMEM)] * 2
        + [pl.BlockSpec(memory_space=pl.ANY)] * 3
        + [vmem] * 6,
        out_specs=(pl.BlockSpec(memory_space=pl.ANY), pl.BlockSpec(memory_space=pl.ANY)),
        scratch_shapes=[
            pltpu.VMEM((length, 2 * HEAD), bf),
            pltpu.SemaphoreType.DMA(()),
            pltpu.VMEM((length, 4 * HEAD), f32),
            pltpu.VMEM((length, 2 * HEAD), bf),
            pltpu.VMEM((length, 4 * HEAD), bf),
            pltpu.SemaphoreType.DMA((blocks,)),
            pltpu.SemaphoreType.DMA((blocks, 3)),
            pltpu.VMEM((blocks, 2 * BLOCK, HEAD), bf),
            pltpu.VMEM((blocks, BLOCK, HEAD), bf),
            pltpu.VMEM((blocks, HEAD, BLOCK), bf),
            pltpu.VMEM((blocks, BLOCK, HEAD), bf),
            pltpu.VMEM((blocks, HEAD, BLOCK), bf),
            pltpu.VMEM((slots, BLOCK, 2 * BLOCK), f32),
            pltpu.VMEM((slots, BLOCK, 2 * BLOCK), bf),
            pltpu.VMEM((blocks, BLOCK, HEAD), f32),
            pltpu.VMEM((blocks, BLOCK, HEAD), f32),
            pltpu.VMEM((HEAD, 2 * BLOCK), f32),
            pltpu.VMEM((HEAD, 2 * BLOCK), bf),
            pltpu.VMEM((8, 2 * BLOCK), f32),
        ],
        compiler_params=pltpu.CompilerParams(vmem_limit_bytes=60 * 1024 * 1024),
        name="attention",
    )(docs, docs2, proj, cot, cot2, *rope_tables(blocks), gain_q.reshape(1, HEAD), gain_k.reshape(1, HEAD))


MESH = pl.DeviceIdType.MESH
KH = 1408
PAD = 64
HALF_ROWS = 64


class Place:
    def __init__(self):
        d, s = lax.axis_index("dp"), lax.axis_index("seq")
        self.z, self.c = d // 2, d % 2
        self.y, self.x = s // 4, s % 4
        self.t = self.x // 2
        self.xp = 3 - self.x
        self.xs = self.x + 1 - 2 * (self.x % 2)
        self.xsp = 3 - self.xs
        self.up_y, self.down_y, self.far_y = (self.y + 1) % 4, (self.y + 3) % 4, (self.y + 2) % 4
        self.same = self.c == self.t
        self.beside = self.at(x=self.xs)
        self.up, self.down = self.at(y=self.up_y), self.at(y=self.down_y)
        self.sibling = self.at(c=1 - self.c)

    def at(self, z=None, c=None, y=None, x=None):
        z = self.z if z is None else z
        c = self.c if c is None else c
        y = self.y if y is None else y
        x = self.x if x is None else x
        return (z * 2 + c, y * 4 + x)


def meet(devices):
    barrier = pltpu.get_barrier_semaphore()
    for device in devices:
        pl.semaphore_signal(barrier, inc=1, device_id=device, device_id_type=MESH)
    pl.semaphore_wait(barrier, len(devices))


class Sends:
    def __init__(self, sems):
        self.sems, self.count, self.open = sems, 0, []

    def sem(self):
        self.count += 1
        return self.sems.at[self.count - 1]

    def send(self, src, dst, recv, device, when=None):
        copy = pltpu.make_async_remote_copy(
            src_ref=src, dst_ref=dst, send_sem=self.sem(), recv_sem=recv,
            device_id=device, device_id_type=MESH,
        )
        if when is None:
            copy.start()
        else:
            pl.when(when)(copy.start)
        self.open.append((copy, when))

    def finish(self):
        for copy, when in self.open:
            if when is None:
                copy.wait_send()
            else:
                pl.when(when)(copy.wait_send)


def arrive(dst, sem):
    pltpu.make_async_copy(dst, dst, sem).wait()


def gather_kernel(
    tokens, wq, wk, wv, cot, docs, proj_hbm, tok_out, w_out, cot_out, docs_out,
    tok, w, wj, wx, other, sib, send_s, p_s, q_s, first_s, w_s, misc_s, sib_s, local_s, join_s, proj_out, proj_s,
):
    me = Place()
    z, c, y, x, t, same = me.z, me.c, me.y, me.x, me.t, me.same
    sends = Sends(send_s)
    width = 4 * HEAD
    part = {"p": (pl.ds(0, HALF_ROWS), p_s), "q": (pl.ds(HALF_ROWS, HALF_ROWS), q_s)}
    piece_rows = wj.shape[0]
    joins = [
        pltpu.make_async_copy(src, wj.at[:, pl.ds(low, src.shape[1])], join_s.at[k])
        for k, (src, low) in enumerate(((wq, 0), (wk, 2 * HEAD), (wv, 3 * HEAD)))
    ]
    for join in joins:
        join.start()
    meet(
        [me.sibling, me.beside, me.up, me.down, me.at(c=0, x=me.xp), me.at(c=1, x=me.xp)]
        + [me.at(z=(z + k) % 4, c=core) for k in (1, 2, 3) for core in range(2)]
    )

    def forward(name, slot, device):
        rows, sems = part[name]
        ref = tok.at[slot, rows, :]
        sends.send(ref, ref, sems.at[slot], device)

    def landed(name, slot):
        rows, sems = part[name]
        arrive(tok.at[slot, rows, :], sems.at[slot])

    own, pair = y * 4 + x, y * 4 + me.xp
    target_x = jnp.where(same, x, me.xp)
    first = first_s.at[jnp.where(same, 0, 1)]
    for k in range(2):
        local = same & (c == k)
        src = tokens.at[:, pl.ds(k * (tokens.shape[1] - KH), KH)]
        sends.send(src, tok.at[own], first, me.at(c=k, x=target_x), when=jnp.logical_not(local))

        @pl.when(local)
        def _():
            pltpu.make_async_copy(src, tok.at[own], first_s.at[0]).start()

    for join in joins:
        join.wait()

    sends.send(wj, wx, misc_s.at[0], me.at(x=me.xp))
    sends.send(docs, docs_out, misc_s.at[2], me.sibling)

    target_c = z // 2
    piece = (z % 2) * 2 + c

    def spread(src, g):
        rows = pl.ds(pl.multiple_of(target_c * PAD + piece * piece_rows, 16), piece_rows)
        dst = w.at[rows, pl.ds(pl.multiple_of(g * width, width), width)]
        sem = w_s.at[piece * 2 + g]
        here = target_c == c
        for k in (1, 3, 2):
            sends.send(src, dst, sem, me.at(z=(z + k) % 4, c=target_c))
        sends.send(src, dst, sem, me.sibling, when=jnp.logical_not(here))

        @pl.when(here)
        def _():
            pltpu.make_async_copy(src, dst, sem).start()

    w[pl.ds(pl.multiple_of((1 - c) * 4 * piece_rows, PAD), PAD), :] = jnp.zeros((PAD, 2 * width), jnp.bfloat16)
    below, above, far = me.down_y * 4, me.up_y * 4, me.far_y * 4
    here, beside = (x, me.xp), (me.xs, me.xsp)
    for slot, sem in ((own, 0), (pair, 1)):
        arrive(tok.at[slot], first_s.at[sem])
        forward("q", slot, me.up)
        forward("q", slot, me.down)
        forward("p", slot, me.beside)
        forward("p", slot, me.up)
        forward("p", slot, me.down)
        forward("q", slot, me.beside)
        if sem == 0:
            spread(wj, t)
            landed("q", below + x)
            forward("q", below + x, me.up)
            forward("q", below + x, me.beside)
    arrive(wx, misc_s.at[0])
    spread(wx, 1 - t)
    swap = jnp.logical_not(same)
    sends.send(cot, cot_out, misc_s.at[1], me.at(c=1 - c, x=me.xp), when=swap)
    landed("q", above + x)
    forward("q", above + x, me.beside)
    landed("q", above + me.xp)
    forward("q", above + me.xp, me.down)
    forward("q", above + me.xp, me.beside)
    landed("q", below + me.xp)
    forward("q", below + me.xp, me.beside)
    for column in beside:
        landed("p", y * 4 + column)
        forward("p", y * 4 + column, me.up)
        forward("p", y * 4 + column, me.down)
    for column in here:
        landed("p", below + column)
        forward("p", below + column, me.up)
        landed("q", far + column)
        forward("q", far + column, me.beside)
    for column in beside:
        landed("p", above + column)
        forward("p", above + column, me.down)

    for i in range(4):
        for g in range(2):
            arrive(w.at[pl.ds(i * piece_rows, piece_rows), pl.ds(g * width, width)], w_s.at[i * 2 + g])
    pltpu.make_async_copy(w, w_out, local_s.at[4]).start()

    plan = (
        (0, "p", ()),
        (0, "q", beside),
        (1, "q", beside),
        (2, "q", beside),
        (1, "p", beside),
        (2, "p", here),
        (3, "p", here + beside),
        (3, "q", beside),
    )
    lines = (y, me.down_y, me.up_y, me.far_y)
    done = [0, 0, 0, 0]
    units = []

    def complete(n):
        slots, rows = units[n]
        arrive(sib.at[slots, rows, :], sib_s.at[n])
        proj_out[slots, rows, :] += sib[slots, rows, :]
        pltpu.make_async_copy(
            proj_out.at[slots, rows, :], proj_hbm.at[slots, rows, :], proj_s.at[n]
        ).start()

    for n, (line, name, need) in enumerate(plan):
        row = lines[line]
        for column in need:
            landed(name, row * 4 + column)
        slots = pl.ds(pl.multiple_of(row * 4, 4), 4)
        done[line] += 1
        if done[line] == 2:
            pltpu.make_async_copy(tok.at[slots], tok_out.at[slots], local_s.at[line]).start()
        rows = part[name][0]
        block = tok[slots, rows, :].reshape(4 * HALF_ROWS, KH)
        shape = (4, HALF_ROWS, width)
        other[slots, rows, :] = mm(block, w[:, pl.ds(pl.multiple_of((1 - c) * width, width), width)]).reshape(shape)
        sends.send(other.at[slots, rows, :], sib.at[slots, rows, :], sib_s.at[n], me.sibling)
        proj_out[slots, rows, :] = mm(block, w[:, pl.ds(pl.multiple_of(c * width, width), width)]).reshape(shape)
        units.append((slots, rows))
        if n:
            complete(n - 1)
    complete(len(plan) - 1)
    for n, (slots, rows) in enumerate(units):
        pltpu.make_async_copy(
            proj_out.at[slots, rows, :], proj_hbm.at[slots, rows, :], proj_s.at[n]
        ).wait()
    for n, row in enumerate(lines):
        slots = pl.ds(pl.multiple_of(row * 4, 4), 4)
        pltpu.make_async_copy(tok.at[slots], tok_out.at[slots], local_s.at[n]).wait()
    pltpu.make_async_copy(w, w_out, local_s.at[4]).wait()
    arrive(docs_out, misc_s.at[2])
    pl.when(swap)(lambda: arrive(cot_out, misc_s.at[1]))
    sends.finish()


def gather(tokens, wq, wk, wv, cot, docs):
    f32, bf = jnp.float32, jnp.bfloat16
    anywhere = pl.BlockSpec(memory_space=pl.ANY)
    dma = pltpu.SemaphoreType.DMA
    return pl.pallas_call(
        gather_kernel,
        out_shape=(
            jax.ShapeDtypeStruct((16, 128, 4 * HEAD), f32),
            jax.ShapeDtypeStruct((16, 128, KH), bf),
            jax.ShapeDtypeStruct((KH, 8 * HEAD), bf),
            jax.ShapeDtypeStruct(cot.shape, bf),
            jax.ShapeDtypeStruct(docs.shape, docs.dtype),
        ),
        in_specs=[anywhere] * 6,
        out_specs=(anywhere,) * 5,
        scratch_shapes=[
            pltpu.VMEM((16, 128, KH), bf),
            pltpu.VMEM((KH, 8 * HEAD), bf),
            pltpu.VMEM((wq.shape[0], 4 * HEAD), bf),
            pltpu.VMEM((wq.shape[0], 4 * HEAD), bf),
            pltpu.VMEM((16, 128, 4 * HEAD), f32),
            pltpu.VMEM((16, 128, 4 * HEAD), f32),
            dma((64,)), dma((16,)), dma((16,)), dma((2,)), dma((8,)), dma((3,)), dma((8,)), dma((5,)), dma((3,)),
            pltpu.VMEM((16, 128, 4 * HEAD), f32), dma((8,)),
        ],
        compiler_params=pltpu.CompilerParams(
            collective_id=0, has_side_effects=True, vmem_limit_bytes=60 * 1024 * 1024
        ),
        name="gather",
    )(tokens, wq, wk, wv, cot, docs)


def scatter_kernel(
    attn, dproj, tok_in, w_in, attn_out, token_out, gq_out, gk_out, gv_out,
    tok, w, dpj, terms, dw, rqx, rp1, rp2, rpx, rq1, rq2, rw, rwx, wsum, grad_out,
    send_s, attn_s, dp_s, local_s, qx_s, p1_s, p2_s, px_s, q1_s, q2_s, rw_s, g_s, rwx_s,
):
    me = Place()
    z, c, y, x, t, same = me.z, me.c, me.y, me.x, me.t, me.same
    sends = Sends(send_s)
    width = 4 * HEAD
    p_rows, q_rows = pl.ds(0, HALF_ROWS), pl.ds(HALF_ROWS, HALF_ROWS)
    order = (me.far_y, me.up_y, me.down_y, y)
    mine = pl.ds(pl.multiple_of(c * width, width), width)
    piece_rows = gq_out.shape[0]

    pltpu.make_async_copy(w_in, w, local_s.at[4]).start()
    meet(
        [me.sibling]
        + [
            me.at(c=core, y=(y + dy) % 4, x=(x + dx) % 4)
            for dy in range(4) for dx in range(4) if dy or dx for core in range(2)
        ]
        + [me.at(z=(z + k) % 4, c=core) for k in (1, 2, 3) for core in range(2)]
    )
    for n, row in enumerate(order):
        rows = pl.ds(pl.multiple_of(row * 512, 512), 512)
        pltpu.make_async_copy(dproj.at[rows, :], dpj.at[rows, mine], local_s.at[n]).start()
        sends.send(dproj.at[rows, :], dpj.at[rows, mine], dp_s.at[n], me.sibling)
    pltpu.make_async_copy(tok_in, tok, local_s.at[5]).start()

    def add(dst, *sources):
        total = dst[...].astype(jnp.float32)
        for source in sources:
            total = total + source[...].astype(jnp.float32)
        dst[...] = total.astype(jnp.bfloat16)

    def compute(n):
        row = order[n]
        rows = pl.ds(pl.multiple_of(row * 512, 512), 512)
        arrive(dpj.at[rows, pl.ds(0, width)], local_s.at[n])
        arrive(dpj.at[rows, pl.ds(0, width)], dp_s.at[n])
        if n == 0:
            arrive(w, local_s.at[4])
        slots = pl.ds(pl.multiple_of(row * 4, 4), 4)
        term = mm(dpj[rows, :], w[...], NT).astype(jnp.bfloat16)
        terms[slots] = term.reshape(4, 128, KH)
        for k, column in enumerate((me.xs, me.xsp)):
            sends.send(terms.at[row * 4 + column, q_rows, :], rqx.at[n, k], qx_s.at[n, k], me.beside)

    def weight_terms(i):
        if i == 0:
            arrive(tok, local_s.at[5])
        low, high = ((0, 512), (512, 768), (768, 1152), (1152, KH))[i]
        left = tok[:, :, low:high].reshape(16 * 128, high - low)
        dw[low:high, :] = mm(left, dpj[...], (((0,), (0,)), ((), ()))).astype(jnp.bfloat16)
        for g in range(2):
            rows = pl.ds(pl.multiple_of(c * PAD + i * piece_rows, 16), piece_rows)
            src = dw.at[rows, pl.ds(g * width, width)]
            dst, sem = rw.at[z * 2 + g], rw_s.at[z * 2 + g]
            to_z, to_c = 2 * c + i // 2, i % 2
            stays = (to_z == z) & (c == to_c)
            sends.send(src, dst, sem, me.at(z=to_z, c=to_c), when=jnp.logical_not(stays))

            @pl.when(stays)
            def _():
                pltpu.make_async_copy(src, dst, sem).start()

    def exchanged(n):
        for k, column in enumerate((x, me.xp)):
            arrive(rqx.at[n, k], qx_s.at[n, k])
            add(terms.at[order[n] * 4 + column, q_rows, :], rqx.at[n, k])

    def finish(n, rows):
        src, dst, sem = terms.at[own + me.xp, rows, :], grad_out.at[c, rows, :], g_s.at[c, n]
        sends.send(src, dst, sem, me.at(c=t, x=me.xp))
        src = terms.at[own + x, rows, :]
        sends.send(src, dst, sem, me.sibling, when=jnp.logical_not(same))

        @pl.when(same)
        def _():
            pltpu.make_async_copy(src, dst, sem).start()

    far, up, down, own = me.far_y * 4, me.up_y * 4, me.down_y * 4, y * 4
    group = y * 4 + jnp.where(same, x, me.xp)
    columns = pl.ds(pl.multiple_of(group * 2 * HEAD, 2 * HEAD), 2 * HEAD)
    compute(0)
    sends.send(terms.at[pl.ds(far, 2), p_rows, :], rp1.at[0], p1_s.at[0], me.up)
    sends.send(terms.at[pl.ds(far + 2, 2), p_rows, :], rp1.at[1], p1_s.at[1], me.down)
    compute(1)
    compute(2)
    compute(3)
    weight_terms(0)
    weight_terms(1)
    arrive(rp1.at[0], p1_s.at[0])
    add(terms.at[pl.ds(up, 2), p_rows, :], rp1.at[0])
    sends.send(terms.at[pl.ds(up, 4), p_rows, :], rp2.at[0], p2_s.at[0], me.up)
    arrive(rp1.at[1], p1_s.at[1])
    add(terms.at[pl.ds(down + 2, 2), p_rows, :], rp1.at[1])
    sends.send(terms.at[pl.ds(down, 4), p_rows, :], rp2.at[1], p2_s.at[1], me.down)
    weight_terms(2)
    weight_terms(3)
    exchanged(0)
    sends.send(terms.at[far + x, q_rows, :], rq1.at[0], q1_s.at[0], me.up)
    sends.send(terms.at[far + me.xp, q_rows, :], rq1.at[1], q1_s.at[1], me.down)
    for n, base, extra, device in ((1, up, x, me.up), (2, down, me.xp, me.down)):
        exchanged(n)
        arrive(rq1.at[n - 1], q1_s.at[n - 1])
        add(terms.at[base + extra, q_rows, :], rq1.at[n - 1])
        for k, column in enumerate((x, me.xp)):
            sends.send(terms.at[base + column, q_rows, :], rq2.at[n - 1, k], q2_s.at[n - 1, k], device)
    arrive(rp2.at[0], p2_s.at[0])
    arrive(rp2.at[1], p2_s.at[1])
    add(terms.at[pl.ds(own, 4), p_rows, :], rp2.at[0], rp2.at[1])
    for k, column in enumerate((me.xs, me.xsp)):
        sends.send(terms.at[own + column, p_rows, :], rpx.at[k], px_s.at[k], me.beside)

    def summed(g):
        total = rw[g].astype(jnp.float32)
        for k in range(1, 4):
            total = total + rw[2 * k + g].astype(jnp.float32)
        return total

    for dy in range(4):
        for dx in range(4):
            to_y, to_x = (y + dy) % 4, (x + dx) % 4
            rows = pl.ds(pl.multiple_of((to_y * 4 + to_x) * 128, 128), 128)
            src, dst = attn.at[rows, :], attn_out.at[:, columns]
            if dy == 0 and dx == 0:
                sends.send(src, dst, attn_s.at[group], me.sibling, when=jnp.logical_not(same))

                @pl.when(same)
                def _():
                    pltpu.make_async_copy(src, dst, attn_s.at[group]).start()
            else:
                sends.send(src, dst, attn_s.at[group], me.at(c=t, y=to_y, x=to_x))

    for k in range(8):
        arrive(rw.at[k], rw_s.at[k])
    wsum[...] = summed(1 - t).astype(jnp.bfloat16)
    sends.send(wsum, rwx, rwx_s.at[0], me.at(x=me.xp))
    for k, column in enumerate((x, me.xp)):
        arrive(rqx.at[3, k], qx_s.at[3, k])
        arrive(rq2.at[0, k], q2_s.at[0, k])
        arrive(rq2.at[1, k], q2_s.at[1, k])
        add(terms.at[own + column, q_rows, :], rqx.at[3, k], rq2.at[0, k], rq2.at[1, k])
    finish(1, q_rows)
    for k, column in enumerate((x, me.xp)):
        arrive(rpx.at[k], px_s.at[k])
        add(terms.at[own + column, p_rows, :], rpx.at[k])
    finish(0, p_rows)
    total = summed(t)
    arrive(rwx, rwx_s.at[0])
    total = total + rwx[...].astype(jnp.float32)
    gq_out[...] = total[:, : 2 * HEAD]
    gk_out[...] = total[:, 2 * HEAD : 3 * HEAD]
    gv_out[...] = total[:, 3 * HEAD :]
    for k in range(16):
        arrive(attn_out.at[:, pl.ds(k * 2 * HEAD, 2 * HEAD)], attn_s.at[k])
    for k in range(2):
        for n, rows in ((0, p_rows), (1, q_rows)):
            arrive(grad_out.at[k, rows, :], g_s.at[k, n])
    low = token_out.shape[1] - KH
    lane = lax.broadcasted_iota(jnp.int32, (128, KH - low), 1)
    token_out[:, :low] = grad_out[0, :, :low]
    token_out[:, low:KH] = jnp.where(lane < PAD, grad_out[0, :, low:], grad_out[1, :, : KH - low])
    token_out[:, KH:] = grad_out[1, :, KH - low :]
    sends.finish()


def scatter(attn, dproj, tok, w, piece_rows):
    f32, bf = jnp.float32, jnp.bfloat16
    anywhere = pl.BlockSpec(memory_space=pl.ANY)
    vmem = pl.BlockSpec(memory_space=pltpu.VMEM)
    dma = pltpu.SemaphoreType.DMA
    length = attn.shape[0]
    half = (HALF_ROWS, KH)
    return pl.pallas_call(
        scatter_kernel,
        out_shape=(
            jax.ShapeDtypeStruct((128, 32 * HEAD), bf),
            jax.ShapeDtypeStruct((128, 2 * (KH - PAD)), bf),
            jax.ShapeDtypeStruct((piece_rows, 2 * HEAD), f32),
            jax.ShapeDtypeStruct((piece_rows, HEAD), f32),
            jax.ShapeDtypeStruct((piece_rows, HEAD), f32),
        ),
        in_specs=[anywhere] * 4,
        out_specs=(anywhere, vmem, vmem, vmem, vmem),
        scratch_shapes=[
            pltpu.VMEM((16, 128, KH), bf),
            pltpu.VMEM((KH, 8 * HEAD), bf),
            pltpu.VMEM((length, 8 * HEAD), bf),
            pltpu.VMEM((16, 128, KH), bf),
            pltpu.VMEM((KH, 8 * HEAD), bf),
            pltpu.VMEM((4, 2) + half, bf),
            pltpu.VMEM((2, 2) + half, bf),
            pltpu.VMEM((2, 4) + half, bf),
            pltpu.VMEM((2,) + half, bf),
            pltpu.VMEM((2,) + half, bf),
            pltpu.VMEM((2, 2) + half, bf),
            pltpu.VMEM((8, piece_rows, 4 * HEAD), bf),
            pltpu.VMEM((piece_rows, 4 * HEAD), bf),
            pltpu.VMEM((piece_rows, 4 * HEAD), bf),
            pltpu.VMEM((2, 128, KH), bf),
            dma((60,)), dma((16,)), dma((4,)), dma((6,)), dma((4, 2)), dma((2,)), dma((2,)),
            dma((2,)), dma((2,)), dma((2, 2)), dma((8,)), dma((2, 2)), dma((1,)),
        ],
        compiler_params=pltpu.CompilerParams(
            collective_id=1, has_side_effects=True, vmem_limit_bytes=60 * 1024 * 1024
        ),
        name="scatter",
    )(attn, dproj, tok, w)


def local(
    tokens, q_weight, key_projection, value_projection, query_norm_gain, key_norm_gain, doc_lengths, out_cot
):
    proj, tok, w, cot2, docs2 = gather(
        tokens, q_weight, key_projection, value_projection, out_cot, doc_lengths
    )
    proj = proj.reshape(out_cot.shape[0], 4 * HEAD)
    attn, dproj = attention(
        doc_lengths, docs2, proj, out_cot, cot2, query_norm_gain, key_norm_gain
    )
    attn_out, token_grad, gq, gk, gv = scatter(attn, dproj, tok, w, q_weight.shape[0])
    return (attn_out, token_grad, gq, gk, gv)


def solution(mesh):
    placed = (
        P(("dp", "seq"), None),
        P("dp", "seq"),
        P("dp", "seq"),
        P("dp", "seq"),
        P(),
        P(),
        P("dp", None),
        P("dp", "seq"),
    )
    return jax.shard_map(
        local,
        mesh=mesh,
        in_specs=placed,
        out_specs=(
            P(("dp", "seq"), None),
            P(("dp", "seq"), None),
            P("dp", "seq"),
            P("dp", "seq"),
            P("dp", "seq"),
        ),
        check_vma=False,
    )
```

```python
import functools
import math

import jax
import jax.numpy as jnp
import numpy as np
from jax import lax
from jax.experimental import pallas as pl
from jax.experimental.pallas import tpu as pltpu
from jax.sharding import PartitionSpec as P

HEAD = 128
WINDOW = 1024
BLOCK = 256
UNROLL = 2
score_scale = 168.0 ** (-0.5)
exp_scale = score_scale * math.log2(math.e)
rope_base = 10000.0
norm_eps = 1e-06
NN = (((1,), (0,)), ((), ()))
NT = (((1,), (1,)), ((), ()))


def mm(a, b, dims=NN):
    return lax.dot_general(a, b, dims, preferred_element_type=jnp.float32)


def rope_tables(blocks):
    inverse = rope_base ** (-np.arange(HEAD // 2) * (2.0 / HEAD))
    inverse = np.concatenate([inverse, inverse])[None, :]
    coarse = (np.arange(blocks) * BLOCK)[:, None] * inverse
    fine = np.arange(BLOCK)[:, None] * inverse
    return [
        jnp.asarray(table, jnp.float32)
        for table in (np.cos(coarse), np.sin(coarse), np.cos(fine), np.sin(fine))
    ]


def norm_factor(x):
    return lax.rsqrt(jnp.mean(x * x, axis=-1, keepdims=True) + norm_eps)


def rotate(n, cosine, sine):
    return n * cosine + pltpu.roll(n, HEAD // 2, 1) * sine


def rotate_back(g, cosine, sine):
    return g * cosine + pltpu.roll(g * sine, HEAD // 2, 1)


def norm_back(dn, x, gain):
    factor = norm_factor(x)
    dn = dn * gain
    inner = jnp.sum(x * dn, axis=-1, keepdims=True) * (1.0 / HEAD)
    return factor * dn - x * (factor * factor * factor * inner)


def attention_kernel(
    docs_ref, docs2_ref, proj_hbm, cot_own, cot_got, cos_a, sin_a, cos_b, sin_b, gq_ref, gk_ref, out_hbm, dproj_hbm,
    cot_ref, cot_sem, proj_ref, out_ref, dproj_ref, in_sem, out_sem, q_s, k_s, kt_s, v_s, vt_s, e_s, eb_s, dk_s, dv_s, acc_s, dot_s, row_s,
):
    length = proj_hbm.shape[0]
    blocks = length // BLOCK
    span = WINDOW // BLOCK
    def block_rows(i):
        return pl.ds(pl.multiple_of(i * BLOCK, BLOCK), BLOCK)

    def load(i):
        rows = block_rows(i)
        return pltpu.make_async_copy(proj_hbm.at[rows, :], proj_ref.at[rows, :], in_sem.at[i])

    def store(i, k):
        rows = block_rows(i)
        src, dst, cols = (
            (out_ref, out_hbm, pl.ds(0, 2 * HEAD)),
            (dproj_ref, dproj_hbm, pl.ds(0, 2 * HEAD)),
            (dproj_ref, dproj_hbm, pl.ds(2 * HEAD, 2 * HEAD)),
        )[k]
        return pltpu.make_async_copy(src.at[rows, cols], dst.at[rows, cols], out_sem.at[i, k])

    for i in range(blocks):
        load(i).start()
    same = lax.axis_index("dp") % 2 == (lax.axis_index("seq") % 4) // 2
    lane = lax.broadcasted_iota(jnp.int32, (1, HEAD), 1)
    sign = jnp.where(lane < HEAD // 2, -1.0, 1.0)

    def tables(i):
        ca, sa = cos_a[pl.ds(i, 1), :], sin_a[pl.ds(i, 1), :]
        return ca * cos_b[...] - sa * sin_b[...], (sa * sign) * cos_b[...] + (ca * sign) * sin_b[...]

    pl.when(same)(lambda: pltpu.make_async_copy(cot_own, cot_ref, cot_sem).start())
    pl.when(jnp.logical_not(same))(lambda: pltpu.make_async_copy(cot_got, cot_ref, cot_sem).start())
    e0, e1, e2 = [jnp.where(same, docs_ref[0, k], docs2_ref[0, k]) for k in range(3)]
    e1 = e0 + e1
    e2 = e1 + e2

    def start_of(t):
        zero = t * 0
        return jnp.maximum(
            jnp.maximum(jnp.where(t >= e0, e0, zero), jnp.where(t >= e1, e1, zero)),
            jnp.where(t >= e2, e2, zero),
        )

    @pl.loop(0, blocks)
    def _(i):
        load(i).wait()
        rows = pl.ds(pl.multiple_of(i * BLOCK, BLOCK), BLOCK)
        cosine, sine = tables(i)
        for h in range(2):
            x = proj_ref[rows, h * HEAD : (h + 1) * HEAD]
            n = x * norm_factor(x) * gq_ref[...]
            q_s[i, h * BLOCK : (h + 1) * BLOCK, :] = rotate(n, cosine, sine).astype(jnp.bfloat16)
        x = proj_ref[rows, 2 * HEAD : 3 * HEAD]
        n = x * norm_factor(x) * gk_ref[...]
        key = rotate(n, cosine, sine)
        k_s[i] = key.astype(jnp.bfloat16)
        kt_s[i] = key.astype(jnp.bfloat16).T
        value = proj_ref[rows, 3 * HEAD : 4 * HEAD]
        v_s[i] = value.astype(jnp.bfloat16)
        vt_s[i] = value.astype(jnp.bfloat16).T
        dk_s[i] = jnp.zeros((BLOCK, HEAD), jnp.float32)
        dv_s[i] = jnp.zeros((BLOCK, HEAD), jnp.float32)

    pltpu.make_async_copy(cot_own, cot_ref, cot_sem).wait()

    @pl.loop(0, blocks)
    def _(i):
        q0 = i * BLOCK
        rows = pl.ds(pl.multiple_of(q0, BLOCK), BLOCK)
        token = q0 + lax.broadcasted_iota(jnp.int32, (1, BLOCK), 1)
        low = jnp.maximum(start_of(token), token - (WINDOW - 1))
        token2 = jnp.concatenate([token, token], axis=1)
        low2 = jnp.concatenate([low, low], axis=1)
        first = jnp.maximum(start_of(q0), q0 - (WINDOW - 1)) // BLOCK
        first = jnp.maximum(first, 0)

        acc_s[...] = jnp.zeros_like(acc_s)
        row_s[...] = jnp.zeros_like(row_s)
        query = q_s[i]

        steps = (i - first + UNROLL) // UNROLL
        start = i + 1 - steps * UNROLL

        @pl.loop(0, steps)
        def _(step):
            low_j = start + step * UNROLL
            keys = [jnp.maximum(low_j + u, 0) for u in range(UNROLL)]
            total, mixed = row_s[...], acc_s[...]
            scores = [mm(k_s[j], query, NT) for j in keys]
            for u, j in enumerate(keys):
                slot = low_j + u - i + span + UNROLL - 1
                key_pos = (low_j + u) * BLOCK + lax.broadcasted_iota(jnp.int32, (BLOCK, 2 * BLOCK), 0)
                e = jnp.exp2(scores[u] * exp_scale)
                e = jnp.where((key_pos >= low2) & (key_pos <= token2), e, 0.0)
                e_s[slot] = e
                eb = e.astype(jnp.bfloat16)
                eb_s[slot] = eb
                total += jnp.sum(e.reshape(BLOCK // 8, 8, 2 * BLOCK), axis=0)
                mixed += mm(vt_s[j], eb)
            row_s[...], acc_s[...] = total, mixed

        inv = 1.0 / jnp.sum(row_s[...], axis=0, keepdims=True)
        out_t = acc_s[...] * inv
        dot = jnp.concatenate(
            [cot_ref[rows, h * HEAD : (h + 1) * HEAD].T.astype(jnp.float32) for h in range(2)], axis=1
        )
        for h in range(2):
            out_ref[rows, h * HEAD : (h + 1) * HEAD] = (
                out_t[:, h * BLOCK : (h + 1) * BLOCK].astype(jnp.bfloat16).T
            )
        store(i, 0).start()
        delta = jnp.sum(out_t * dot, axis=0, keepdims=True) * inv
        dot_s[...] = (dot * inv).astype(jnp.bfloat16)
        dout = dot_s[...].T
        acc_s[...] = jnp.zeros_like(acc_s)

        @pl.loop(0, steps)
        def _(step):
            low_j = start + step * UNROLL
            keys = [jnp.maximum(low_j + u, 0) for u in range(UNROLL)]
            slots = [low_j + u - i + span + UNROLL - 1 for u in range(UNROLL)]
            d_probs = [mm(v_s[j], dot_s[...]) for j in keys]
            d_scores = [(e_s[slot] * (dp - delta)).astype(jnp.bfloat16) for slot, dp in zip(slots, d_probs)]
            d_values = [mm(eb_s[slot], dout) for slot in slots]
            d_keys = [mm(ds, query) for ds in d_scores]
            mixed = acc_s[...]
            for j, ds in zip(keys, d_scores):
                mixed += mm(kt_s[j], ds)
            acc_s[...] = mixed
            for j, dv, dk in zip(keys, d_values, d_keys):
                dv_s[j] += dv
                dk_s[j] += dk

        cosine, sine = tables(i)
        for h in range(2):
            g = acc_s[:, h * BLOCK : (h + 1) * BLOCK].T * score_scale
            x = proj_ref[rows, h * HEAD : (h + 1) * HEAD]
            dx = norm_back(rotate_back(g, cosine, sine), x, gq_ref[...])
            dproj_ref[rows, h * HEAD : (h + 1) * HEAD] = dx.astype(jnp.bfloat16)
        store(i, 1).start()

    @pl.loop(0, blocks)
    def _(i):
        rows = pl.ds(pl.multiple_of(i * BLOCK, BLOCK), BLOCK)
        cosine, sine = tables(i)
        x = proj_ref[rows, 2 * HEAD : 3 * HEAD]
        dx = norm_back(rotate_back(dk_s[i] * score_scale, cosine, sine), x, gk_ref[...])
        dproj_ref[rows, 2 * HEAD : 3 * HEAD] = dx.astype(jnp.bfloat16)
        dproj_ref[rows, 3 * HEAD : 4 * HEAD] = dv_s[i].astype(jnp.bfloat16)
        store(i, 2).start()

    for i in range(blocks):
        for k in range(3):
            store(i, k).wait()


def attention(docs, docs2, proj, cot, cot2, gain_q, gain_k):
    length = proj.shape[0]
    blocks = length // BLOCK
    slots = WINDOW // BLOCK + UNROLL
    vmem = pl.BlockSpec(memory_space=pltpu.VMEM)
    bf, f32 = jnp.bfloat16, jnp.float32
    return pl.pallas_call(
        attention_kernel,
        out_shape=(
            jax.ShapeDtypeStruct((length, 2 * HEAD), bf),
            jax.ShapeDtypeStruct((length, 4 * HEAD), bf),
        ),
        in_specs=[pl.BlockSpec(memory_space=pltpu.SMEM)] * 2
        + [pl.BlockSpec(memory_space=pl.ANY)] * 3
        + [vmem] * 6,
        out_specs=(pl.BlockSpec(memory_space=pl.ANY), pl.BlockSpec(memory_space=pl.ANY)),
        scratch_shapes=[
            pltpu.VMEM((length, 2 * HEAD), bf),
            pltpu.SemaphoreType.DMA(()),
            pltpu.VMEM((length, 4 * HEAD), f32),
            pltpu.VMEM((length, 2 * HEAD), bf),
            pltpu.VMEM((length, 4 * HEAD), bf),
            pltpu.SemaphoreType.DMA((blocks,)),
            pltpu.SemaphoreType.DMA((blocks, 3)),
            pltpu.VMEM((blocks, 2 * BLOCK, HEAD), bf),
            pltpu.VMEM((blocks, BLOCK, HEAD), bf),
            pltpu.VMEM((blocks, HEAD, BLOCK), bf),
            pltpu.VMEM((blocks, BLOCK, HEAD), bf),
            pltpu.VMEM((blocks, HEAD, BLOCK), bf),
            pltpu.VMEM((slots, BLOCK, 2 * BLOCK), f32),
            pltpu.VMEM((slots, BLOCK, 2 * BLOCK), bf),
            pltpu.VMEM((blocks, BLOCK, HEAD), f32),
            pltpu.VMEM((blocks, BLOCK, HEAD), f32),
            pltpu.VMEM((HEAD, 2 * BLOCK), f32),
            pltpu.VMEM((HEAD, 2 * BLOCK), bf),
            pltpu.VMEM((8, 2 * BLOCK), f32),
        ],
        compiler_params=pltpu.CompilerParams(vmem_limit_bytes=60 * 1024 * 1024),
        name="attention",
    )(docs, docs2, proj, cot, cot2, *rope_tables(blocks), gain_q.reshape(1, HEAD), gain_k.reshape(1, HEAD))


MESH = pl.DeviceIdType.MESH
KH = 1408
PAD = 64
HALF_ROWS = 64


class Place:
    def __init__(self):
        d, s = lax.axis_index("dp"), lax.axis_index("seq")
        self.z, self.c = d // 2, d % 2
        self.y, self.x = s // 4, s % 4
        self.t = self.x // 2
        self.xp = 3 - self.x
        self.xs = self.x + 1 - 2 * (self.x % 2)
        self.xsp = 3 - self.xs
        self.up_y, self.down_y, self.far_y = (self.y + 1) % 4, (self.y + 3) % 4, (self.y + 2) % 4
        self.same = self.c == self.t
        self.beside = self.at(x=self.xs)
        self.up, self.down = self.at(y=self.up_y), self.at(y=self.down_y)
        self.sibling = self.at(c=1 - self.c)

    def at(self, z=None, c=None, y=None, x=None):
        z = self.z if z is None else z
        c = self.c if c is None else c
        y = self.y if y is None else y
        x = self.x if x is None else x
        return (z * 2 + c, y * 4 + x)


def meet(devices):
    barrier = pltpu.get_barrier_semaphore()
    for device in devices:
        pl.semaphore_signal(barrier, inc=1, device_id=device, device_id_type=MESH)
    pl.semaphore_wait(barrier, len(devices))


class Sends:
    def __init__(self, sems):
        self.sems, self.count, self.open = sems, 0, []

    def sem(self):
        self.count += 1
        return self.sems.at[self.count - 1]

    def send(self, src, dst, recv, device, when=None):
        copy = pltpu.make_async_remote_copy(
            src_ref=src, dst_ref=dst, send_sem=self.sem(), recv_sem=recv,
            device_id=device, device_id_type=MESH,
        )
        if when is None:
            copy.start()
        else:
            pl.when(when)(copy.start)
        self.open.append((copy, when))

    def finish(self):
        for copy, when in self.open:
            if when is None:
                copy.wait_send()
            else:
                pl.when(when)(copy.wait_send)


def arrive(dst, sem):
    pltpu.make_async_copy(dst, dst, sem).wait()


def gather_kernel(
    tokens, wq, wk, wv, cot, docs, proj_hbm, tok_out, w_out, cot_out, docs_out,
    tok, w, wj, wx, other, sib, send_s, p_s, q_s, first_s, w_s, misc_s, sib_s, local_s, join_s, proj_out, proj_s,
):
    me = Place()
    z, c, y, x, t, same = me.z, me.c, me.y, me.x, me.t, me.same
    sends = Sends(send_s)
    width = 4 * HEAD
    part = {"p": (pl.ds(0, HALF_ROWS), p_s), "q": (pl.ds(HALF_ROWS, HALF_ROWS), q_s)}
    piece_rows = wj.shape[0]
    joins = [
        pltpu.make_async_copy(src, wj.at[:, pl.ds(low, src.shape[1])], join_s.at[k])
        for k, (src, low) in enumerate(((wq, 0), (wk, 2 * HEAD), (wv, 3 * HEAD)))
    ]
    for join in joins:
        join.start()
    meet(
        [me.sibling, me.beside, me.up, me.down, me.at(c=0, x=me.xp), me.at(c=1, x=me.xp)]
        + [me.at(z=(z + k) % 4, c=core) for k in (1, 2, 3) for core in range(2)]
    )

    def forward(name, slot, device):
        rows, sems = part[name]
        ref = tok.at[slot, rows, :]
        sends.send(ref, ref, sems.at[slot], device)

    def landed(name, slot):
        rows, sems = part[name]
        arrive(tok.at[slot, rows, :], sems.at[slot])

    own, pair = y * 4 + x, y * 4 + me.xp
    target_x = jnp.where(same, x, me.xp)
    first = first_s.at[jnp.where(same, 0, 1)]
    for k in range(2):
        local = same & (c == k)
        src = tokens.at[:, pl.ds(k * (tokens.shape[1] - KH), KH)]
        sends.send(src, tok.at[own], first, me.at(c=k, x=target_x), when=jnp.logical_not(local))

        @pl.when(local)
        def _():
            pltpu.make_async_copy(src, tok.at[own], first_s.at[0]).start()

    for join in joins:
        join.wait()

    sends.send(wj, wx, misc_s.at[0], me.at(x=me.xp))
    sends.send(docs, docs_out, misc_s.at[2], me.sibling)

    target_c = z // 2
    piece = (z % 2) * 2 + c

    def spread(src, g):
        rows = pl.ds(pl.multiple_of(target_c * PAD + piece * piece_rows, 16), piece_rows)
        dst = w.at[rows, pl.ds(pl.multiple_of(g * width, width), width)]
        sem = w_s.at[piece * 2 + g]
        here = target_c == c
        for k in (1, 3, 2):
            sends.send(src, dst, sem, me.at(z=(z + k) % 4, c=target_c))
        sends.send(src, dst, sem, me.sibling, when=jnp.logical_not(here))

        @pl.when(here)
        def _():
            pltpu.make_async_copy(src, dst, sem).start()

    w[pl.ds(pl.multiple_of((1 - c) * 4 * piece_rows, PAD), PAD), :] = jnp.zeros((PAD, 2 * width), jnp.bfloat16)
    below, above, far = me.down_y * 4, me.up_y * 4, me.far_y * 4
    here, beside = (x, me.xp), (me.xs, me.xsp)
    for slot, sem in ((own, 0), (pair, 1)):
        arrive(tok.at[slot], first_s.at[sem])
        forward("q", slot, me.up)
        forward("q", slot, me.down)
        forward("p", slot, me.beside)
        forward("p", slot, me.up)
        forward("p", slot, me.down)
        forward("q", slot, me.beside)
        if sem == 0:
            spread(wj, t)
            landed("q", below + x)
            forward("q", below + x, me.up)
            forward("q", below + x, me.beside)
    arrive(wx, misc_s.at[0])
    spread(wx, 1 - t)
    swap = jnp.logical_not(same)
    sends.send(cot, cot_out, misc_s.at[1], me.at(c=1 - c, x=me.xp), when=swap)
    landed("q", above + x)
    forward("q", above + x, me.beside)
    landed("q", above + me.xp)
    forward("q", above + me.xp, me.down)
    forward("q", above + me.xp, me.beside)
    landed("q", below + me.xp)
    forward("q", below + me.xp, me.beside)
    for column in beside:
        landed("p", y * 4 + column)
        forward("p", y * 4 + column, me.up)
        forward("p", y * 4 + column, me.down)
    for column in here:
        landed("p", below + column)
        forward("p", below + column, me.up)
        landed("q", far + column)
        forward("q", far + column, me.beside)
    for column in beside:
        landed("p", above + column)
        forward("p", above + column, me.down)

    for i in range(4):
        for g in range(2):
            arrive(w.at[pl.ds(i * piece_rows, piece_rows), pl.ds(g * width, width)], w_s.at[i * 2 + g])
    pltpu.make_async_copy(w, w_out, local_s.at[4]).start()

    plan = (
        (0, "p", ()),
        (0, "q", beside),
        (1, "q", beside),
        (2, "q", beside),
        (1, "p", beside),
        (2, "p", here),
        (3, "p", here + beside),
        (3, "q", beside),
    )
    lines = (y, me.down_y, me.up_y, me.far_y)
    done = [0, 0, 0, 0]
    units = []

    def complete(n):
        slots, rows = units[n]
        arrive(sib.at[slots, rows, :], sib_s.at[n])
        proj_out[slots, rows, :] += sib[slots, rows, :]
        pltpu.make_async_copy(
            proj_out.at[slots, rows, :], proj_hbm.at[slots, rows, :], proj_s.at[n]
        ).start()

    for n, (line, name, need) in enumerate(plan):
        row = lines[line]
        for column in need:
            landed(name, row * 4 + column)
        slots = pl.ds(pl.multiple_of(row * 4, 4), 4)
        done[line] += 1
        if done[line] == 2:
            pltpu.make_async_copy(tok.at[slots], tok_out.at[slots], local_s.at[line]).start()
        rows = part[name][0]
        block = tok[slots, rows, :].reshape(4 * HALF_ROWS, KH)
        shape = (4, HALF_ROWS, width)
        other[slots, rows, :] = mm(block, w[:, pl.ds(pl.multiple_of((1 - c) * width, width), width)]).reshape(shape)
        sends.send(other.at[slots, rows, :], sib.at[slots, rows, :], sib_s.at[n], me.sibling)
        proj_out[slots, rows, :] = mm(block, w[:, pl.ds(pl.multiple_of(c * width, width), width)]).reshape(shape)
        units.append((slots, rows))
        if n:
            complete(n - 1)
    complete(len(plan) - 1)
    for n, (slots, rows) in enumerate(units):
        pltpu.make_async_copy(
            proj_out.at[slots, rows, :], proj_hbm.at[slots, rows, :], proj_s.at[n]
        ).wait()
    for n, row in enumerate(lines):
        slots = pl.ds(pl.multiple_of(row * 4, 4), 4)
        pltpu.make_async_copy(tok.at[slots], tok_out.at[slots], local_s.at[n]).wait()
    pltpu.make_async_copy(w, w_out, local_s.at[4]).wait()
    arrive(docs_out, misc_s.at[2])
    pl.when(swap)(lambda: arrive(cot_out, misc_s.at[1]))
    sends.finish()


def gather(tokens, wq, wk, wv, cot, docs):
    f32, bf = jnp.float32, jnp.bfloat16
    anywhere = pl.BlockSpec(memory_space=pl.ANY)
    dma = pltpu.SemaphoreType.DMA
    return pl.pallas_call(
        gather_kernel,
        out_shape=(
            jax.ShapeDtypeStruct((16, 128, 4 * HEAD), f32),
            jax.ShapeDtypeStruct((16, 128, KH), bf),
            jax.ShapeDtypeStruct((KH, 8 * HEAD), bf),
            jax.ShapeDtypeStruct(cot.shape, bf),
            jax.ShapeDtypeStruct(docs.shape, docs.dtype),
        ),
        in_specs=[anywhere] * 6,
        out_specs=(anywhere,) * 5,
        scratch_shapes=[
            pltpu.VMEM((16, 128, KH), bf),
            pltpu.VMEM((KH, 8 * HEAD), bf),
            pltpu.VMEM((wq.shape[0], 4 * HEAD), bf),
            pltpu.VMEM((wq.shape[0], 4 * HEAD), bf),
            pltpu.VMEM((16, 128, 4 * HEAD), f32),
            pltpu.VMEM((16, 128, 4 * HEAD), f32),
            dma((64,)), dma((16,)), dma((16,)), dma((2,)), dma((8,)), dma((3,)), dma((8,)), dma((5,)), dma((3,)),
            pltpu.VMEM((16, 128, 4 * HEAD), f32), dma((8,)),
        ],
        compiler_params=pltpu.CompilerParams(
            collective_id=0, has_side_effects=True, vmem_limit_bytes=60 * 1024 * 1024
        ),
        name="gather",
    )(tokens, wq, wk, wv, cot, docs)


def scatter_kernel(
    attn, dproj, tok_in, w_in, attn_out, token_out, gq_out, gk_out, gv_out,
    tok, w, dpj, terms, dw, rqx, rp1, rp2, rpx, rq1, rq2, rw, rwx, wsum, grad_out,
    send_s, attn_s, dp_s, local_s, qx_s, p1_s, p2_s, px_s, q1_s, q2_s, rw_s, g_s, rwx_s,
):
    me = Place()
    z, c, y, x, t, same = me.z, me.c, me.y, me.x, me.t, me.same
    sends = Sends(send_s)
    width = 4 * HEAD
    p_rows, q_rows = pl.ds(0, HALF_ROWS), pl.ds(HALF_ROWS, HALF_ROWS)
    order = (me.far_y, me.up_y, me.down_y, y)
    mine = pl.ds(pl.multiple_of(c * width, width), width)
    piece_rows = gq_out.shape[0]

    for n, row in enumerate(order):
        rows = pl.ds(pl.multiple_of(row * 512, 512), 512)
        pltpu.make_async_copy(dproj.at[rows, :], dpj.at[rows, mine], local_s.at[n]).start()
        if n == 0:
            pltpu.make_async_copy(w_in, w, local_s.at[4]).start()
    pltpu.make_async_copy(tok_in, tok, local_s.at[5]).start()
    meet(
        [me.sibling]
        + [
            me.at(c=core, y=(y + dy) % 4, x=(x + dx) % 4)
            for dy in range(4) for dx in range(4) if dy or dx for core in range(2)
        ]
        + [me.at(z=(z + k) % 4, c=core) for k in (1, 2, 3) for core in range(2)]
    )
    for n, row in enumerate(order):
        rows = pl.ds(pl.multiple_of(row * 512, 512), 512)
        sends.send(dproj.at[rows, :], dpj.at[rows, mine], dp_s.at[n], me.sibling)

    def add(dst, *sources):
        total = dst[...].astype(jnp.float32)
        for source in sources:
            total = total + source[...].astype(jnp.float32)
        dst[...] = total.astype(jnp.bfloat16)

    def compute(n):
        row = order[n]
        rows = pl.ds(pl.multiple_of(row * 512, 512), 512)
        arrive(dpj.at[rows, pl.ds(0, width)], local_s.at[n])
        arrive(dpj.at[rows, pl.ds(0, width)], dp_s.at[n])
        if n == 0:
            arrive(w, local_s.at[4])
        slots = pl.ds(pl.multiple_of(row * 4, 4), 4)
        term = mm(dpj[rows, :], w[...], NT).astype(jnp.bfloat16)
        terms[slots] = term.reshape(4, 128, KH)
        for k, column in enumerate((me.xs, me.xsp)):
            sends.send(terms.at[row * 4 + column, q_rows, :], rqx.at[n, k], qx_s.at[n, k], me.beside)

    def weight_terms(i):
        if i == 0:
            arrive(tok, local_s.at[5])
        low, high = ((0, 512), (512, 768), (768, 1152), (1152, KH))[i]
        left = tok[:, :, low:high].reshape(16 * 128, high - low)
        dw[low:high, :] = mm(left, dpj[...], (((0,), (0,)), ((), ()))).astype(jnp.bfloat16)
        for g in range(2):
            rows = pl.ds(pl.multiple_of(c * PAD + i * piece_rows, 16), piece_rows)
            src = dw.at[rows, pl.ds(g * width, width)]
            dst, sem = rw.at[z * 2 + g], rw_s.at[z * 2 + g]
            to_z, to_c = 2 * c + i // 2, i % 2
            stays = (to_z == z) & (c == to_c)
            sends.send(src, dst, sem, me.at(z=to_z, c=to_c), when=jnp.logical_not(stays))

            @pl.when(stays)
            def _():
                pltpu.make_async_copy(src, dst, sem).start()

    def exchanged(n):
        for k, column in enumerate((x, me.xp)):
            arrive(rqx.at[n, k], qx_s.at[n, k])
            add(terms.at[order[n] * 4 + column, q_rows, :], rqx.at[n, k])

    def finish(n, rows):
        src, dst, sem = terms.at[own + me.xp, rows, :], grad_out.at[c, rows, :], g_s.at[c, n]
        sends.send(src, dst, sem, me.at(c=t, x=me.xp))
        src = terms.at[own + x, rows, :]
        sends.send(src, dst, sem, me.sibling, when=jnp.logical_not(same))

        @pl.when(same)
        def _():
            pltpu.make_async_copy(src, dst, sem).start()

    far, up, down, own = me.far_y * 4, me.up_y * 4, me.down_y * 4, y * 4
    group = y * 4 + jnp.where(same, x, me.xp)
    columns = pl.ds(pl.multiple_of(group * 2 * HEAD, 2 * HEAD), 2 * HEAD)
    compute(0)
    sends.send(terms.at[pl.ds(far, 2), p_rows, :], rp1.at[0], p1_s.at[0], me.up)
    sends.send(terms.at[pl.ds(far + 2, 2), p_rows, :], rp1.at[1], p1_s.at[1], me.down)
    compute(1)
    compute(2)
    compute(3)
    weight_terms(0)
    weight_terms(1)
    arrive(rp1.at[0], p1_s.at[0])
    add(terms.at[pl.ds(up, 2), p_rows, :], rp1.at[0])
    sends.send(terms.at[pl.ds(up, 4), p_rows, :], rp2.at[0], p2_s.at[0], me.up)
    arrive(rp1.at[1], p1_s.at[1])
    add(terms.at[pl.ds(down + 2, 2), p_rows, :], rp1.at[1])
    sends.send(terms.at[pl.ds(down, 4), p_rows, :], rp2.at[1], p2_s.at[1], me.down)
    weight_terms(2)
    weight_terms(3)
    exchanged(0)
    sends.send(terms.at[far + x, q_rows, :], rq1.at[0], q1_s.at[0], me.up)
    sends.send(terms.at[far + me.xp, q_rows, :], rq1.at[1], q1_s.at[1], me.down)
    for n, base, extra, device in ((1, up, x, me.up), (2, down, me.xp, me.down)):
        exchanged(n)
        arrive(rq1.at[n - 1], q1_s.at[n - 1])
        add(terms.at[base + extra, q_rows, :], rq1.at[n - 1])
        for k, column in enumerate((x, me.xp)):
            sends.send(terms.at[base + column, q_rows, :], rq2.at[n - 1, k], q2_s.at[n - 1, k], device)
    arrive(rp2.at[0], p2_s.at[0])
    arrive(rp2.at[1], p2_s.at[1])
    add(terms.at[pl.ds(own, 4), p_rows, :], rp2.at[0], rp2.at[1])
    for k, column in enumerate((me.xs, me.xsp)):
        sends.send(terms.at[own + column, p_rows, :], rpx.at[k], px_s.at[k], me.beside)

    def summed(g):
        total = rw[g].astype(jnp.float32)
        for k in range(1, 4):
            total = total + rw[2 * k + g].astype(jnp.float32)
        return total

    for dy in range(4):
        for dx in range(4):
            to_y, to_x = (y + dy) % 4, (x + dx) % 4
            rows = pl.ds(pl.multiple_of((to_y * 4 + to_x) * 128, 128), 128)
            src, dst = attn.at[rows, :], attn_out.at[:, columns]
            if dy == 0 and dx == 0:
                sends.send(src, dst, attn_s.at[group], me.sibling, when=jnp.logical_not(same))

                @pl.when(same)
                def _():
                    pltpu.make_async_copy(src, dst, attn_s.at[group]).start()
            else:
                sends.send(src, dst, attn_s.at[group], me.at(c=t, y=to_y, x=to_x))

    for k, column in enumerate((x, me.xp)):
        arrive(rqx.at[3, k], qx_s.at[3, k])
        arrive(rq2.at[0, k], q2_s.at[0, k])
        arrive(rq2.at[1, k], q2_s.at[1, k])
        add(terms.at[own + column, q_rows, :], rqx.at[3, k], rq2.at[0, k], rq2.at[1, k])
    finish(1, q_rows)
    for k in range(8):
        arrive(rw.at[k], rw_s.at[k])
    wsum[...] = summed(1 - t).astype(jnp.bfloat16)
    sends.send(wsum, rwx, rwx_s.at[0], me.at(x=me.xp))
    for k, column in enumerate((x, me.xp)):
        arrive(rpx.at[k], px_s.at[k])
        add(terms.at[own + column, p_rows, :], rpx.at[k])
    finish(0, p_rows)
    total = summed(t)
    arrive(rwx, rwx_s.at[0])
    total = total + rwx[...].astype(jnp.float32)
    gq_out[...] = total[:, : 2 * HEAD]
    gk_out[...] = total[:, 2 * HEAD : 3 * HEAD]
    gv_out[...] = total[:, 3 * HEAD :]
    for k in range(16):
        arrive(attn_out.at[:, pl.ds(k * 2 * HEAD, 2 * HEAD)], attn_s.at[k])
    for k in range(2):
        for n, rows in ((0, p_rows), (1, q_rows)):
            arrive(grad_out.at[k, rows, :], g_s.at[k, n])
    low = token_out.shape[1] - KH
    lane = lax.broadcasted_iota(jnp.int32, (128, KH - low), 1)
    token_out[:, :low] = grad_out[0, :, :low]
    token_out[:, low:KH] = jnp.where(lane < PAD, grad_out[0, :, low:], grad_out[1, :, : KH - low])
    token_out[:, KH:] = grad_out[1, :, KH - low :]
    sends.finish()


def scatter(attn, dproj, tok, w, piece_rows):
    f32, bf = jnp.float32, jnp.bfloat16
    anywhere = pl.BlockSpec(memory_space=pl.ANY)
    vmem = pl.BlockSpec(memory_space=pltpu.VMEM)
    dma = pltpu.SemaphoreType.DMA
    length = attn.shape[0]
    half = (HALF_ROWS, KH)
    return pl.pallas_call(
        scatter_kernel,
        out_shape=(
            jax.ShapeDtypeStruct((128, 32 * HEAD), bf),
            jax.ShapeDtypeStruct((128, 2 * (KH - PAD)), bf),
            jax.ShapeDtypeStruct((piece_rows, 2 * HEAD), f32),
            jax.ShapeDtypeStruct((piece_rows, HEAD), f32),
            jax.ShapeDtypeStruct((piece_rows, HEAD), f32),
        ),
        in_specs=[anywhere] * 4,
        out_specs=(anywhere, vmem, vmem, vmem, vmem),
        scratch_shapes=[
            pltpu.VMEM((16, 128, KH), bf),
            pltpu.VMEM((KH, 8 * HEAD), bf),
            pltpu.VMEM((length, 8 * HEAD), bf),
            pltpu.VMEM((16, 128, KH), bf),
            pltpu.VMEM((KH, 8 * HEAD), bf),
            pltpu.VMEM((4, 2) + half, bf),
            pltpu.VMEM((2, 2) + half, bf),
            pltpu.VMEM((2, 4) + half, bf),
            pltpu.VMEM((2,) + half, bf),
            pltpu.VMEM((2,) + half, bf),
            pltpu.VMEM((2, 2) + half, bf),
            pltpu.VMEM((8, piece_rows, 4 * HEAD), bf),
            pltpu.VMEM((piece_rows, 4 * HEAD), bf),
            pltpu.VMEM((piece_rows, 4 * HEAD), bf),
            pltpu.VMEM((2, 128, KH), bf),
            dma((60,)), dma((16,)), dma((4,)), dma((6,)), dma((4, 2)), dma((2,)), dma((2,)),
            dma((2,)), dma((2,)), dma((2, 2)), dma((8,)), dma((2, 2)), dma((1,)),
        ],
        compiler_params=pltpu.CompilerParams(
            collective_id=1, has_side_effects=True, vmem_limit_bytes=50 * 1024 * 1024
        ),
        name="scatter",
    )(attn, dproj, tok, w)


def local(
    tokens, q_weight, key_projection, value_projection, query_norm_gain, key_norm_gain, doc_lengths, out_cot
):
    proj, tok, w, cot2, docs2 = gather(
        tokens, q_weight, key_projection, value_projection, out_cot, doc_lengths
    )
    proj = proj.reshape(out_cot.shape[0], 4 * HEAD)
    attn, dproj = attention(
        doc_lengths, docs2, proj, out_cot, cot2, query_norm_gain, key_norm_gain
    )
    attn_out, token_grad, gq, gk, gv = scatter(attn, dproj, tok, w, q_weight.shape[0])
    return (attn_out, token_grad, gq, gk, gv)


def solution(mesh):
    placed = (
        P(("dp", "seq"), None),
        P("dp", "seq"),
        P("dp", "seq"),
        P("dp", "seq"),
        P(),
        P(),
        P("dp", None),
        P("dp", "seq"),
    )
    return jax.shard_map(
        local,
        mesh=mesh,
        in_specs=placed,
        out_specs=(
            P(("dp", "seq"), None),
            P(("dp", "seq"), None),
            P("dp", "seq"),
            P("dp", "seq"),
            P("dp", "seq"),
        ),
        check_vma=False,
    )
```

```python
import functools
import math

import jax
import jax.numpy as jnp
import numpy as np
from jax import lax
from jax.experimental import pallas as pl
from jax.experimental.pallas import tpu as pltpu
from jax.sharding import PartitionSpec as P

HEAD = 128
WINDOW = 1024
BLOCK = 256
UNROLL = 2
score_scale = 168.0 ** (-0.5)
exp_scale = score_scale * math.log2(math.e)
rope_base = 10000.0
norm_eps = 1e-06
NN = (((1,), (0,)), ((), ()))
NT = (((1,), (1,)), ((), ()))


def mm(a, b, dims=NN):
    return lax.dot_general(a, b, dims, preferred_element_type=jnp.float32)


def rope_tables(blocks):
    inverse = rope_base ** (-np.arange(HEAD // 2) * (2.0 / HEAD))
    inverse = np.concatenate([inverse, inverse])[None, :]
    coarse = (np.arange(blocks) * BLOCK)[:, None] * inverse
    fine = np.arange(BLOCK)[:, None] * inverse
    return [
        jnp.asarray(table, jnp.float32)
        for table in (np.cos(coarse), np.sin(coarse), np.cos(fine), np.sin(fine))
    ]


def norm_factor(x):
    return lax.rsqrt(jnp.mean(x * x, axis=-1, keepdims=True) + norm_eps)


def rotate(n, cosine, sine):
    return n * cosine + pltpu.roll(n, HEAD // 2, 1) * sine


def rotate_back(g, cosine, sine):
    return g * cosine + pltpu.roll(g * sine, HEAD // 2, 1)


def norm_back(dn, x, gain):
    factor = norm_factor(x)
    dn = dn * gain
    inner = jnp.sum(x * dn, axis=-1, keepdims=True) * (1.0 / HEAD)
    return factor * dn - x * (factor * factor * factor * inner)


def attention_kernel(
    docs_ref, docs2_ref, proj_hbm, cot_own, cot_got, cos_a, sin_a, cos_b, sin_b, gq_ref, gk_ref, both_hbm,
    cot_ref, cot_sem, proj_ref, out_ref, dproj_ref, in_sem, out_sem, q_s, k_s, kt_s, v_s, vt_s, e_s, eb_s, dk_s, dv_s, acc_s, dot_s, row_s,
):
    length = proj_hbm.shape[0]
    blocks = length // BLOCK
    span = WINDOW // BLOCK
    def block_rows(i):
        return pl.ds(pl.multiple_of(i * BLOCK, BLOCK), BLOCK)

    def load(i):
        rows = block_rows(i)
        return pltpu.make_async_copy(proj_hbm.at[rows, :], proj_ref.at[rows, :], in_sem.at[i])

    def store(i, k):
        rows = block_rows(i)
        src, low = ((out_ref, 0), (dproj_ref, 0), (dproj_ref, 2 * HEAD))[k]
        return pltpu.make_async_copy(
            src.at[rows, pl.ds(low, 2 * HEAD)],
            both_hbm.at[rows, pl.ds(k * 2 * HEAD, 2 * HEAD)],
            out_sem.at[i, k],
        )

    for i in range(blocks):
        load(i).start()
    same = lax.axis_index("dp") % 2 == (lax.axis_index("seq") % 4) // 2
    lane = lax.broadcasted_iota(jnp.int32, (1, HEAD), 1)
    sign = jnp.where(lane < HEAD // 2, -1.0, 1.0)

    def tables(i):
        ca, sa = cos_a[pl.ds(i, 1), :], sin_a[pl.ds(i, 1), :]
        return ca * cos_b[...] - sa * sin_b[...], (sa * sign) * cos_b[...] + (ca * sign) * sin_b[...]

    pl.when(same)(lambda: pltpu.make_async_copy(cot_own, cot_ref, cot_sem).start())
    pl.when(jnp.logical_not(same))(lambda: pltpu.make_async_copy(cot_got, cot_ref, cot_sem).start())
    e0, e1, e2 = [jnp.where(same, docs_ref[0, k], docs2_ref[0, k]) for k in range(3)]
    e1 = e0 + e1
    e2 = e1 + e2

    def start_of(t):
        zero = t * 0
        return jnp.maximum(
            jnp.maximum(jnp.where(t >= e0, e0, zero), jnp.where(t >= e1, e1, zero)),
            jnp.where(t >= e2, e2, zero),
        )

    @pl.loop(0, blocks)
    def _(i):
        load(i).wait()
        rows = pl.ds(pl.multiple_of(i * BLOCK, BLOCK), BLOCK)
        cosine, sine = tables(i)
        for h in range(2):
            x = proj_ref[rows, h * HEAD : (h + 1) * HEAD]
            n = x * norm_factor(x) * gq_ref[...]
            q_s[i, h * BLOCK : (h + 1) * BLOCK, :] = rotate(n, cosine, sine).astype(jnp.bfloat16)
        x = proj_ref[rows, 2 * HEAD : 3 * HEAD]
        n = x * norm_factor(x) * gk_ref[...]
        key = rotate(n, cosine, sine)
        k_s[i] = key.astype(jnp.bfloat16)
        kt_s[i] = key.astype(jnp.bfloat16).T
        value = proj_ref[rows, 3 * HEAD : 4 * HEAD]
        v_s[i] = value.astype(jnp.bfloat16)
        vt_s[i] = value.astype(jnp.bfloat16).T
        dk_s[i] = jnp.zeros((BLOCK, HEAD), jnp.float32)
        dv_s[i] = jnp.zeros((BLOCK, HEAD), jnp.float32)

    pltpu.make_async_copy(cot_own, cot_ref, cot_sem).wait()

    @pl.loop(0, blocks)
    def _(i):
        q0 = i * BLOCK
        rows = pl.ds(pl.multiple_of(q0, BLOCK), BLOCK)
        token = q0 + lax.broadcasted_iota(jnp.int32, (1, BLOCK), 1)
        low = jnp.maximum(start_of(token), token - (WINDOW - 1))
        token2 = jnp.concatenate([token, token], axis=1)
        low2 = jnp.concatenate([low, low], axis=1)
        first = jnp.maximum(start_of(q0), q0 - (WINDOW - 1)) // BLOCK
        first = jnp.maximum(first, 0)

        acc_s[...] = jnp.zeros_like(acc_s)
        row_s[...] = jnp.zeros_like(row_s)
        query = q_s[i]

        steps = (i - first + UNROLL) // UNROLL
        start = i + 1 - steps * UNROLL

        @pl.loop(0, steps)
        def _(step):
            low_j = start + step * UNROLL
            keys = [jnp.maximum(low_j + u, 0) for u in range(UNROLL)]
            total, mixed = row_s[...], acc_s[...]
            scores = [mm(k_s[j], query, NT) for j in keys]
            for u, j in enumerate(keys):
                slot = low_j + u - i + span + UNROLL - 1
                key_pos = (low_j + u) * BLOCK + lax.broadcasted_iota(jnp.int32, (BLOCK, 2 * BLOCK), 0)
                e = jnp.exp2(scores[u] * exp_scale)
                e = jnp.where((key_pos >= low2) & (key_pos <= token2), e, 0.0)
                e_s[slot] = e
                eb = e.astype(jnp.bfloat16)
                eb_s[slot] = eb
                total += jnp.sum(e.reshape(BLOCK // 8, 8, 2 * BLOCK), axis=0)
                mixed += mm(vt_s[j], eb)
            row_s[...], acc_s[...] = total, mixed

        inv = 1.0 / jnp.sum(row_s[...], axis=0, keepdims=True)
        out_t = acc_s[...] * inv
        dot = jnp.concatenate(
            [cot_ref[rows, h * HEAD : (h + 1) * HEAD].T.astype(jnp.float32) for h in range(2)], axis=1
        )
        for h in range(2):
            out_ref[rows, h * HEAD : (h + 1) * HEAD] = (
                out_t[:, h * BLOCK : (h + 1) * BLOCK].astype(jnp.bfloat16).T
            )
        store(i, 0).start()
        delta = jnp.sum(out_t * dot, axis=0, keepdims=True) * inv
        dot_s[...] = (dot * inv).astype(jnp.bfloat16)
        dout = dot_s[...].T
        acc_s[...] = jnp.zeros_like(acc_s)

        @pl.loop(0, steps)
        def _(step):
            low_j = start + step * UNROLL
            keys = [jnp.maximum(low_j + u, 0) for u in range(UNROLL)]
            slots = [low_j + u - i + span + UNROLL - 1 for u in range(UNROLL)]
            d_probs = [mm(v_s[j], dot_s[...]) for j in keys]
            d_scores = [(e_s[slot] * (dp - delta)).astype(jnp.bfloat16) for slot, dp in zip(slots, d_probs)]
            d_values = [mm(eb_s[slot], dout) for slot in slots]
            d_keys = [mm(ds, query) for ds in d_scores]
            mixed = acc_s[...]
            for j, ds in zip(keys, d_scores):
                mixed += mm(kt_s[j], ds)
            acc_s[...] = mixed
            for j, dv, dk in zip(keys, d_values, d_keys):
                dv_s[j] += dv
                dk_s[j] += dk

        cosine, sine = tables(i)
        for h in range(2):
            g = acc_s[:, h * BLOCK : (h + 1) * BLOCK].T * score_scale
            x = proj_ref[rows, h * HEAD : (h + 1) * HEAD]
            dx = norm_back(rotate_back(g, cosine, sine), x, gq_ref[...])
            dproj_ref[rows, h * HEAD : (h + 1) * HEAD] = dx.astype(jnp.bfloat16)
        store(i, 1).start()

    @pl.loop(0, blocks)
    def _(i):
        rows = pl.ds(pl.multiple_of(i * BLOCK, BLOCK), BLOCK)
        cosine, sine = tables(i)
        x = proj_ref[rows, 2 * HEAD : 3 * HEAD]
        dx = norm_back(rotate_back(dk_s[i] * score_scale, cosine, sine), x, gk_ref[...])
        dproj_ref[rows, 2 * HEAD : 3 * HEAD] = dx.astype(jnp.bfloat16)
        dproj_ref[rows, 3 * HEAD : 4 * HEAD] = dv_s[i].astype(jnp.bfloat16)
        store(i, 2).start()

    for i in range(blocks):
        for k in range(3):
            store(i, k).wait()


def attention(docs, docs2, proj, cot, cot2, gain_q, gain_k):
    length = proj.shape[0]
    blocks = length // BLOCK
    slots = WINDOW // BLOCK + UNROLL
    vmem = pl.BlockSpec(memory_space=pltpu.VMEM)
    bf, f32 = jnp.bfloat16, jnp.float32
    return pl.pallas_call(
        attention_kernel,
        out_shape=jax.ShapeDtypeStruct((length, 6 * HEAD), bf),
        in_specs=[pl.BlockSpec(memory_space=pltpu.SMEM)] * 2
        + [pl.BlockSpec(memory_space=pl.ANY)] * 3
        + [vmem] * 6,
        out_specs=pl.BlockSpec(memory_space=pl.ANY),
        scratch_shapes=[
            pltpu.VMEM((length, 2 * HEAD), bf),
            pltpu.SemaphoreType.DMA(()),
            pltpu.VMEM((length, 4 * HEAD), f32),
            pltpu.VMEM((length, 2 * HEAD), bf),
            pltpu.VMEM((length, 4 * HEAD), bf),
            pltpu.SemaphoreType.DMA((blocks,)),
            pltpu.SemaphoreType.DMA((blocks, 3)),
            pltpu.VMEM((blocks, 2 * BLOCK, HEAD), bf),
            pltpu.VMEM((blocks, BLOCK, HEAD), bf),
            pltpu.VMEM((blocks, HEAD, BLOCK), bf),
            pltpu.VMEM((blocks, BLOCK, HEAD), bf),
            pltpu.VMEM((blocks, HEAD, BLOCK), bf),
            pltpu.VMEM((slots, BLOCK, 2 * BLOCK), f32),
            pltpu.VMEM((slots, BLOCK, 2 * BLOCK), bf),
            pltpu.VMEM((blocks, BLOCK, HEAD), f32),
            pltpu.VMEM((blocks, BLOCK, HEAD), f32),
            pltpu.VMEM((HEAD, 2 * BLOCK), f32),
            pltpu.VMEM((HEAD, 2 * BLOCK), bf),
            pltpu.VMEM((8, 2 * BLOCK), f32),
        ],
        compiler_params=pltpu.CompilerParams(vmem_limit_bytes=60 * 1024 * 1024),
        name="attention",
    )(docs, docs2, proj, cot, cot2, *rope_tables(blocks), gain_q.reshape(1, HEAD), gain_k.reshape(1, HEAD))


MESH = pl.DeviceIdType.MESH
KH = 1408
PAD = 64
HALF_ROWS = 64


class Place:
    def __init__(self):
        d, s = lax.axis_index("dp"), lax.axis_index("seq")
        self.z, self.c = d // 2, d % 2
        self.y, self.x = s // 4, s % 4
        self.t = self.x // 2
        self.xp = 3 - self.x
        self.xs = self.x + 1 - 2 * (self.x % 2)
        self.xsp = 3 - self.xs
        self.up_y, self.down_y, self.far_y = (self.y + 1) % 4, (self.y + 3) % 4, (self.y + 2) % 4
        self.same = self.c == self.t
        self.beside = self.at(x=self.xs)
        self.up, self.down = self.at(y=self.up_y), self.at(y=self.down_y)
        self.sibling = self.at(c=1 - self.c)

    def at(self, z=None, c=None, y=None, x=None):
        z = self.z if z is None else z
        c = self.c if c is None else c
        y = self.y if y is None else y
        x = self.x if x is None else x
        return (z * 2 + c, y * 4 + x)


def meet(devices):
    barrier = pltpu.get_barrier_semaphore()
    for device in devices:
        pl.semaphore_signal(barrier, inc=1, device_id=device, device_id_type=MESH)
    pl.semaphore_wait(barrier, len(devices))


class Sends:
    def __init__(self, sems):
        self.sems, self.count, self.open = sems, 0, []

    def sem(self):
        self.count += 1
        return self.sems.at[self.count - 1]

    def send(self, src, dst, recv, device, when=None):
        copy = pltpu.make_async_remote_copy(
            src_ref=src, dst_ref=dst, send_sem=self.sem(), recv_sem=recv,
            device_id=device, device_id_type=MESH,
        )
        if when is None:
            copy.start()
        else:
            pl.when(when)(copy.start)
        self.open.append((copy, when))

    def finish(self):
        for copy, when in self.open:
            if when is None:
                copy.wait_send()
            else:
                pl.when(when)(copy.wait_send)


def arrive(dst, sem):
    pltpu.make_async_copy(dst, dst, sem).wait()


def gather_kernel(
    tokens, wq, wk, wv, cot, docs, proj_hbm, tok_out, w_out, cot_out, docs_out,
    tok, w, wj, wx, other, sib, send_s, p_s, q_s, first_s, w_s, misc_s, sib_s, local_s, join_s, proj_out, proj_s,
):
    me = Place()
    z, c, y, x, t, same = me.z, me.c, me.y, me.x, me.t, me.same
    sends = Sends(send_s)
    width = 4 * HEAD
    part = {"p": (pl.ds(0, HALF_ROWS), p_s), "q": (pl.ds(HALF_ROWS, HALF_ROWS), q_s)}
    piece_rows = wj.shape[0]
    joins = [
        pltpu.make_async_copy(src, wj.at[:, pl.ds(low, src.shape[1])], join_s.at[k])
        for k, (src, low) in enumerate(((wq, 0), (wk, 2 * HEAD), (wv, 3 * HEAD)))
    ]
    for join in joins:
        join.start()
    meet(
        [me.sibling, me.beside, me.up, me.down, me.at(c=0, x=me.xp), me.at(c=1, x=me.xp)]
        + [me.at(z=(z + k) % 4, c=core) for k in (1, 2, 3) for core in range(2)]
    )

    def forward(name, slot, device):
        rows, sems = part[name]
        ref = tok.at[slot, rows, :]
        sends.send(ref, ref, sems.at[slot], device)

    def landed(name, slot):
        rows, sems = part[name]
        arrive(tok.at[slot, rows, :], sems.at[slot])

    own, pair = y * 4 + x, y * 4 + me.xp
    target_x = jnp.where(same, x, me.xp)
    first = first_s.at[jnp.where(same, 0, 1)]
    for k in range(2):
        local = same & (c == k)
        src = tokens.at[:, pl.ds(k * (tokens.shape[1] - KH), KH)]
        sends.send(src, tok.at[own], first, me.at(c=k, x=target_x), when=jnp.logical_not(local))

        @pl.when(local)
        def _():
            pltpu.make_async_copy(src, tok.at[own], first_s.at[0]).start()

    for join in joins:
        join.wait()

    sends.send(wj, wx, misc_s.at[0], me.at(x=me.xp))
    sends.send(docs, docs_out, misc_s.at[2], me.sibling)

    target_c = z // 2
    piece = (z % 2) * 2 + c

    def spread(src, g):
        rows = pl.ds(pl.multiple_of(target_c * PAD + piece * piece_rows, 16), piece_rows)
        dst = w.at[rows, pl.ds(pl.multiple_of(g * width, width), width)]
        sem = w_s.at[piece * 2 + g]
        here = target_c == c
        for k in (1, 3, 2):
            sends.send(src, dst, sem, me.at(z=(z + k) % 4, c=target_c))
        sends.send(src, dst, sem, me.sibling, when=jnp.logical_not(here))

        @pl.when(here)
        def _():
            pltpu.make_async_copy(src, dst, sem).start()

    w[pl.ds(pl.multiple_of((1 - c) * 4 * piece_rows, PAD), PAD), :] = jnp.zeros((PAD, 2 * width), jnp.bfloat16)
    below, above, far = me.down_y * 4, me.up_y * 4, me.far_y * 4
    here, beside = (x, me.xp), (me.xs, me.xsp)
    for slot, sem in ((own, 0), (pair, 1)):
        arrive(tok.at[slot], first_s.at[sem])
        forward("q", slot, me.up)
        forward("q", slot, me.down)
        forward("p", slot, me.beside)
        forward("p", slot, me.up)
        forward("p", slot, me.down)
        forward("q", slot, me.beside)
        if sem == 0:
            spread(wj, t)
            landed("q", below + x)
            forward("q", below + x, me.up)
            forward("q", below + x, me.beside)
    arrive(wx, misc_s.at[0])
    spread(wx, 1 - t)
    swap = jnp.logical_not(same)
    sends.send(cot, cot_out, misc_s.at[1], me.at(c=1 - c, x=me.xp), when=swap)
    landed("q", above + x)
    forward("q", above + x, me.beside)
    landed("q", above + me.xp)
    forward("q", above + me.xp, me.down)
    forward("q", above + me.xp, me.beside)
    landed("q", below + me.xp)
    forward("q", below + me.xp, me.beside)
    for column in beside:
        landed("p", y * 4 + column)
        forward("p", y * 4 + column, me.up)
        forward("p", y * 4 + column, me.down)
    for column in here:
        landed("p", below + column)
        forward("p", below + column, me.up)
        landed("q", far + column)
        forward("q", far + column, me.beside)
    for column in beside:
        landed("p", above + column)
        forward("p", above + column, me.down)

    for i in range(4):
        for g in range(2):
            arrive(w.at[pl.ds(i * piece_rows, piece_rows), pl.ds(g * width, width)], w_s.at[i * 2 + g])
    pltpu.make_async_copy(w, w_out, local_s.at[4]).start()

    plan = (
        (0, "p", ()),
        (0, "q", beside),
        (1, "q", beside),
        (2, "q", beside),
        (1, "p", beside),
        (2, "p", here),
        (3, "p", here + beside),
        (3, "q", beside),
    )
    lines = (y, me.down_y, me.up_y, me.far_y)
    done = [0, 0, 0, 0]
    units = []

    def complete(n):
        slots, rows = units[n]
        arrive(sib.at[slots, rows, :], sib_s.at[n])
        proj_out[slots, rows, :] += sib[slots, rows, :]
        pltpu.make_async_copy(
            proj_out.at[slots, rows, :], proj_hbm.at[slots, rows, :], proj_s.at[n]
        ).start()

    for n, (line, name, need) in enumerate(plan):
        row = lines[line]
        for column in need:
            landed(name, row * 4 + column)
        slots = pl.ds(pl.multiple_of(row * 4, 4), 4)
        done[line] += 1
        if done[line] == 2:
            pltpu.make_async_copy(tok.at[slots], tok_out.at[slots], local_s.at[line]).start()
        rows = part[name][0]
        block = tok[slots, rows, :].reshape(4 * HALF_ROWS, KH)
        shape = (4, HALF_ROWS, width)
        other[slots, rows, :] = mm(block, w[:, pl.ds(pl.multiple_of((1 - c) * width, width), width)]).reshape(shape)
        sends.send(other.at[slots, rows, :], sib.at[slots, rows, :], sib_s.at[n], me.sibling)
        proj_out[slots, rows, :] = mm(block, w[:, pl.ds(pl.multiple_of(c * width, width), width)]).reshape(shape)
        units.append((slots, rows))
        if n:
            complete(n - 1)
    complete(len(plan) - 1)
    for n, (slots, rows) in enumerate(units):
        pltpu.make_async_copy(
            proj_out.at[slots, rows, :], proj_hbm.at[slots, rows, :], proj_s.at[n]
        ).wait()
    for n, row in enumerate(lines):
        slots = pl.ds(pl.multiple_of(row * 4, 4), 4)
        pltpu.make_async_copy(tok.at[slots], tok_out.at[slots], local_s.at[n]).wait()
    pltpu.make_async_copy(w, w_out, local_s.at[4]).wait()
    arrive(docs_out, misc_s.at[2])
    pl.when(swap)(lambda: arrive(cot_out, misc_s.at[1]))
    sends.finish()


def gather(tokens, wq, wk, wv, cot, docs):
    f32, bf = jnp.float32, jnp.bfloat16
    anywhere = pl.BlockSpec(memory_space=pl.ANY)
    dma = pltpu.SemaphoreType.DMA
    return pl.pallas_call(
        gather_kernel,
        out_shape=(
            jax.ShapeDtypeStruct((16, 128, 4 * HEAD), f32),
            jax.ShapeDtypeStruct((16, 128, KH), bf),
            jax.ShapeDtypeStruct((KH, 8 * HEAD), bf),
            jax.ShapeDtypeStruct(cot.shape, bf),
            jax.ShapeDtypeStruct(docs.shape, docs.dtype),
        ),
        in_specs=[anywhere] * 6,
        out_specs=(anywhere,) * 5,
        scratch_shapes=[
            pltpu.VMEM((16, 128, KH), bf),
            pltpu.VMEM((KH, 8 * HEAD), bf),
            pltpu.VMEM((wq.shape[0], 4 * HEAD), bf),
            pltpu.VMEM((wq.shape[0], 4 * HEAD), bf),
            pltpu.VMEM((16, 128, 4 * HEAD), f32),
            pltpu.VMEM((16, 128, 4 * HEAD), f32),
            dma((64,)), dma((16,)), dma((16,)), dma((2,)), dma((8,)), dma((3,)), dma((8,)), dma((5,)), dma((3,)),
            pltpu.VMEM((16, 128, 4 * HEAD), f32), dma((8,)),
        ],
        compiler_params=pltpu.CompilerParams(
            collective_id=0, has_side_effects=True, vmem_limit_bytes=60 * 1024 * 1024
        ),
        name="gather",
    )(tokens, wq, wk, wv, cot, docs)


def scatter_kernel(
    both, tok_in, w_in, attn_out, token_out, gq_out, gk_out, gv_out,
    tok, w, dpj, terms, dw, rqx, rp1, rp2, rpx, rq1, rq2, rw, rwx, wsum, grad_out,
    send_s, attn_s, dp_s, local_s, qx_s, p1_s, p2_s, px_s, q1_s, q2_s, rw_s, g_s, rwx_s,
):
    me = Place()
    z, c, y, x, t, same = me.z, me.c, me.y, me.x, me.t, me.same
    sends = Sends(send_s)
    width = 4 * HEAD
    p_rows, q_rows = pl.ds(0, HALF_ROWS), pl.ds(HALF_ROWS, HALF_ROWS)
    order = (me.far_y, me.up_y, me.down_y, y)
    mine = pl.ds(pl.multiple_of(c * width, width), width)
    piece_rows = gq_out.shape[0]

    attn, dproj = both.at[:, pl.ds(0, 2 * HEAD)], both.at[:, pl.ds(2 * HEAD, width)]
    for n, row in enumerate(order):
        rows = pl.ds(pl.multiple_of(row * 512, 512), 512)
        pltpu.make_async_copy(dproj.at[rows, :], dpj.at[rows, mine], local_s.at[n]).start()
        if n == 0:
            pltpu.make_async_copy(w_in, w, local_s.at[4]).start()
    pltpu.make_async_copy(tok_in, tok, local_s.at[5]).start()
    meet(
        [me.sibling]
        + [
            me.at(c=core, y=(y + dy) % 4, x=(x + dx) % 4)
            for dy in range(4) for dx in range(4) if dy or dx for core in range(2)
        ]
        + [me.at(z=(z + k) % 4, c=core) for k in (1, 2, 3) for core in range(2)]
    )
    for n, row in enumerate(order):
        rows = pl.ds(pl.multiple_of(row * 512, 512), 512)
        sends.send(dproj.at[rows, :], dpj.at[rows, mine], dp_s.at[n], me.sibling)

    def add(dst, *sources):
        total = dst[...].astype(jnp.float32)
        for source in sources:
            total = total + source[...].astype(jnp.float32)
        dst[...] = total.astype(jnp.bfloat16)

    def compute(n):
        row = order[n]
        rows = pl.ds(pl.multiple_of(row * 512, 512), 512)
        arrive(dpj.at[rows, pl.ds(0, width)], local_s.at[n])
        arrive(dpj.at[rows, pl.ds(0, width)], dp_s.at[n])
        if n == 0:
            arrive(w, local_s.at[4])
        slots = pl.ds(pl.multiple_of(row * 4, 4), 4)
        term = mm(dpj[rows, :], w[...], NT).astype(jnp.bfloat16)
        terms[slots] = term.reshape(4, 128, KH)
        for k, column in enumerate((me.xs, me.xsp)):
            sends.send(terms.at[row * 4 + column, q_rows, :], rqx.at[n, k], qx_s.at[n, k], me.beside)

    def weight_terms(i):
        if i == 0:
            arrive(tok, local_s.at[5])
        low, high = ((0, 512), (512, 768), (768, 1152), (1152, KH))[i]
        left = tok[:, :, low:high].reshape(16 * 128, high - low)
        dw[low:high, :] = mm(left, dpj[...], (((0,), (0,)), ((), ()))).astype(jnp.bfloat16)
        for g in range(2):
            rows = pl.ds(pl.multiple_of(c * PAD + i * piece_rows, 16), piece_rows)
            src = dw.at[rows, pl.ds(g * width, width)]
            dst, sem = rw.at[z * 2 + g], rw_s.at[z * 2 + g]
            to_z, to_c = 2 * c + i // 2, i % 2
            stays = (to_z == z) & (c == to_c)
            sends.send(src, dst, sem, me.at(z=to_z, c=to_c), when=jnp.logical_not(stays))

            @pl.when(stays)
            def _():
                pltpu.make_async_copy(src, dst, sem).start()

    def exchanged(n):
        for k, column in enumerate((x, me.xp)):
            arrive(rqx.at[n, k], qx_s.at[n, k])
            add(terms.at[order[n] * 4 + column, q_rows, :], rqx.at[n, k])

    def finish(n, rows):
        src, dst, sem = terms.at[own + me.xp, rows, :], grad_out.at[c, rows, :], g_s.at[c, n]
        sends.send(src, dst, sem, me.at(c=t, x=me.xp))
        src = terms.at[own + x, rows, :]
        sends.send(src, dst, sem, me.sibling, when=jnp.logical_not(same))

        @pl.when(same)
        def _():
            pltpu.make_async_copy(src, dst, sem).start()

    far, up, down, own = me.far_y * 4, me.up_y * 4, me.down_y * 4, y * 4
    group = y * 4 + jnp.where(same, x, me.xp)
    columns = pl.ds(pl.multiple_of(group * 2 * HEAD, 2 * HEAD), 2 * HEAD)
    compute(0)
    sends.send(terms.at[pl.ds(far, 2), p_rows, :], rp1.at[0], p1_s.at[0], me.up)
    sends.send(terms.at[pl.ds(far + 2, 2), p_rows, :], rp1.at[1], p1_s.at[1], me.down)
    compute(1)
    compute(2)
    compute(3)
    weight_terms(0)
    weight_terms(1)
    arrive(rp1.at[0], p1_s.at[0])
    add(terms.at[pl.ds(up, 2), p_rows, :], rp1.at[0])
    sends.send(terms.at[pl.ds(up, 4), p_rows, :], rp2.at[0], p2_s.at[0], me.up)
    arrive(rp1.at[1], p1_s.at[1])
    add(terms.at[pl.ds(down + 2, 2), p_rows, :], rp1.at[1])
    sends.send(terms.at[pl.ds(down, 4), p_rows, :], rp2.at[1], p2_s.at[1], me.down)
    weight_terms(2)
    weight_terms(3)
    exchanged(0)
    sends.send(terms.at[far + x, q_rows, :], rq1.at[0], q1_s.at[0], me.up)
    sends.send(terms.at[far + me.xp, q_rows, :], rq1.at[1], q1_s.at[1], me.down)
    for n, base, extra, device in ((1, up, x, me.up), (2, down, me.xp, me.down)):
        exchanged(n)
        arrive(rq1.at[n - 1], q1_s.at[n - 1])
        add(terms.at[base + extra, q_rows, :], rq1.at[n - 1])
        for k, column in enumerate((x, me.xp)):
            sends.send(terms.at[base + column, q_rows, :], rq2.at[n - 1, k], q2_s.at[n - 1, k], device)
    arrive(rp2.at[0], p2_s.at[0])
    arrive(rp2.at[1], p2_s.at[1])
    add(terms.at[pl.ds(own, 4), p_rows, :], rp2.at[0], rp2.at[1])
    for k, column in enumerate((me.xs, me.xsp)):
        sends.send(terms.at[own + column, p_rows, :], rpx.at[k], px_s.at[k], me.beside)

    def summed(g):
        total = rw[g].astype(jnp.float32)
        for k in range(1, 4):
            total = total + rw[2 * k + g].astype(jnp.float32)
        return total

    for dy in range(4):
        for dx in range(4):
            to_y, to_x = (y + dy) % 4, (x + dx) % 4
            rows = pl.ds(pl.multiple_of((to_y * 4 + to_x) * 128, 128), 128)
            src, dst = attn.at[rows, :], attn_out.at[:, columns]
            if dy == 0 and dx == 0:
                sends.send(src, dst, attn_s.at[group], me.sibling, when=jnp.logical_not(same))

                @pl.when(same)
                def _():
                    pltpu.make_async_copy(src, dst, attn_s.at[group]).start()
            else:
                sends.send(src, dst, attn_s.at[group], me.at(c=t, y=to_y, x=to_x))

    for k, column in enumerate((x, me.xp)):
        arrive(rqx.at[3, k], qx_s.at[3, k])
        arrive(rq2.at[0, k], q2_s.at[0, k])
        arrive(rq2.at[1, k], q2_s.at[1, k])
        add(terms.at[own + column, q_rows, :], rqx.at[3, k], rq2.at[0, k], rq2.at[1, k])
    finish(1, q_rows)
    for k in range(8):
        arrive(rw.at[k], rw_s.at[k])
    wsum[...] = summed(1 - t).astype(jnp.bfloat16)
    sends.send(wsum, rwx, rwx_s.at[0], me.at(x=me.xp))
    for k, column in enumerate((x, me.xp)):
        arrive(rpx.at[k], px_s.at[k])
        add(terms.at[own + column, p_rows, :], rpx.at[k])
    finish(0, p_rows)
    total = summed(t)
    arrive(rwx, rwx_s.at[0])
    total = total + rwx[...].astype(jnp.float32)
    gq_out[...] = total[:, : 2 * HEAD]
    gk_out[...] = total[:, 2 * HEAD : 3 * HEAD]
    gv_out[...] = total[:, 3 * HEAD :]
    for k in range(16):
        arrive(attn_out.at[:, pl.ds(k * 2 * HEAD, 2 * HEAD)], attn_s.at[k])
    for k in range(2):
        for n, rows in ((0, p_rows), (1, q_rows)):
            arrive(grad_out.at[k, rows, :], g_s.at[k, n])
    low = token_out.shape[1] - KH
    lane = lax.broadcasted_iota(jnp.int32, (128, KH - low), 1)
    token_out[:, :low] = grad_out[0, :, :low]
    token_out[:, low:KH] = jnp.where(lane < PAD, grad_out[0, :, low:], grad_out[1, :, : KH - low])
    token_out[:, KH:] = grad_out[1, :, KH - low :]
    sends.finish()


def scatter(both, tok, w, piece_rows):
    f32, bf = jnp.float32, jnp.bfloat16
    anywhere = pl.BlockSpec(memory_space=pl.ANY)
    vmem = pl.BlockSpec(memory_space=pltpu.VMEM)
    dma = pltpu.SemaphoreType.DMA
    length = both.shape[0]
    half = (HALF_ROWS, KH)
    return pl.pallas_call(
        scatter_kernel,
        out_shape=(
            jax.ShapeDtypeStruct((128, 32 * HEAD), bf),
            jax.ShapeDtypeStruct((128, 2 * (KH - PAD)), bf),
            jax.ShapeDtypeStruct((piece_rows, 2 * HEAD), f32),
            jax.ShapeDtypeStruct((piece_rows, HEAD), f32),
            jax.ShapeDtypeStruct((piece_rows, HEAD), f32),
        ),
        in_specs=[anywhere] * 3,
        out_specs=(anywhere, vmem, vmem, vmem, vmem),
        scratch_shapes=[
            pltpu.VMEM((16, 128, KH), bf),
            pltpu.VMEM((KH, 8 * HEAD), bf),
            pltpu.VMEM((length, 8 * HEAD), bf),
            pltpu.VMEM((16, 128, KH), bf),
            pltpu.VMEM((KH, 8 * HEAD), bf),
            pltpu.VMEM((4, 2) + half, bf),
            pltpu.VMEM((2, 2) + half, bf),
            pltpu.VMEM((2, 4) + half, bf),
            pltpu.VMEM((2,) + half, bf),
            pltpu.VMEM((2,) + half, bf),
            pltpu.VMEM((2, 2) + half, bf),
            pltpu.VMEM((8, piece_rows, 4 * HEAD), bf),
            pltpu.VMEM((piece_rows, 4 * HEAD), bf),
            pltpu.VMEM((piece_rows, 4 * HEAD), bf),
            pltpu.VMEM((2, 128, KH), bf),
            dma((60,)), dma((16,)), dma((4,)), dma((6,)), dma((4, 2)), dma((2,)), dma((2,)),
            dma((2,)), dma((2,)), dma((2, 2)), dma((8,)), dma((2, 2)), dma((1,)),
        ],
        compiler_params=pltpu.CompilerParams(
            collective_id=1, has_side_effects=True, vmem_limit_bytes=50 * 1024 * 1024
        ),
        name="scatter",
    )(both, tok, w)


def local(
    tokens, q_weight, key_projection, value_projection, query_norm_gain, key_norm_gain, doc_lengths, out_cot
):
    proj, tok, w, cot2, docs2 = gather(
        tokens, q_weight, key_projection, value_projection, out_cot, doc_lengths
    )
    proj = proj.reshape(out_cot.shape[0], 4 * HEAD)
    both = attention(
        doc_lengths, docs2, proj, out_cot, cot2, query_norm_gain, key_norm_gain
    )
    attn_out, token_grad, gq, gk, gv = scatter(both, tok, w, q_weight.shape[0])
    return (attn_out, token_grad, gq, gk, gv)


def solution(mesh):
    placed = (
        P(("dp", "seq"), None),
        P("dp", "seq"),
        P("dp", "seq"),
        P("dp", "seq"),
        P(),
        P(),
        P("dp", None),
        P("dp", "seq"),
    )
    return jax.shard_map(
        local,
        mesh=mesh,
        in_specs=placed,
        out_specs=(
            P(("dp", "seq"), None),
            P(("dp", "seq"), None),
            P("dp", "seq"),
            P("dp", "seq"),
            P("dp", "seq"),
        ),
        check_vma=False,
    )
```

```python
import functools
import math

import jax
import jax.numpy as jnp
import numpy as np
from jax import lax
from jax.experimental import pallas as pl
from jax.experimental.pallas import tpu as pltpu
from jax.sharding import PartitionSpec as P

HEAD = 128
WINDOW = 1024
BLOCK = 256
UNROLL = 2
score_scale = 168.0 ** (-0.5)
exp_scale = score_scale * math.log2(math.e)
rope_base = 10000.0
norm_eps = 1e-06
NN = (((1,), (0,)), ((), ()))
NT = (((1,), (1,)), ((), ()))


def mm(a, b, dims=NN):
    return lax.dot_general(a, b, dims, preferred_element_type=jnp.float32)


def rope_tables(blocks):
    inverse = rope_base ** (-np.arange(HEAD // 2) * (2.0 / HEAD))
    inverse = np.concatenate([inverse, inverse])[None, :]
    coarse = (np.arange(blocks) * BLOCK)[:, None] * inverse
    fine = np.arange(BLOCK)[:, None] * inverse
    return [
        jnp.asarray(table, jnp.float32)
        for table in (np.cos(coarse), np.sin(coarse), np.cos(fine), np.sin(fine))
    ]


def norm_factor(x):
    return lax.rsqrt(jnp.mean(x * x, axis=-1, keepdims=True) + norm_eps)


def rotate(n, cosine, sine):
    return n * cosine + pltpu.roll(n, HEAD // 2, 1) * sine


def rotate_back(g, cosine, sine):
    return g * cosine + pltpu.roll(g * sine, HEAD // 2, 1)


def norm_back(dn, x, gain):
    factor = norm_factor(x)
    dn = dn * gain
    inner = jnp.sum(x * dn, axis=-1, keepdims=True) * (1.0 / HEAD)
    return factor * dn - x * (factor * factor * factor * inner)


def attention_kernel(
    docs_ref, docs2_ref, proj_hbm, cot_own, cot_got, cos_a, sin_a, cos_b, sin_b, gq_ref, gk_ref, both_hbm,
    cot_ref, cot_sem, proj_ref, out_ref, dproj_ref, in_sem, out_sem, q_s, k_s, kt_s, v_s, vt_s, e_s, eb_s, dk_s, dv_s, acc_s, dot_s, row_s,
):
    length = proj_hbm.shape[0]
    blocks = length // BLOCK
    span = WINDOW // BLOCK
    def block_rows(i):
        return pl.ds(pl.multiple_of(i * BLOCK, BLOCK), BLOCK)

    def load(i):
        rows = block_rows(i)
        return pltpu.make_async_copy(proj_hbm.at[rows, :], proj_ref.at[rows, :], in_sem.at[i])

    def store(i, k):
        rows = block_rows(i)
        src, low = ((out_ref, 0), (dproj_ref, 0), (dproj_ref, 2 * HEAD))[k]
        return pltpu.make_async_copy(
            src.at[rows, pl.ds(low, 2 * HEAD)],
            both_hbm.at[rows, pl.ds(k * 2 * HEAD, 2 * HEAD)],
            out_sem.at[i, k],
        )

    for i in range(blocks):
        load(i).start()
    same = lax.axis_index("dp") % 2 == (lax.axis_index("seq") % 4) // 2
    lane = lax.broadcasted_iota(jnp.int32, (1, HEAD), 1)
    sign = jnp.where(lane < HEAD // 2, -1.0, 1.0)

    def tables(i):
        ca, sa = cos_a[pl.ds(i, 1), :], sin_a[pl.ds(i, 1), :]
        return ca * cos_b[...] - sa * sin_b[...], (sa * sign) * cos_b[...] + (ca * sign) * sin_b[...]

    pl.when(same)(lambda: pltpu.make_async_copy(cot_own, cot_ref, cot_sem).start())
    pl.when(jnp.logical_not(same))(lambda: pltpu.make_async_copy(cot_got, cot_ref, cot_sem).start())
    e0, e1, e2 = [jnp.where(same, docs_ref[0, k], docs2_ref[0, k]) for k in range(3)]
    e1 = e0 + e1
    e2 = e1 + e2

    def start_of(t):
        zero = t * 0
        return jnp.maximum(
            jnp.maximum(jnp.where(t >= e0, e0, zero), jnp.where(t >= e1, e1, zero)),
            jnp.where(t >= e2, e2, zero),
        )

    @pl.loop(0, blocks)
    def _(i):
        load(i).wait()
        rows = pl.ds(pl.multiple_of(i * BLOCK, BLOCK), BLOCK)
        cosine, sine = tables(i)
        for h in range(2):
            x = proj_ref[rows, h * HEAD : (h + 1) * HEAD]
            n = x * norm_factor(x) * gq_ref[...]
            q_s[i, h * BLOCK : (h + 1) * BLOCK, :] = rotate(n, cosine, sine).astype(jnp.bfloat16)
        x = proj_ref[rows, 2 * HEAD : 3 * HEAD]
        n = x * norm_factor(x) * gk_ref[...]
        key = rotate(n, cosine, sine)
        k_s[i] = key.astype(jnp.bfloat16)
        kt_s[i] = key.astype(jnp.bfloat16).T
        value = proj_ref[rows, 3 * HEAD : 4 * HEAD]
        v_s[i] = value.astype(jnp.bfloat16)
        vt_s[i] = value.astype(jnp.bfloat16).T
        dk_s[i] = jnp.zeros((BLOCK, HEAD), jnp.float32)
        dv_s[i] = jnp.zeros((BLOCK, HEAD), jnp.float32)

    pltpu.make_async_copy(cot_own, cot_ref, cot_sem).wait()

    @pl.loop(0, blocks)
    def _(i):
        q0 = i * BLOCK
        rows = pl.ds(pl.multiple_of(q0, BLOCK), BLOCK)
        token = q0 + lax.broadcasted_iota(jnp.int32, (1, BLOCK), 1)
        low = jnp.maximum(start_of(token), token - (WINDOW - 1))
        token2 = jnp.concatenate([token, token], axis=1)
        low2 = jnp.concatenate([low, low], axis=1)
        first = jnp.maximum(start_of(q0), q0 - (WINDOW - 1)) // BLOCK
        first = jnp.maximum(first, 0)

        acc_s[...] = jnp.zeros_like(acc_s)
        row_s[...] = jnp.zeros_like(row_s)
        query = q_s[i]

        steps = (i - first + UNROLL) // UNROLL
        start = i + 1 - steps * UNROLL

        @pl.loop(0, steps)
        def _(step):
            low_j = start + step * UNROLL
            keys = [jnp.maximum(low_j + u, 0) for u in range(UNROLL)]
            total, mixed = row_s[...], acc_s[...]
            scores = [mm(k_s[j], query, NT) for j in keys]
            for u, j in enumerate(keys):
                slot = low_j + u - i + span + UNROLL - 1
                key_pos = (low_j + u) * BLOCK + lax.broadcasted_iota(jnp.int32, (BLOCK, 2 * BLOCK), 0)
                e = jnp.exp2(scores[u] * exp_scale)
                e = jnp.where((key_pos >= low2) & (key_pos <= token2), e, 0.0)
                e_s[slot] = e
                eb = e.astype(jnp.bfloat16)
                eb_s[slot] = eb
                total += jnp.sum(e.reshape(BLOCK // 8, 8, 2 * BLOCK), axis=0)
                mixed += mm(vt_s[j], eb)
            row_s[...], acc_s[...] = total, mixed

        inv = 1.0 / jnp.sum(row_s[...], axis=0, keepdims=True)
        out_t = acc_s[...] * inv
        dot = jnp.concatenate(
            [cot_ref[rows, h * HEAD : (h + 1) * HEAD].T.astype(jnp.float32) for h in range(2)], axis=1
        )
        for h in range(2):
            out_ref[rows, h * HEAD : (h + 1) * HEAD] = (
                out_t[:, h * BLOCK : (h + 1) * BLOCK].astype(jnp.bfloat16).T
            )
        store(i, 0).start()
        delta = jnp.sum(out_t * dot, axis=0, keepdims=True) * inv
        dot_s[...] = (dot * inv).astype(jnp.bfloat16)
        dout = dot_s[...].T
        acc_s[...] = jnp.zeros_like(acc_s)

        @pl.loop(0, steps)
        def _(step):
            low_j = start + step * UNROLL
            keys = [jnp.maximum(low_j + u, 0) for u in range(UNROLL)]
            slots = [low_j + u - i + span + UNROLL - 1 for u in range(UNROLL)]
            d_probs = [mm(v_s[j], dot_s[...]) for j in keys]
            d_scores = [(e_s[slot] * (dp - delta)).astype(jnp.bfloat16) for slot, dp in zip(slots, d_probs)]
            d_values = [mm(eb_s[slot], dout) for slot in slots]
            d_keys = [mm(ds, query) for ds in d_scores]
            mixed = acc_s[...]
            for j, ds in zip(keys, d_scores):
                mixed += mm(kt_s[j], ds)
            acc_s[...] = mixed
            for j, dv, dk in zip(keys, d_values, d_keys):
                dv_s[j] += dv
                dk_s[j] += dk

        cosine, sine = tables(i)
        for h in range(2):
            g = acc_s[:, h * BLOCK : (h + 1) * BLOCK].T * score_scale
            x = proj_ref[rows, h * HEAD : (h + 1) * HEAD]
            dx = norm_back(rotate_back(g, cosine, sine), x, gq_ref[...])
            dproj_ref[rows, h * HEAD : (h + 1) * HEAD] = dx.astype(jnp.bfloat16)
        store(i, 1).start()

    @pl.loop(0, blocks)
    def _(i):
        rows = pl.ds(pl.multiple_of(i * BLOCK, BLOCK), BLOCK)
        cosine, sine = tables(i)
        x = proj_ref[rows, 2 * HEAD : 3 * HEAD]
        dx = norm_back(rotate_back(dk_s[i] * score_scale, cosine, sine), x, gk_ref[...])
        dproj_ref[rows, 2 * HEAD : 3 * HEAD] = dx.astype(jnp.bfloat16)
        dproj_ref[rows, 3 * HEAD : 4 * HEAD] = dv_s[i].astype(jnp.bfloat16)
        store(i, 2).start()

    for i in range(blocks):
        for k in range(3):
            store(i, k).wait()


def attention(docs, docs2, proj, cot, cot2, gain_q, gain_k):
    length = proj.shape[0]
    blocks = length // BLOCK
    slots = WINDOW // BLOCK + UNROLL
    vmem = pl.BlockSpec(memory_space=pltpu.VMEM)
    bf, f32 = jnp.bfloat16, jnp.float32
    return pl.pallas_call(
        attention_kernel,
        out_shape=jax.ShapeDtypeStruct((length, 6 * HEAD), bf),
        in_specs=[pl.BlockSpec(memory_space=pltpu.SMEM)] * 2
        + [pl.BlockSpec(memory_space=pl.ANY)] * 3
        + [vmem] * 6,
        out_specs=pl.BlockSpec(memory_space=pl.ANY),
        scratch_shapes=[
            pltpu.VMEM((length, 2 * HEAD), bf),
            pltpu.SemaphoreType.DMA(()),
            pltpu.VMEM((length, 4 * HEAD), f32),
            pltpu.VMEM((length, 2 * HEAD), bf),
            pltpu.VMEM((length, 4 * HEAD), bf),
            pltpu.SemaphoreType.DMA((blocks,)),
            pltpu.SemaphoreType.DMA((blocks, 3)),
            pltpu.VMEM((blocks, 2 * BLOCK, HEAD), bf),
            pltpu.VMEM((blocks, BLOCK, HEAD), bf),
            pltpu.VMEM((blocks, HEAD, BLOCK), bf),
            pltpu.VMEM((blocks, BLOCK, HEAD), bf),
            pltpu.VMEM((blocks, HEAD, BLOCK), bf),
            pltpu.VMEM((slots, BLOCK, 2 * BLOCK), f32),
            pltpu.VMEM((slots, BLOCK, 2 * BLOCK), bf),
            pltpu.VMEM((blocks, BLOCK, HEAD), f32),
            pltpu.VMEM((blocks, BLOCK, HEAD), f32),
            pltpu.VMEM((HEAD, 2 * BLOCK), f32),
            pltpu.VMEM((HEAD, 2 * BLOCK), bf),
            pltpu.VMEM((8, 2 * BLOCK), f32),
        ],
        compiler_params=pltpu.CompilerParams(vmem_limit_bytes=60 * 1024 * 1024),
        name="attention",
    )(docs, docs2, proj, cot, cot2, *rope_tables(blocks), gain_q.reshape(1, HEAD), gain_k.reshape(1, HEAD))


MESH = pl.DeviceIdType.MESH
KH = 1408
PAD = 64
HALF_ROWS = 64


class Place:
    def __init__(self):
        d, s = lax.axis_index("dp"), lax.axis_index("seq")
        self.z, self.c = d // 2, d % 2
        self.y, self.x = s // 4, s % 4
        self.t = self.x // 2
        self.xp = 3 - self.x
        self.xs = self.x + 1 - 2 * (self.x % 2)
        self.xsp = 3 - self.xs
        self.up_y, self.down_y, self.far_y = (self.y + 1) % 4, (self.y + 3) % 4, (self.y + 2) % 4
        self.same = self.c == self.t
        self.beside = self.at(x=self.xs)
        self.up, self.down = self.at(y=self.up_y), self.at(y=self.down_y)
        self.sibling = self.at(c=1 - self.c)

    def at(self, z=None, c=None, y=None, x=None):
        z = self.z if z is None else z
        c = self.c if c is None else c
        y = self.y if y is None else y
        x = self.x if x is None else x
        return (z * 2 + c, y * 4 + x)


def meet(devices):
    barrier = pltpu.get_barrier_semaphore()
    for device in devices:
        pl.semaphore_signal(barrier, inc=1, device_id=device, device_id_type=MESH)
    pl.semaphore_wait(barrier, len(devices))


class Sends:
    def __init__(self, sems):
        self.sems, self.count, self.open = sems, 0, []

    def sem(self):
        self.count += 1
        return self.sems.at[self.count - 1]

    def send(self, src, dst, recv, device, when=None):
        copy = pltpu.make_async_remote_copy(
            src_ref=src, dst_ref=dst, send_sem=self.sem(), recv_sem=recv,
            device_id=device, device_id_type=MESH,
        )
        if when is None:
            copy.start()
        else:
            pl.when(when)(copy.start)
        self.open.append((copy, when))

    def finish(self):
        for copy, when in self.open:
            if when is None:
                copy.wait_send()
            else:
                pl.when(when)(copy.wait_send)


def arrive(dst, sem):
    pltpu.make_async_copy(dst, dst, sem).wait()


def gather_kernel(
    tokens, wq, wk, wv, cot, docs, proj_hbm, tok_out, w_out, cot_out, docs_out,
    tok, w, wj, wx, other, sib, send_s, p_s, q_s, first_s, w_s, misc_s, sib_s, local_s, join_s, proj_out, proj_s,
):
    me = Place()
    z, c, y, x, t, same = me.z, me.c, me.y, me.x, me.t, me.same
    sends = Sends(send_s)
    width = 4 * HEAD
    part = {"p": (pl.ds(0, HALF_ROWS), p_s), "q": (pl.ds(HALF_ROWS, HALF_ROWS), q_s)}
    piece_rows = wj.shape[0]
    joins = [
        pltpu.make_async_copy(src, wj.at[:, pl.ds(low, src.shape[1])], join_s.at[k])
        for k, (src, low) in enumerate(((wq, 0), (wk, 2 * HEAD), (wv, 3 * HEAD)))
    ]
    for join in joins:
        join.start()
    meet(
        [me.sibling, me.beside, me.up, me.down, me.at(c=0, x=me.xp), me.at(c=1, x=me.xp)]
        + [me.at(z=(z + k) % 4, c=core) for k in (1, 2, 3) for core in range(2)]
    )

    def forward(name, slot, device):
        rows, sems = part[name]
        ref = tok.at[slot, rows, :]
        sends.send(ref, ref, sems.at[slot], device)

    def landed(name, slot):
        rows, sems = part[name]
        arrive(tok.at[slot, rows, :], sems.at[slot])

    own, pair = y * 4 + x, y * 4 + me.xp
    target_x = jnp.where(same, x, me.xp)
    first = first_s.at[jnp.where(same, 0, 1)]
    for k in range(2):
        local = same & (c == k)
        src = tokens.at[:, pl.ds(k * (tokens.shape[1] - KH), KH)]
        sends.send(src, tok.at[own], first, me.at(c=k, x=target_x), when=jnp.logical_not(local))

        @pl.when(local)
        def _():
            pltpu.make_async_copy(src, tok.at[own], first_s.at[0]).start()

    for join in joins:
        join.wait()

    sends.send(wj, wx, misc_s.at[0], me.at(x=me.xp))
    sends.send(docs, docs_out, misc_s.at[2], me.sibling)

    target_c = z // 2
    piece = (z % 2) * 2 + c

    def spread(src, g):
        rows = pl.ds(pl.multiple_of(target_c * PAD + piece * piece_rows, 16), piece_rows)
        dst = w.at[rows, pl.ds(pl.multiple_of(g * width, width), width)]
        sem = w_s.at[piece * 2 + g]
        here = target_c == c
        for k in (1, 3, 2):
            sends.send(src, dst, sem, me.at(z=(z + k) % 4, c=target_c))
        sends.send(src, dst, sem, me.sibling, when=jnp.logical_not(here))

        @pl.when(here)
        def _():
            pltpu.make_async_copy(src, dst, sem).start()

    w[pl.ds(pl.multiple_of((1 - c) * 4 * piece_rows, PAD), PAD), :] = jnp.zeros((PAD, 2 * width), jnp.bfloat16)
    below, above, far = me.down_y * 4, me.up_y * 4, me.far_y * 4
    here, beside = (x, me.xp), (me.xs, me.xsp)
    for slot, sem in ((own, 0), (pair, 1)):
        arrive(tok.at[slot], first_s.at[sem])
        forward("q", slot, me.up)
        forward("q", slot, me.down)
        forward("p", slot, me.beside)
        forward("p", slot, me.up)
        forward("p", slot, me.down)
        forward("q", slot, me.beside)
        if sem == 0:
            spread(wj, t)
            landed("q", below + x)
            forward("q", below + x, me.up)
            forward("q", below + x, me.beside)
    arrive(wx, misc_s.at[0])
    spread(wx, 1 - t)
    swap = jnp.logical_not(same)
    sends.send(cot, cot_out, misc_s.at[1], me.at(c=1 - c, x=me.xp), when=swap)
    landed("q", above + x)
    forward("q", above + x, me.beside)
    landed("q", above + me.xp)
    forward("q", above + me.xp, me.down)
    forward("q", above + me.xp, me.beside)
    landed("q", below + me.xp)
    forward("q", below + me.xp, me.beside)
    for column in beside:
        landed("p", y * 4 + column)
        forward("p", y * 4 + column, me.up)
        forward("p", y * 4 + column, me.down)
    for column in here:
        landed("p", below + column)
        forward("p", below + column, me.up)
        landed("q", far + column)
        forward("q", far + column, me.beside)
    for column in beside:
        landed("p", above + column)
        forward("p", above + column, me.down)

    for i in range(4):
        for g in range(2):
            arrive(w.at[pl.ds(i * piece_rows, piece_rows), pl.ds(g * width, width)], w_s.at[i * 2 + g])
    pltpu.make_async_copy(w, w_out, local_s.at[4]).start()

    plan = (
        (0, "p", ()),
        (0, "q", beside),
        (1, "q", beside),
        (2, "q", beside),
        (1, "p", beside),
        (2, "p", here),
        (3, "p", here + beside),
        (3, "q", beside),
    )
    lines = (y, me.down_y, me.up_y, me.far_y)
    done = [0, 0, 0, 0]
    units = []

    def complete(n):
        slots, rows = units[n]
        arrive(sib.at[slots, rows, :], sib_s.at[n])
        proj_out[slots, rows, :] += sib[slots, rows, :]
        pltpu.make_async_copy(
            proj_out.at[slots, rows, :], proj_hbm.at[slots, rows, :], proj_s.at[n]
        ).start()

    for n, (line, name, need) in enumerate(plan):
        row = lines[line]
        for column in need:
            landed(name, row * 4 + column)
        slots = pl.ds(pl.multiple_of(row * 4, 4), 4)
        done[line] += 1
        if done[line] == 2:
            pltpu.make_async_copy(tok.at[slots], tok_out.at[slots], local_s.at[line]).start()
        rows = part[name][0]
        block = tok[slots, rows, :].reshape(4 * HALF_ROWS, KH)
        shape = (4, HALF_ROWS, width)
        other[slots, rows, :] = mm(block, w[:, pl.ds(pl.multiple_of((1 - c) * width, width), width)]).reshape(shape)
        sends.send(other.at[slots, rows, :], sib.at[slots, rows, :], sib_s.at[n], me.sibling)
        proj_out[slots, rows, :] = mm(block, w[:, pl.ds(pl.multiple_of(c * width, width), width)]).reshape(shape)
        units.append((slots, rows))
        if n:
            complete(n - 1)
    complete(len(plan) - 1)
    for n, (slots, rows) in enumerate(units):
        pltpu.make_async_copy(
            proj_out.at[slots, rows, :], proj_hbm.at[slots, rows, :], proj_s.at[n]
        ).wait()
    for n, row in enumerate(lines):
        slots = pl.ds(pl.multiple_of(row * 4, 4), 4)
        pltpu.make_async_copy(tok.at[slots], tok_out.at[slots], local_s.at[n]).wait()
    pltpu.make_async_copy(w, w_out, local_s.at[4]).wait()
    arrive(docs_out, misc_s.at[2])
    pl.when(swap)(lambda: arrive(cot_out, misc_s.at[1]))
    sends.finish()


def gather(tokens, wq, wk, wv, cot, docs):
    f32, bf = jnp.float32, jnp.bfloat16
    anywhere = pl.BlockSpec(memory_space=pl.ANY)
    dma = pltpu.SemaphoreType.DMA
    return pl.pallas_call(
        gather_kernel,
        out_shape=(
            jax.ShapeDtypeStruct((16, 128, 4 * HEAD), f32),
            jax.ShapeDtypeStruct((16, 128, KH), bf),
            jax.ShapeDtypeStruct((KH, 8 * HEAD), bf),
            jax.ShapeDtypeStruct(cot.shape, bf),
            jax.ShapeDtypeStruct(docs.shape, docs.dtype),
        ),
        in_specs=[anywhere] * 6,
        out_specs=(anywhere,) * 5,
        scratch_shapes=[
            pltpu.VMEM((16, 128, KH), bf),
            pltpu.VMEM((KH, 8 * HEAD), bf),
            pltpu.VMEM((wq.shape[0], 4 * HEAD), bf),
            pltpu.VMEM((wq.shape[0], 4 * HEAD), bf),
            pltpu.VMEM((16, 128, 4 * HEAD), f32),
            pltpu.VMEM((16, 128, 4 * HEAD), f32),
            dma((64,)), dma((16,)), dma((16,)), dma((2,)), dma((8,)), dma((3,)), dma((8,)), dma((5,)), dma((3,)),
            pltpu.VMEM((16, 128, 4 * HEAD), f32), dma((8,)),
        ],
        compiler_params=pltpu.CompilerParams(
            collective_id=0, has_side_effects=True, vmem_limit_bytes=60 * 1024 * 1024
        ),
        name="gather",
    )(tokens, wq, wk, wv, cot, docs)


def scatter_kernel(
    both, tok_in, w_in, attn_out, token_out, gq_out, gk_out, gv_out,
    tok, w, dpj, terms, dw, rqx, rp1, rp2, rpx, rq1, rq2, rw, rwx, wsum, grad_out,
    send_s, attn_s, dp_s, local_s, qx_s, p1_s, p2_s, px_s, q1_s, q2_s, rw_s, g_s, rwx_s,
):
    me = Place()
    z, c, y, x, t, same = me.z, me.c, me.y, me.x, me.t, me.same
    sends = Sends(send_s)
    width = 4 * HEAD
    p_rows, q_rows = pl.ds(0, HALF_ROWS), pl.ds(HALF_ROWS, HALF_ROWS)
    order = (me.far_y, me.up_y, me.down_y, y)
    mine = pl.ds(pl.multiple_of(c * width, width), width)
    piece_rows = gq_out.shape[0]

    attn, dproj = both.at[:, pl.ds(0, 2 * HEAD)], both.at[:, pl.ds(2 * HEAD, width)]
    for n, row in enumerate(order):
        rows = pl.ds(pl.multiple_of(row * 512, 512), 512)
        pltpu.make_async_copy(dproj.at[rows, :], dpj.at[rows, mine], local_s.at[n]).start()
        if n == 0:
            pltpu.make_async_copy(w_in, w, local_s.at[4]).start()
    pltpu.make_async_copy(tok_in, tok, local_s.at[5]).start()
    meet(
        [me.sibling]
        + [
            me.at(c=core, y=(y + dy) % 4, x=(x + dx) % 4)
            for dy in range(4) for dx in range(4) if dy or dx for core in range(2)
        ]
        + [me.at(z=(z + k) % 4, c=core) for k in (1, 2, 3) for core in range(2)]
    )
    for n, row in enumerate(order):
        rows = pl.ds(pl.multiple_of(row * 512, 512), 512)
        sends.send(dproj.at[rows, :], dpj.at[rows, mine], dp_s.at[n], me.sibling)

    def add(dst, *sources):
        total = dst[...].astype(jnp.float32)
        for source in sources:
            total = total + source[...].astype(jnp.float32)
        dst[...] = total.astype(jnp.bfloat16)

    def compute(n):
        row = order[n]
        rows = pl.ds(pl.multiple_of(row * 512, 512), 512)
        arrive(dpj.at[rows, pl.ds(0, width)], local_s.at[n])
        arrive(dpj.at[rows, pl.ds(0, width)], dp_s.at[n])
        if n == 0:
            arrive(w, local_s.at[4])
        slots = pl.ds(pl.multiple_of(row * 4, 4), 4)
        term = mm(dpj[rows, :], w[...], NT).astype(jnp.bfloat16)
        terms[slots] = term.reshape(4, 128, KH)
        for k, column in enumerate((me.xs, me.xsp)):
            sends.send(terms.at[row * 4 + column, q_rows, :], rqx.at[n, k], qx_s.at[n, k], me.beside)

    def weight_terms(i):
        if i == 0:
            arrive(tok, local_s.at[5])
        low, high = ((0, 512), (512, 768), (768, 1152), (1152, KH))[i]
        left = tok[:, :, low:high].reshape(16 * 128, high - low)
        dw[low:high, :] = mm(left, dpj[...], (((0,), (0,)), ((), ()))).astype(jnp.bfloat16)
        for g in range(2):
            rows = pl.ds(pl.multiple_of(c * PAD + i * piece_rows, 16), piece_rows)
            src = dw.at[rows, pl.ds(g * width, width)]
            dst, sem = rw.at[z * 2 + g], rw_s.at[z * 2 + g]
            to_z, to_c = 2 * c + i // 2, i % 2
            stays = (to_z == z) & (c == to_c)
            sends.send(src, dst, sem, me.at(z=to_z, c=to_c), when=jnp.logical_not(stays))

            @pl.when(stays)
            def _():
                pltpu.make_async_copy(src, dst, sem).start()

    def exchanged(n):
        for k, column in enumerate((x, me.xp)):
            arrive(rqx.at[n, k], qx_s.at[n, k])
            add(terms.at[order[n] * 4 + column, q_rows, :], rqx.at[n, k])

    def finish(n, rows):
        src, dst, sem = terms.at[own + me.xp, rows, :], grad_out.at[c, rows, :], g_s.at[c, n]
        sends.send(src, dst, sem, me.at(c=t, x=me.xp))
        src = terms.at[own + x, rows, :]
        sends.send(src, dst, sem, me.sibling, when=jnp.logical_not(same))

        @pl.when(same)
        def _():
            pltpu.make_async_copy(src, dst, sem).start()

    far, up, down, own = me.far_y * 4, me.up_y * 4, me.down_y * 4, y * 4
    group = y * 4 + jnp.where(same, x, me.xp)
    columns = pl.ds(pl.multiple_of(group * 2 * HEAD, 2 * HEAD), 2 * HEAD)
    for dy in range(4):
        for dx in range(4):
            to_y, to_x = (y + dy) % 4, (x + dx) % 4
            rows = pl.ds(pl.multiple_of((to_y * 4 + to_x) * 128, 128), 128)
            src, dst = attn.at[rows, :], attn_out.at[:, columns]
            if dy == 0 and dx == 0:
                sends.send(src, dst, attn_s.at[group], me.sibling, when=jnp.logical_not(same))

                @pl.when(same)
                def _():
                    pltpu.make_async_copy(src, dst, attn_s.at[group]).start()
            else:
                sends.send(src, dst, attn_s.at[group], me.at(c=t, y=to_y, x=to_x))

    compute(0)
    sends.send(terms.at[pl.ds(far, 2), p_rows, :], rp1.at[0], p1_s.at[0], me.up)
    sends.send(terms.at[pl.ds(far + 2, 2), p_rows, :], rp1.at[1], p1_s.at[1], me.down)
    compute(1)
    compute(2)
    compute(3)
    weight_terms(0)
    weight_terms(1)
    arrive(rp1.at[0], p1_s.at[0])
    add(terms.at[pl.ds(up, 2), p_rows, :], rp1.at[0])
    sends.send(terms.at[pl.ds(up, 4), p_rows, :], rp2.at[0], p2_s.at[0], me.up)
    arrive(rp1.at[1], p1_s.at[1])
    add(terms.at[pl.ds(down + 2, 2), p_rows, :], rp1.at[1])
    sends.send(terms.at[pl.ds(down, 4), p_rows, :], rp2.at[1], p2_s.at[1], me.down)
    weight_terms(2)
    weight_terms(3)
    exchanged(0)
    sends.send(terms.at[far + x, q_rows, :], rq1.at[0], q1_s.at[0], me.up)
    sends.send(terms.at[far + me.xp, q_rows, :], rq1.at[1], q1_s.at[1], me.down)
    for n, base, extra, device in ((1, up, x, me.up), (2, down, me.xp, me.down)):
        exchanged(n)
        arrive(rq1.at[n - 1], q1_s.at[n - 1])
        add(terms.at[base + extra, q_rows, :], rq1.at[n - 1])
        for k, column in enumerate((x, me.xp)):
            sends.send(terms.at[base + column, q_rows, :], rq2.at[n - 1, k], q2_s.at[n - 1, k], device)
    arrive(rp2.at[0], p2_s.at[0])
    arrive(rp2.at[1], p2_s.at[1])
    add(terms.at[pl.ds(own, 4), p_rows, :], rp2.at[0], rp2.at[1])
    for k, column in enumerate((me.xs, me.xsp)):
        sends.send(terms.at[own + column, p_rows, :], rpx.at[k], px_s.at[k], me.beside)

    def summed(g):
        total = rw[g].astype(jnp.float32)
        for k in range(1, 4):
            total = total + rw[2 * k + g].astype(jnp.float32)
        return total

    for k, column in enumerate((x, me.xp)):
        arrive(rqx.at[3, k], qx_s.at[3, k])
        arrive(rq2.at[0, k], q2_s.at[0, k])
        arrive(rq2.at[1, k], q2_s.at[1, k])
        add(terms.at[own + column, q_rows, :], rqx.at[3, k], rq2.at[0, k], rq2.at[1, k])
    finish(1, q_rows)
    for k in range(8):
        arrive(rw.at[k], rw_s.at[k])
    wsum[...] = summed(1 - t).astype(jnp.bfloat16)
    sends.send(wsum, rwx, rwx_s.at[0], me.at(x=me.xp))
    for k, column in enumerate((x, me.xp)):
        arrive(rpx.at[k], px_s.at[k])
        add(terms.at[own + column, p_rows, :], rpx.at[k])
    finish(0, p_rows)
    total = summed(t)
    arrive(rwx, rwx_s.at[0])
    total = total + rwx[...].astype(jnp.float32)
    gq_out[...] = total[:, : 2 * HEAD]
    gk_out[...] = total[:, 2 * HEAD : 3 * HEAD]
    gv_out[...] = total[:, 3 * HEAD :]
    for k in range(16):
        arrive(attn_out.at[:, pl.ds(k * 2 * HEAD, 2 * HEAD)], attn_s.at[k])
    for k in range(2):
        for n, rows in ((0, p_rows), (1, q_rows)):
            arrive(grad_out.at[k, rows, :], g_s.at[k, n])
    low = token_out.shape[1] - KH
    lane = lax.broadcasted_iota(jnp.int32, (128, KH - low), 1)
    token_out[:, :low] = grad_out[0, :, :low]
    token_out[:, low:KH] = jnp.where(lane < PAD, grad_out[0, :, low:], grad_out[1, :, : KH - low])
    token_out[:, KH:] = grad_out[1, :, KH - low :]
    sends.finish()


def scatter(both, tok, w, piece_rows):
    f32, bf = jnp.float32, jnp.bfloat16
    anywhere = pl.BlockSpec(memory_space=pl.ANY)
    vmem = pl.BlockSpec(memory_space=pltpu.VMEM)
    dma = pltpu.SemaphoreType.DMA
    length = both.shape[0]
    half = (HALF_ROWS, KH)
    return pl.pallas_call(
        scatter_kernel,
        out_shape=(
            jax.ShapeDtypeStruct((128, 32 * HEAD), bf),
            jax.ShapeDtypeStruct((128, 2 * (KH - PAD)), bf),
            jax.ShapeDtypeStruct((piece_rows, 2 * HEAD), f32),
            jax.ShapeDtypeStruct((piece_rows, HEAD), f32),
            jax.ShapeDtypeStruct((piece_rows, HEAD), f32),
        ),
        in_specs=[anywhere] * 3,
        out_specs=(anywhere, vmem, vmem, vmem, vmem),
        scratch_shapes=[
            pltpu.VMEM((16, 128, KH), bf),
            pltpu.VMEM((KH, 8 * HEAD), bf),
            pltpu.VMEM((length, 8 * HEAD), bf),
            pltpu.VMEM((16, 128, KH), bf),
            pltpu.VMEM((KH, 8 * HEAD), bf),
            pltpu.VMEM((4, 2) + half, bf),
            pltpu.VMEM((2, 2) + half, bf),
            pltpu.VMEM((2, 4) + half, bf),
            pltpu.VMEM((2,) + half, bf),
            pltpu.VMEM((2,) + half, bf),
            pltpu.VMEM((2, 2) + half, bf),
            pltpu.VMEM((8, piece_rows, 4 * HEAD), bf),
            pltpu.VMEM((piece_rows, 4 * HEAD), bf),
            pltpu.VMEM((piece_rows, 4 * HEAD), bf),
            pltpu.VMEM((2, 128, KH), bf),
            dma((60,)), dma((16,)), dma((4,)), dma((6,)), dma((4, 2)), dma((2,)), dma((2,)),
            dma((2,)), dma((2,)), dma((2, 2)), dma((8,)), dma((2, 2)), dma((1,)),
        ],
        compiler_params=pltpu.CompilerParams(
            collective_id=1, has_side_effects=True, vmem_limit_bytes=50 * 1024 * 1024
        ),
        name="scatter",
    )(both, tok, w)


def local(
    tokens, q_weight, key_projection, value_projection, query_norm_gain, key_norm_gain, doc_lengths, out_cot
):
    proj, tok, w, cot2, docs2 = gather(
        tokens, q_weight, key_projection, value_projection, out_cot, doc_lengths
    )
    proj = proj.reshape(out_cot.shape[0], 4 * HEAD)
    both = attention(
        doc_lengths, docs2, proj, out_cot, cot2, query_norm_gain, key_norm_gain
    )
    attn_out, token_grad, gq, gk, gv = scatter(both, tok, w, q_weight.shape[0])
    return (attn_out, token_grad, gq, gk, gv)


def solution(mesh):
    placed = (
        P(("dp", "seq"), None),
        P("dp", "seq"),
        P("dp", "seq"),
        P("dp", "seq"),
        P(),
        P(),
        P("dp", None),
        P("dp", "seq"),
    )
    return jax.shard_map(
        local,
        mesh=mesh,
        in_specs=placed,
        out_specs=(
            P(("dp", "seq"), None),
            P(("dp", "seq"), None),
            P("dp", "seq"),
            P("dp", "seq"),
            P("dp", "seq"),
        ),
        check_vma=False,
    )
```
